128 devices in a mesh: fsdp: 16 (over y, x_lo, core), tp: 8 (over z, x_hi).
Axes of the slice: x: 4 (x_hi: 2, x_lo: 2; x = x_hi * 2 + x_lo), y: 4, z: 4, core: 2. Of those that a mesh axis runs over, the one named last changes fastest.
Arguments:
- tokens: bfloat16 [16384, 2048], P(('fsdp', 'tp')), may hold values from -6 to 6
- prefixes: int32 [8], replicated, may hold values from 1152 to 1536, as said below
- norm_gain: bfloat16 [2048], replicated, may hold values from 0.5 to 1.5
- query_weight: bfloat16 [2048, 2048], P('fsdp', 'tp'), may hold values from -0.1875 to 0.1875
- key_weight: bfloat16 [2048, 2048], P('fsdp', 'tp'), may hold values from -0.1875 to 0.1875
- value_weight: bfloat16 [2048, 2048], P('fsdp', 'tp'), may hold values from -0.125 to 0.125
- output_weight: bfloat16 [2048, 2048], P('tp', 'fsdp'), may hold values from -0.5 to 0.5
- feed_gain: bfloat16 [2048], replicated, may hold values from 0.5 to 1.5
- gate_weight: bfloat16 [2048, 5504], P('fsdp', 'tp'), may hold values from -0.125 to 0.125
- up_weight: bfloat16 [2048, 5504], P('fsdp', 'tp'), may hold values from -0.125 to 0.125
- down_weight: bfloat16 [5504, 2048], P('tp', 'fsdp'), may hold values from -0.15625 to 0.15625
- cotangent: bfloat16 [16384, 2048], P(('fsdp', 'tp')), may hold values from -6 to 6
Outputs:
- layer_output: bfloat16 [16384, 2048], P(('fsdp', 'tp'))
- token_grad: float32 [16384, 2048], P(('fsdp', 'tp'))
- norm_grad: float32 [2048], P('fsdp')
- query_grad: float32 [2048, 2048], P('fsdp', 'tp')
- key_grad: float32 [2048, 2048], P('fsdp', 'tp')
- value_grad: float32 [2048, 2048], P('fsdp', 'tp')
- output_grad: float32 [2048, 2048], P('tp', 'fsdp')
- feed_grad: float32 [2048], P('fsdp')
- gate_grad: float32 [2048, 5504], P('fsdp', 'tp')
- up_grad: float32 [2048, 5504], P('fsdp', 'tp')
- down_grad: float32 [5504, 2048], P('tp', 'fsdp')
The draws below stay inside these ranges and needn't reach their ends.
Inputs may be any that keep to these rules, and one draw needn't show every extreme that they name: prefixes[s] tokens at the start of sequence s attend both ways; some sequence has the shortest prefix 9 * 128 and some the longest 3 * 512.
All inputs are finite; a program needn't handle non-finite values.
Results may differ from the reference program's by a relative error of at most 0.03.
Values may be sent and summed in bfloat16 or wider, within the bound.
A program may use at most 192 MiB of HBM per device.

```python
import math
import jax
import jax.numpy as jnp
from jax import lax

D = 2048
H = 16
FF = 5504
HD = 128
TOKENS = 16384
SEQ = 2048
NSEQ = 8


def draw_prefixes(key, part):
    number = TOKENS // SEQ
    shortest = SEQ * 9 // 16
    longest = SEQ * 3 // 4
    lengths_drawn = jax.random.randint(jax.random.fold_in(key, 11), (number,), shortest, longest + 1)
    shuffled = jax.random.permutation(jax.random.fold_in(key, 12), number)
    lengths_drawn = lengths_drawn.at[shuffled[0]].set(longest)
    lengths_drawn = lengths_drawn.at[shuffled[1]].set(shortest)
    return lengths_drawn.astype(jnp.int32)


def block_scale(own_key, dims, shards, smallest, largest):
    def one(axis_at, parts):
        draws = jax.random.uniform(jax.random.fold_in(jax.random.fold_in(own_key, 6), axis_at), (parts,), jnp.float32, smallest / len(shards), largest / len(shards))
        return jnp.repeat(jnp.exp(draws), dims[axis_at] // parts).reshape((-1,) + (1,) * (len(dims) - axis_at - 1))

    level = one(*shards[0])
    for cut in shards[1:]:
        level = level * one(*cut)
    return level


def scatter_about(key, shape, width, reach, split=(), kind=jnp.bfloat16):
    values = jax.random.normal(key, shape, jnp.float32) * width
    if len(split) > 0:
        values = block_scale(key, shape, split, -0.22, 0.18) * values
    return jnp.clip(values, min=-reach, max=reach).astype(kind)


def setup_inputs(seed: int = 0) -> dict:
    arg_keys = jax.random.split(jax.random.key(seed), 13)
    return {
        "tokens": scatter_about(arg_keys[0], (TOKENS, D), 1.0, 6.0, ((0, 128),)),
        "prefixes": draw_prefixes(jax.random.fold_in(arg_keys[12], 71), 0),
        "norm_gain": jnp.clip(1.0 + 0.1 * jax.random.normal(arg_keys[2], (D,), jnp.float32), 0.5, 1.5).astype(jnp.bfloat16),
        "query_weight": scatter_about(arg_keys[3], (D, D), (D // 2) ** -0.5, 0.1875, ((0, 16), (1, 8))),
        "key_weight": scatter_about(arg_keys[4], (D, D), (D // 2) ** -0.5, 0.1875, ((0, 16), (1, 8))),
        "value_weight": scatter_about(arg_keys[5], (D, D), D ** -0.5, 0.125, ((0, 16), (1, 8))),
        "output_weight": scatter_about(arg_keys[6], (D, D), (D // 16) ** -0.5, 0.5, ((0, 8), (1, 16))),
        "feed_gain": jnp.clip(1.0 + 0.1 * jax.random.normal(arg_keys[7], (D,), jnp.float32), 0.5, 1.5).astype(jnp.bfloat16),
        "gate_weight": scatter_about(arg_keys[8], (D, FF), D ** -0.5, 0.125, ((0, 16), (1, 8))),
        "up_weight": scatter_about(arg_keys[9], (D, FF), D ** -0.5, 0.125, ((0, 16), (1, 8))),
        "down_weight": scatter_about(arg_keys[10], (FF, D), (FF // 4) ** -0.5, 0.15625, ((0, 8), (1, 16))),
        "cotangent": scatter_about(arg_keys[11], (TOKENS, D), 1.0, 6.0, ((0, 128),)),
    }


epsilon = 1e-05
rope_base = 10000.0

@jax.custom_vjp
def low(v):
    return lax.optimization_barrier(v.astype(jnp.bfloat16)).astype(jnp.float32)

@jax.custom_vjp
def low_back(v):
    return v

def low_keep(v):
    return (low(v), None)

def low_pass(kept, grad):
    return (grad,)

def back_keep(v):
    return (v, None)

def back_low(kept, grad):
    return (low(grad),)
low.defvjp(low_keep, low_pass)
low_back.defvjp(back_keep, back_low)

def matmul_full(factor_left, factor_right):
    return jnp.dot(factor_left, factor_right, precision=lax.Precision.HIGHEST, preferred_element_type=jnp.float32)

def rope_tables(positions, head_width):
    midway = head_width // 2
    counter = jnp.arange(midway, dtype=jnp.float32)
    inverse = jnp.exp(counter * (-2.0 / head_width) * math.log(rope_base))
    frequency = jnp.concatenate([inverse, inverse])
    angles = positions.astype(jnp.float32)[:, None] * frequency[None, :]
    return (jnp.cos(angles), jnp.sin(angles))

def rotate(values, cosine, sine_table):
    midway = values.shape[-1] // 2
    turned = jnp.concatenate([-values[..., midway:], values[..., :midway]], -1)
    return values * cosine[:, None, :] + turned * sine_table[:, None, :]

def head_attention(query_head, key_head, value_head, allowed):
    scores = low_back(matmul_full(query_head, key_head.T) * (1.0 / math.sqrt(HD)))
    masked = jnp.where(allowed, scores, -1e+30)
    weights = jax.nn.softmax(masked, axis=-1)
    return matmul_full(low(weights), value_head)

def layer_forward(rows_in, prefix_here, norm_gain, query_weight, key_weight, value_weight, output_weight, feed_gain, gate_weight, up_weight, down_weight):
    row_count = rows_in.shape[0]
    scaled_one = rows_in * lax.rsqrt(lax.optimization_barrier(jnp.mean(rows_in * rows_in, -1, keepdims=True)) + epsilon)
    normed = low(scaled_one * norm_gain)
    positions = jnp.arange(row_count, dtype=jnp.int32)
    cosine, sine_table = rope_tables(positions, HD)
    queries = low(rotate(low_back(matmul_full(normed, query_weight)).reshape(row_count, H, HD), cosine, sine_table))
    keys_all = low(rotate(low_back(matmul_full(normed, key_weight)).reshape(row_count, H, HD), cosine, sine_table))
    values_all = low(low_back(matmul_full(normed, value_weight))).reshape(row_count, H, HD)
    allowed = (positions[None, :] <= positions[:, None]) | (positions[None, :] < prefix_here)

    def one_head(triple):
        return head_attention(triple[0], triple[1], triple[2], allowed)
    heads_out = lax.map(jax.checkpoint(one_head), (queries.transpose(1, 0, 2), keys_all.transpose(1, 0, 2), values_all.transpose(1, 0, 2)))
    attended = low(low_back(heads_out.transpose(1, 0, 2).reshape(row_count, D)))
    middle = rows_in + low_back(matmul_full(attended, output_weight))
    scaled_two = middle * lax.rsqrt(lax.optimization_barrier(jnp.mean(middle * middle, -1, keepdims=True)) + epsilon)
    normed_two = low(scaled_two * feed_gain)
    gating = low_back(matmul_full(normed_two, gate_weight))
    upward = low_back(matmul_full(normed_two, up_weight))
    hidden = low(jax.nn.silu(gating) * upward)
    return middle + matmul_full(hidden, down_weight)

def reference(tokens, prefixes, norm_gain, query_weight, key_weight, value_weight, output_weight, feed_gain, gate_weight, up_weight, down_weight, cotangent):
    floats = tuple((member.astype(jnp.float32) for member in (tokens, norm_gain, query_weight, key_weight, value_weight, output_weight, feed_gain, gate_weight, up_weight, down_weight)))

    def forward(rows_all, gain_one, query_full, key_full, value_full, output_full, gain_two, gate_full, up_full, down_full):

        def one_sequence(pair):
            return layer_forward(pair[0], pair[1], gain_one, query_full, key_full, value_full, output_full, gain_two, gate_full, up_full, down_full)
        stacked = rows_all.reshape(NSEQ, SEQ, D)
        return lax.map(jax.checkpoint(one_sequence), (stacked, prefixes)).reshape(TOKENS, D)
    result, pullback = jax.vjp(forward, *floats)
    gradients = pullback(cotangent.astype(jnp.float32))
    return (result.astype(jnp.bfloat16), gradients[0], gradients[1], gradients[2], gradients[3], gradients[4], gradients[5], gradients[6], gradients[7], gradients[8], gradients[9])
```

```python
import functools
import math

import jax
import jax.numpy as jnp
from jax import lax
from jax.experimental import pallas as pl
from jax.experimental.pallas import tpu as pltpu
from jax.sharding import PartitionSpec as P

HD = 128
EPS = 1e-05
ROPE_BASE = 10000.0
F32 = jnp.float32
BF16 = jnp.bfloat16
MESH = pl.DeviceIdType.MESH
AXES = ("fsdp", "tp")
ROWS = 128
WIDE = 2048
PACK = 768
SCALE = 1.0 / math.sqrt(HD)
LOG2E = 1.4426950408889634
VMEM = 56 << 20


class Spot:
    def __init__(self):
        f, t = lax.axis_index("fsdp"), lax.axis_index("tp")
        self.y, self.xl, self.c = lax.div(f, 4), lax.rem(lax.div(f, 2), 2), lax.rem(f, 2)
        self.z, self.xh = lax.div(t, 2), lax.rem(t, 2)
        self.x = self.xh * 2 + self.xl
        self.own = self.xl * 2 + self.c
        self.away = lax.rem(self.xh + self.c, 2)
        self.home = self.away == 0

    def at(self, dy=0, dx=0, dz=0, core=None):
        y, z, x = lax.rem(self.y + dy, 4), lax.rem(self.z + dz, 4), lax.rem(self.x + dx, 4)
        return (y * 4 + lax.rem(x, 2) * 2 + (self.c if core is None else core), z * 2 + lax.div(x, 2))

    def other(self):
        return self.at(core=1 - self.c)

    def seat(self, slot):
        return (self.y * 4 + slot, self.z * 2 + self.c)

    def bench(self, slot):
        return (self.y * 4 + slot, self.z * 2 + self.xh)

    def block(self, dz=0, flip=False):
        return (1 - self.c if flip else self.c) * 4 + lax.rem(self.z + dz, 4)


class Post:
    def __init__(self, out_sems, in_sems):
        self.out_sems, self.in_sems, self.n_out, self.n_in = out_sems, in_sems, 0, 0

    def slots(self, n):
        base = self.n_in
        self.n_in += n
        return base

    def copy(self, src, dst, device, slot=None):
        slot = self.slots(1) if slot is None else slot
        self.n_out += 1
        return pltpu.make_async_remote_copy(
            src_ref=src,
            dst_ref=dst,
            send_sem=self.out_sems.at[self.n_out - 1],
            recv_sem=self.in_sems.at[slot],
            device_id=device,
            device_id_type=MESH,
        )

    def local(self, src, dst):
        self.n_out += 1
        return pltpu.make_async_copy(src, dst, self.out_sems.at[self.n_out - 1])


def greet(spot, sources, away_source, count):
    barrier = pltpu.get_barrier_semaphore()
    for source in sources:
        pl.semaphore_signal(barrier, inc=1, device_id=source, device_id_type=MESH)
    if away_source is not None:

        @pl.when(jnp.logical_not(spot.home))
        def _():
            pl.semaphore_signal(barrier, inc=1, device_id=away_source, device_id_type=MESH)

        count = count + spot.away
    pl.semaphore_wait(barrier, count)


def row_peers(spot):
    return [spot.at(dz=1), spot.at(dz=3), spot.other()]


def y_peers(spot):
    return [spot.at(dy=k) for k in (1, 2, 3)]


def after(spot, k):
    return lax.rem(spot.own + k, 4)


def run(*jobs):
    live = list(jobs)
    while live:
        for job in list(live):
            try:
                next(job)
            except StopIteration:
                live.remove(job)


def gather_rows(spot, post, own, rows):
    up, down, core = spot.at(dz=1), spot.at(dz=3), spot.other()
    half = ROWS // 2
    low, high = pl.ds(0, half), pl.ds(half, half)
    here, below, above, far = (spot.block(dz) for dz in (0, 3, 1, 2))
    a = post.copy(own, rows.at[here], up)
    b = post.copy(own, rows.at[here], down)
    k0 = post.copy(own, rows.at[here], core)
    keep = post.local(own, rows.at[here])
    for copy in (a, b, k0, keep):
        copy.start()
    yield
    a.wait_recv()
    fa = post.copy(rows.at[below, low], rows.at[below, low], up)
    k1 = post.copy(rows.at[below], rows.at[below], core)
    fa.start()
    k1.start()
    b.wait_recv()
    fb = post.copy(rows.at[above, high], rows.at[above, high], down)
    k2 = post.copy(rows.at[above], rows.at[above], core)
    fb.start()
    k2.start()
    yield
    fa.wait_recv()
    fb.wait_recv()
    k3 = post.copy(rows.at[far], rows.at[far], core)
    k3.start()
    yield
    keep.wait()
    for copy in (k0, k1, k2, k3):
        copy.wait_recv()
    for copy in (a, b, fa, fb, k0, k1, k2, k3):
        copy.wait_send()


def in_strips(count, body):
    def step(i, carry):
        body(pl.ds(pl.multiple_of(i * 16, 16), 16))
        return carry

    lax.fori_loop(0, count // 16, step, 0)


def add_into(target, other, rows=ROWS, start=0):
    def body(strip):
        strip = pl.ds(pl.multiple_of(strip.start + start, 16), 16)
        target[strip, :] = (target[strip, :].astype(F32) + other[strip, :].astype(F32)).astype(BF16)

    in_strips(rows, body)


def scatter_rows(spot, post, part, mine, land, far, gone):
    up, down, core = spot.at(dz=1), spot.at(dz=3), spot.other()
    half = ROWS // 2
    low, high = pl.ds(0, half), pl.ds(half, half)
    steps = [lax.rem(spot.z + dz, 4) for dz in (2, 3, 1, 0)]
    to_core = [post.copy(part.at[(1 - spot.c) * 4 + s], land.at[s], core) for s in steps]
    load = [post.local(part.at[spot.c * 4 + s], mine.at[s]) for s in steps]
    for a, b in zip(to_core, load):
        a.start()
        b.start()
    yield

    def ready(k):
        to_core[k].wait_recv()
        load[k].wait()

    distant, lower, upper, here = steps
    ready(0)
    add_into(mine.at[distant], land.at[distant])
    f_low = post.copy(mine.at[distant, low], far.at[low], down)
    f_high = post.copy(mine.at[distant, high], far.at[high], up)
    f_low.start()
    f_high.start()
    ready(1)
    add_into(mine.at[lower], land.at[lower])
    d_high = post.copy(mine.at[lower, high], gone.at[0, high], down)
    d_high.start()
    ready(2)
    add_into(mine.at[upper], land.at[upper])
    u_low = post.copy(mine.at[upper, low], gone.at[1, low], up)
    u_low.start()
    ready(3)
    yield
    f_low.wait_recv()
    add_into(mine.at[lower], far, half)
    d_low = post.copy(mine.at[lower, low], gone.at[0, low], down)
    d_low.start()
    f_high.wait_recv()
    add_into(mine.at[upper], far, half, half)
    u_high = post.copy(mine.at[upper, high], gone.at[1, high], up)
    u_high.start()
    yield
    for copy in (d_high, u_low, d_low, u_high):
        copy.wait_recv()
    for copy in to_core + [f_low, f_high, d_high, u_low, d_low, u_high]:
        copy.wait_send()


def row_sum(spot, mine, land, gone, strip):
    parts = [mine[spot.z, strip, :], land[spot.z, strip, :], gone[0, strip, :], gone[1, strip, :]]
    return sum(part.astype(F32) for part in parts)


def scatter_scratch():
    block = (ROWS, WIDE)
    return [
        pltpu.VMEM((4,) + block, BF16),
        pltpu.VMEM((4,) + block, BF16),
        pltpu.VMEM(block, BF16),
        pltpu.VMEM((2,) + block, BF16),
    ]


def x_spread(spot, post, src, dst_at):
    base = post.slots(4)
    copies = [post.copy(src, dst_at(spot.own), spot.at(dx=k, core=spot.xh), base + spot.own) for k in range(4)]
    keep = post.local(src, dst_at(spot.own))
    return x_start(spot, post, copies, keep, lambda k: (src, dst_at(after(spot, k)), base + after(spot, k)))


def x_collect(spot, post, src_at, dst):
    base = post.slots(4)
    copies = [post.copy(src_at(spot.own), dst.at[spot.x], spot.seat(spot.own), base + spot.x)]
    copies += [
        post.copy(src_at(after(spot, k)), dst.at[spot.x], spot.seat(after(spot, k)), base + spot.x) for k in (1, 2, 3)
    ]
    keep = post.local(src_at(spot.own), dst.at[spot.x])

    def arrival(k):
        x = lax.rem(spot.x + k, 4)
        return src_at(spot.own), dst.at[x], base + x

    return x_start(spot, post, copies, keep, arrival)


def x_start(spot, post, copies, keep, arrival):
    for k in (2, 1, 3):
        copies[k].start()

    @pl.when(spot.home)
    def _():
        keep.start()

    @pl.when(jnp.logical_not(spot.home))
    def _():
        copies[0].start()

    def landed(k):
        src, dst, slot = arrival(k)
        pltpu.make_async_remote_copy(
            src_ref=src,
            dst_ref=dst,
            send_sem=post.out_sems.at[0],
            recv_sem=post.in_sems.at[slot],
            device_id=spot.at(dx=1),
            device_id_type=MESH,
        ).wait_recv()

    def arrive():
        for k in (1, 3, 2):
            landed(k)

        @pl.when(spot.home)
        def _():
            keep.wait()

        @pl.when(jnp.logical_not(spot.home))
        def _():
            landed(0)

    def leave():
        for k in (1, 2, 3):
            copies[k].wait_send()

        @pl.when(jnp.logical_not(spot.home))
        def _():
            copies[0].wait_send()

    return arrive, leave


def gather_weights(spot, post, shard, full, stage):
    here = full.at[spot.y, :, 0]
    a1_arrive, a1_leave = x_spread(spot, post, shard.at[0], lambda slot: full.at[spot.y, slot, 0])
    keep = post.local(shard.at[1], stage.at[spot.y])
    b1 = [post.copy(shard.at[1], stage.at[spot.y], spot.at(dy=k)) for k in (2, 1, 3)]
    for copy in [keep] + b1:
        copy.start()
    yield
    a1_arrive()
    a2 = [post.copy(here, here, spot.at(dy=k)) for k in (2, 1, 3)]
    for copy in a2:
        copy.start()
    keep.wait()
    for copy in b1:
        copy.wait_recv()
    b2_arrive, b2_leave = x_spread(spot, post, stage, lambda slot: full.at[:, slot, 1])
    yield
    for copy in a2:
        copy.wait_recv()
    b2_arrive()
    a1_leave()
    b2_leave()
    for copy in b1 + a2:
        copy.wait_send()


def gather_sources(spot):
    return [spot.seat(after(spot, k)) for k in (1, 2, 3)], spot.seat(spot.own)


def scatter_sources(spot):
    return [spot.at(dx=k, core=spot.xh) for k in (1, 2, 3)], spot.at(core=spot.xh)


def sum_four(parts, write, rows=64):
    def body(strip):
        write(strip, sum(part[strip, :].astype(F32) for part in parts))

    in_strips(rows, body)


def scatter_weights(spot, post, full, out, from_x, from_y, sum_a, sum_b, last_y, last_x):
    a1_arrive, a1_leave = x_collect(spot, post, lambda slot: full.at[:, slot, 0], from_x)
    b1 = []
    for i, k in enumerate((2, 1, 3)):
        y = lax.rem(spot.y + k, 4)
        b1.append(post.copy(full.at[y, :, 1], from_y.at[i], spot.at(dy=k)))
    keep = post.local(full.at[spot.y, :, 1], from_y.at[3])
    for copy in b1 + [keep]:
        copy.start()
    yield
    a1_arrive()
    a2 = []
    for i, k in enumerate((2, 1, 3, 0)):
        y = lax.rem(spot.y + k, 4)

        def write_a(strip, total, y=y):
            sum_a[y, strip, :] = total.astype(BF16)

        sum_four([from_x.at[j, y] for j in range(4)], write_a)
        if k:
            a2.append(post.copy(sum_a.at[y], last_y.at[i], spot.at(dy=k)))
            a2[-1].start()
    for copy in b1:
        copy.wait_recv()
    keep.wait()
    for slot in range(4):

        def write_b(strip, total, slot=slot):
            sum_b[slot, strip, :] = total.astype(BF16)

        sum_four([from_y.at[j, slot] for j in range(4)], write_b)
    b2_arrive, b2_leave = x_collect(spot, post, lambda slot: sum_b.at[slot], last_x)
    yield
    for copy in a2:
        copy.wait_recv()

    def write_low(strip, total):
        out[strip, :] = total

    sum_four([last_y.at[0], last_y.at[1], last_y.at[2], sum_a.at[spot.y]], write_low)
    b2_arrive()

    def write_high(strip, total):
        out[pl.ds(pl.multiple_of(strip.start + 64, 16), 16), :] = total

    sum_four([last_x.at[j] for j in range(4)], write_high)
    a1_leave()
    b2_leave()
    for copy in b1 + a2:
        copy.wait_send()


def weight_scratch(n):
    return [
        pltpu.VMEM((4, 4, 64, n), BF16),
        pltpu.VMEM((4, 4, 64, n), BF16),
        pltpu.VMEM((4, 64, n), BF16),
        pltpu.VMEM((4, 64, n), BF16),
        pltpu.VMEM((3, 64, n), BF16),
        pltpu.VMEM((4, 64, n), BF16),
    ]


def sum_gains(spot, post, parts, out, from_y, over_y, from_chip, over_fsdp, from_tp):
    y_copies = []
    for i, k in enumerate((2, 1, 3)):
        y = lax.rem(spot.y + k, 4)
        y_copies.append(post.copy(parts.at[pl.ds(y * 4, 4)], from_y.at[i], spot.at(dy=k)))
        y_copies[-1].start()
    yield
    for copy in y_copies:
        copy.wait_recv()
    over_y[...] = parts[pl.ds(spot.y * 4, 4)] + from_y[0] + from_y[1] + from_y[2]
    chip_copies = []
    for i, k in enumerate((1, 2, 3)):
        slot = after(spot, k)
        chip_copies.append(post.copy(over_y.at[slot], from_chip.at[i], spot.bench(slot)))
        chip_copies[-1].start()
    yield
    for copy in chip_copies:
        copy.wait_recv()
    over_fsdp[...] = over_y[spot.own] + from_chip[0] + from_chip[1] + from_chip[2]
    tp_copies = []
    for i, (dz, dx) in enumerate(TP_MOVES):
        tp_copies.append(post.copy(over_fsdp, from_tp.at[i], spot.at(dz=dz, dx=dx)))
        tp_copies[-1].start()
    yield
    for copy in tp_copies:
        copy.wait_recv()
    out[...] = over_fsdp[...] + sum(from_tp[i] for i in range(7))
    for copy in y_copies + chip_copies + tp_copies:
        copy.wait_send()


TP_MOVES = [(dz, dx) for dx in (0, 2) for dz in (0, 1, 2, 3) if (dz, dx) != (0, 0)]


def gain_sources(spot):
    return (
        y_peers(spot)
        + [spot.bench(after(spot, k)) for k in (1, 2, 3)]
        + [spot.at(dz=(4 - dz) % 4, dx=dx) for dz, dx in TP_MOVES]
    )


ANY = pl.BlockSpec(memory_space=pl.ANY)
INSIDE = pl.BlockSpec(memory_space=pltpu.VMEM)


def sems(n):
    return [pltpu.SemaphoreType.DMA((n,)), pltpu.SemaphoreType.DMA((n,))]


def moving(kernel, name, outs, inputs, in_specs, out_specs, scratch, cid):
    return pl.pallas_call(
        kernel,
        name=name,
        out_shape=outs,
        in_specs=in_specs,
        out_specs=out_specs,
        scratch_shapes=scratch,
        compiler_params=pltpu.CompilerParams(collective_id=cid, has_side_effects=True, vmem_limit_bytes=VMEM),
    )(*inputs)


def shape(dims, dtype):
    return jax.ShapeDtypeStruct(dims, dtype)


def normed(rows, gain):
    inverse = lax.rsqrt(jnp.mean(rows * rows, -1, keepdims=True) + EPS)
    scaled = rows * inverse
    return inverse, scaled, (scaled * gain).astype(BF16)


def enter(tokens, gain, shard):
    n = shard.shape[1]

    def kernel(tokens_ref, gain_ref, shard_ref, rows_ref, full_ref, stage_ref, own, out_sems, in_sems):
        spot, post = Spot(), Post(out_sems, in_sems)
        seats, away = gather_sources(spot)
        greet(spot, row_peers(spot) + y_peers(spot) + seats, away, 9)
        weights = gather_weights(spot, post, shard_ref, full_ref, stage_ref)
        next(weights)

        def body(strip):
            own[strip, :] = normed(tokens_ref[strip, :].astype(F32), gain_ref[...])[2]

        in_strips(ROWS, body)
        run(weights, gather_rows(spot, post, own, rows_ref))

    return moving(
        kernel,
        "enter",
        (shape((8, ROWS, WIDE), BF16), shape((4, 4, 2, 64, n), BF16), shape((4, 64, n), BF16)),
        (tokens, gain, shard.reshape(2, 64, n)),
        [INSIDE, INSIDE, ANY],
        (ANY, ANY, ANY),
        [pltpu.VMEM((ROWS, WIDE), BF16)] + sems(40),
        1,
    )[:2]


def middle(part, tokens, gain, cotangent, shard):
    n = shard.shape[1]

    def kernel(
        part_ref, tokens_ref, gain_ref, cot_ref, shard_ref, mid_ref, rows_ref, grads_ref, full_ref, stage_ref, own, *rest
    ):
        scatter, (out_sems, in_sems) = rest[:4], rest[4:]
        mine, land, far, gone = scatter
        spot, post = Spot(), Post(out_sems, in_sems)
        seats, away = gather_sources(spot)
        greet(spot, row_peers(spot) + y_peers(spot) + seats, away, 9)

        def main():
            yield from scatter_rows(spot, post, part_ref, mine, land, far, gone)

            def body(strip):
                mid = tokens_ref[strip, :].astype(F32) + row_sum(spot, mine, land, gone, strip)
                mid_ref[strip, :] = mid
                own[strip, :] = normed(mid, gain_ref[...])[2]

            in_strips(ROWS, body)
            yield from gather_rows(spot, post, own, rows_ref)

        def second():
            for _ in range(4):
                yield
            yield from gather_rows(spot, post, cot_ref, grads_ref)

        run(main(), gather_weights(spot, post, shard_ref, full_ref, stage_ref), second())

    rows = shape((8, ROWS, WIDE), BF16)
    return moving(
        kernel,
        "middle",
        (shape((ROWS, WIDE), F32), rows, rows, shape((4, 4, 2, 64, n), BF16), shape((4, 64, n), BF16)),
        (part, tokens, gain, cotangent, shard.reshape(2, 64, n)),
        [ANY, INSIDE, INSIDE, ANY, ANY],
        (INSIDE, ANY, ANY, ANY, ANY),
        [pltpu.VMEM((ROWS, WIDE), BF16)] + scatter_scratch() + sems(64),
        2,
    )[:4]


def norm_back(upstream, rows, gain):
    inverse, scaled, _ = normed(rows, gain)
    weighted = upstream * gain
    through = inverse * (weighted - scaled * jnp.mean(weighted * scaled, -1, keepdims=True))
    return through, jnp.sum(upstream * scaled, 0, keepdims=True)


def turn(part, part_out, mid, gain, cotangent, full):
    n = full.shape[1]

    def kernel(
        part_ref, out_part_ref, mid_ref, gain_ref, cot_ref, full_ref, layer_ref, grad_ref, rows_ref, feed_ref, weight_ref,
        own, *rest,
    ):
        first, second, weights, (out_sems, in_sems) = rest[:4], rest[4:8], rest[8:14], rest[14:]
        spot, post = Spot(), Post(out_sems, in_sems)
        sources, away = scatter_sources(spot)
        greet(spot, row_peers(spot) + y_peers(spot) + sources, away, 9)

        def main():
            yield from scatter_rows(spot, post, part_ref, *first)
            feed_ref[...] = jnp.zeros_like(feed_ref)

            def body(strip):
                upstream = row_sum(spot, first[0], first[1], first[3], strip)
                through, feed = norm_back(upstream, mid_ref[strip, :], gain_ref[...])
                grad = cot_ref[strip, :].astype(F32) + through
                grad_ref[strip, :] = grad
                own[strip, :] = grad.astype(BF16)
                feed_ref[...] += feed

            in_strips(ROWS, body)
            yield from gather_rows(spot, post, own, rows_ref)

        def output():
            for _ in range(4):
                yield
            yield from scatter_rows(spot, post, out_part_ref, *second)

            def body(strip):
                layer_ref[strip, :] = (mid_ref[strip, :] + row_sum(spot, second[0], second[1], second[3], strip)).astype(BF16)

            in_strips(ROWS, body)

        run(main(), scatter_weights(spot, post, full_ref, weight_ref, *weights), output())

    return moving(
        kernel,
        "turn",
        (
            shape((ROWS, WIDE), BF16),
            shape((ROWS, WIDE), F32),
            shape((8, ROWS, WIDE), BF16),
            shape((1, WIDE), F32),
            shape((ROWS, n), F32),
        ),
        (part, part_out, mid, gain, cotangent, full.reshape(4, 4, 2, 64, n)),
        [ANY, ANY, INSIDE, INSIDE, INSIDE, ANY],
        (INSIDE, INSIDE, ANY, INSIDE, INSIDE),
        [pltpu.VMEM((ROWS, WIDE), BF16)] + scatter_scratch() * 2 + weight_scratch(n) + sems(80),
        3,
    )


def leave(part, tokens, gain, grad_mid, feed_part, full):
    n = full.shape[1]

    def kernel(
        part_ref, tokens_ref, gain_ref, grad_ref, feed_ref, full_ref, token_ref, gains_ref, weight_ref, norm_part, parts,
        from_y, over_y, from_chip, over_fsdp, from_tp, *rest,
    ):
        first, weights, (out_sems, in_sems) = rest[:4], rest[4:10], rest[10:]
        spot, post = Spot(), Post(out_sems, in_sems)
        sources, away = scatter_sources(spot)
        greet(spot, row_peers(spot) + y_peers(spot) + sources + gain_sources(spot), away, 9 + 13)

        def main():
            yield from scatter_rows(spot, post, part_ref, *first)
            norm_part[...] = jnp.zeros_like(norm_part)

            def body(strip):
                upstream = row_sum(spot, first[0], first[1], first[3], strip)
                through, norm = norm_back(upstream, tokens_ref[strip, :].astype(F32), gain_ref[...])
                token_ref[strip, :] = grad_ref[strip, :] + through
                norm_part[...] += norm

            in_strips(ROWS, body)
            parts[...] = jnp.zeros_like(parts)
            for f in range(16):
                parts[f, 0:1, :] = norm_part[:, f * 128 : (f + 1) * 128]
                parts[f, 1:2, :] = feed_ref[:, f * 128 : (f + 1) * 128]
            yield from sum_gains(spot, post, parts, gains_ref, from_y, over_y, from_chip, over_fsdp, from_tp)

        run(main(), scatter_weights(spot, post, full_ref, weight_ref, *weights))

    small = (8, 128)
    return moving(
        kernel,
        "leave",
        (shape((ROWS, WIDE), F32), shape(small, F32), shape((ROWS, n), F32)),
        (part, tokens, gain, grad_mid, feed_part, full.reshape(4, 4, 2, 64, n)),
        [ANY, INSIDE, INSIDE, INSIDE, INSIDE, ANY],
        (INSIDE, INSIDE, INSIDE),
        [pltpu.VMEM((1, WIDE), F32), pltpu.VMEM((16,) + small, F32)]
        + [pltpu.VMEM(dims + small, F32) for dims in ((3, 4), (4,), (3,), (), (7,))]
        + scatter_scratch()
        + weight_scratch(n)
        + sems(80),
        4,
    )


def dot(a, b, da=1, db=0):
    return lax.dot_general(a, b, (((da,), (db,)), ((), ())), preferred_element_type=F32)


def plain(kernel, name, grid, inputs, in_specs, outs, out_specs, scratch=()):
    return pl.pallas_call(
        kernel,
        name=name,
        out_shape=outs,
        grid=grid,
        in_specs=in_specs,
        out_specs=out_specs,
        scratch_shapes=list(scratch),
        compiler_params=pltpu.CompilerParams(vmem_limit_bytes=VMEM),
    )(*inputs)


def by_rows(n, width, column=0):
    return pl.BlockSpec((n, width), lambda i: (i, column))


def whole(dims, *index):
    at = index or (0,) * len(dims)
    return pl.BlockSpec(dims, lambda i: at)


def project(rows, weights, cosine, sine):
    step = 256

    def kernel(rows_ref, w_ref, cos_ref, sin_ref, q_ref, k_ref, v_ref):
        out = dot(rows_ref[...], w_ref[...])
        cos, sin = cos_ref[...], sin_ref[...]
        for head in range(4):
            u = out[:, head * HD : (head + 1) * HD]
            turned = (u * cos + pltpu.roll(u, HD // 2, 1) * sin).astype(BF16)
            target = q_ref if head < 2 else k_ref
            target[:, head % 2 * HD : (head % 2 + 1) * HD] = turned
        v_ref[...] = out[:, 4 * HD :].astype(BF16)

    out = shape((8 * ROWS, 2 * HD), BF16)
    return plain(
        kernel,
        "project",
        (8 * ROWS // step,),
        (rows, weights, cosine, sine),
        [by_rows(step, WIDE), whole((WIDE, PACK)), by_rows(step, HD), by_rows(step, HD)],
        (out, out, out),
        (by_rows(step, 2 * HD),) * 3,
    )


def partial_rows(pairs, name, extra=None):
    step = 256
    sets = [pairs] + ([extra] if extra else [])
    flat = [pair for group in sets for pair in group]

    def kernel(*refs):
        values, outs = refs[: 2 * len(flat)], refs[2 * len(flat) :]
        at = 0
        for group, out in zip(sets, outs):
            total = None
            for _ in group:
                term = dot(values[at][...], values[at + 1][...], 1, 1)
                total = term if total is None else total + term
                at += 2
            out[...] = total.astype(BF16)

    inputs, specs = [], []
    for a, b, width, column in flat:
        inputs += [a, b]
        specs += [by_rows(step, width), whole((WIDE, width), 0, column)]
    out = tuple(shape((8 * ROWS, WIDE), BF16) for _ in sets)
    return plain(kernel, name, (8 * ROWS // step,), inputs, specs, out, tuple(by_rows(step, WIDE) for _ in sets))


def feed_forward(rows, grads, weights):
    step = 256

    def kernel(rows_ref, grads_ref, g_ref, u_ref, d_ref, hid_ref, dgate_ref, dup_ref):
        gate = dot(rows_ref[...], g_ref[...])
        up = dot(rows_ref[...], u_ref[...])
        d_hid = dot(grads_ref[...], d_ref[...])
        sigma = 1.0 / (1.0 + jnp.exp(-gate))
        silu = gate * sigma
        hid_ref[...] = (silu * up).astype(BF16)
        dup_ref[...] = (d_hid * silu).astype(BF16)
        dgate_ref[...] = (d_hid * up * sigma * (1.0 + gate * (1.0 - sigma))).astype(BF16)

    out = shape((8 * ROWS, PACK), BF16)
    return plain(
        kernel,
        "feed_forward",
        (8 * ROWS // step,),
        (rows, grads, weights, weights, weights),
        [by_rows(step, WIDE)] * 2 + [whole((WIDE, PACK), 0, i) for i in range(3)],
        (out,) * 3,
        (by_rows(step, PACK),) * 3,
    )


def outer(groups, name):
    step = 256
    count = 8 * ROWS

    def kernel(*refs):
        out = refs[-1]
        at, column = 0, 0
        for rows, values in groups:
            left = refs[at][...]
            for i, value in enumerate(values):
                width = value.shape[1]
                out[:, column : column + width] = dot(left, refs[at + 1 + i][...], 0, 0).astype(BF16)
                column += width
            at += 1 + len(values)

    inputs, specs, total = [], [], 0
    for rows, values in groups:
        inputs += [rows] + list(values)
        specs += [pl.BlockSpec((count, step), lambda i: (0, i))] + [whole(value.shape) for value in values]
        total += sum(value.shape[1] for value in values)
    return plain(kernel, name, (WIDE // step,), inputs, specs, shape((WIDE, total), BF16), by_rows(step, total))


def back_to_heads(rows, weights):
    step = 256

    def kernel(rows_ref, w_ref, out_ref):
        out_ref[...] = dot(rows_ref[...], w_ref[...]).astype(BF16)

    return plain(
        kernel,
        "back_to_heads",
        (8 * ROWS // step,),
        (rows, weights),
        [by_rows(step, WIDE), whole((WIDE, 2 * HD), 0, 3)],
        shape((8 * ROWS, 2 * HD), BF16),
        by_rows(step, 2 * HD),
    )


TILE = 256
CHUNK = 512


def place_of(start, count, xh, axis):
    dims = (count, 1) if axis == 0 else (1, count)
    j = lax.broadcasted_iota(jnp.int32, dims, axis)
    return 2 * (j + start) - lax.rem(j, ROWS) + xh * ROWS


def key_chunks():
    return [(((0, 0, 512),), None), (((1, 0, 512),), None), (((0, 512, 256), (1, 512, 256)), "near")], (
        ((0, 768, 256), (1, 768, 256)),
        "far",
    )


def allowed_in(pieces, q_pos, prefix, xh):
    k_pos = jnp.concatenate([place_of(start, count, lax.rem(xh + side, 2), 0) for side, start, count in pieces], 0)
    return jnp.logical_or(k_pos <= q_pos, k_pos < prefix)


def take(pieces, sides, which, cols):
    parts = [sides[side][which, pl.ds(start, count), cols] for side, start, count in pieces]
    return parts[0] if len(parts) == 1 else jnp.concatenate(parts, 0)


def attend(meta, queries, here, there):
    def kernel(meta_ref, q_ref, here_ref, there_ref, o_ref, lse_ref, top_ref, sum_ref, acc_ref):
        prefix, xh = meta_ref[0], meta_ref[1]
        sides = (here_ref, there_ref)
        always, last = key_chunks()

        def step(i, carry):
            head, tile = lax.div(i, 4), lax.rem(i, 4)
            cols = pl.ds(pl.multiple_of(head * HD, HD), HD)
            rows = pl.ds(pl.multiple_of(tile * TILE, TILE), TILE)
            q = q_ref[rows, cols]
            q_pos = place_of(tile * TILE, TILE, xh, 1)

            def chunk(pieces, masked, first):
                keys = take(pieces, sides, 0, cols)
                scores = dot(keys, q, 1, 1) * (SCALE * LOG2E)
                if masked:
                    scores = jnp.where(allowed_in(pieces, q_pos, prefix, xh), scores, -1e30)
                top = jnp.max(scores, 0, keepdims=True)
                if not first:
                    before = top_ref[...]
                    top = jnp.maximum(top, before)
                raised = jnp.exp2(scores - top)
                total = jnp.sum(raised, 0, keepdims=True)
                mixed = dot(take(pieces, sides, 1, cols), raised.astype(BF16), 0, 0)
                if not first:
                    fade = jnp.exp2(before - top)
                    total = total + sum_ref[...] * fade
                    mixed = mixed + acc_ref[...] * fade
                top_ref[...] = top
                sum_ref[...] = total
                acc_ref[...] = mixed

            for number, (pieces, masked) in enumerate(always):
                chunk(pieces, masked, number == 0)

            @pl.when(tile == 3)
            def _():
                chunk(*last, False)

            total = sum_ref[...]
            o_ref[rows, cols] = (acc_ref[...] / total).T.astype(BF16)
            lse_ref[pl.ds(i, 1), :] = top_ref[...] + jnp.log2(total)
            return carry

        lax.fori_loop(0, 8, step, 0)

    return pl.pallas_call(
        kernel,
        name="attend",
        out_shape=(shape((8 * ROWS, 2 * HD), BF16), shape((8, TILE), F32)),
        in_specs=[pl.BlockSpec(memory_space=pltpu.SMEM), INSIDE, INSIDE, INSIDE],
        out_specs=(INSIDE, INSIDE),
        scratch_shapes=[pltpu.VMEM((1, TILE), F32), pltpu.VMEM((1, TILE), F32), pltpu.VMEM((HD, TILE), F32)],
        compiler_params=pltpu.CompilerParams(vmem_limit_bytes=VMEM),
    )(meta, queries, here, there)


def attend_back(meta, queries, here, there, grads, lse, delta, cosine, sine):
    def kernel(
        meta_ref, q_ref, here_ref, there_ref, g_ref, lse_ref, delta_ref, cos_ref, sin_ref, dq_ref, near_ref, far_ref,
        dq_acc, acc_here, acc_there,
    ):
        prefix, xh = meta_ref[0], meta_ref[1]
        sides, accs = (here_ref, there_ref), (acc_here, acc_there)
        always, last = key_chunks()
        acc_here[...] = jnp.zeros_like(acc_here)
        acc_there[...] = jnp.zeros_like(acc_there)

        def step(i, carry):
            head, tile = lax.div(i, 4), lax.rem(i, 4)
            cols = pl.ds(pl.multiple_of(head * HD, HD), HD)
            rows = pl.ds(pl.multiple_of(tile * TILE, TILE), TILE)
            q, g = q_ref[rows, cols], g_ref[rows, cols]
            q_pos = place_of(tile * TILE, TILE, xh, 1)
            level, offset = lse_ref[pl.ds(i, 1), :], delta_ref[pl.ds(i, 1), :]

            def chunk(pieces, masked, first):
                keys = take(pieces, sides, 0, cols)
                scores = dot(keys, q, 1, 1) * (SCALE * LOG2E)
                if masked:
                    scores = jnp.where(allowed_in(pieces, q_pos, prefix, xh), scores, -1e30)
                probs = jnp.exp2(scores - level)
                d_probs = dot(take(pieces, sides, 1, cols), g, 1, 1)
                d_scores = (probs * (d_probs - offset)).astype(BF16)
                d_values = dot(probs.astype(BF16), g)
                d_keys = dot(d_scores, q)
                at = 0
                for side, start, count in pieces:
                    span = pl.ds(start, count)
                    accs[side][0, span, cols] += d_keys[at : at + count]
                    accs[side][1, span, cols] += d_values[at : at + count]
                    at += count
                d_query = dot(d_scores, keys, 0, 0)
                dq_acc[...] = d_query if first else dq_acc[...] + d_query

            for number, (pieces, masked) in enumerate(always):
                chunk(pieces, masked, number == 0)

            @pl.when(tile == 3)
            def _():
                chunk(*last, False)

            u = dq_acc[...] * SCALE
            dq_ref[rows, cols] = (u * cos_ref[rows, :] - pltpu.roll(u, HD // 2, 1) * sin_ref[rows, :]).astype(BF16)
            return carry

        lax.fori_loop(0, 8, step, 0)
        near_ref[...] = acc_here[...]
        far_ref[...] = acc_there[...].astype(BF16)

    pair = (2, 8 * ROWS, 2 * HD)
    return pl.pallas_call(
        kernel,
        name="attend_back",
        out_shape=(shape((8 * ROWS, 2 * HD), BF16), shape(pair, F32), shape(pair, BF16)),
        in_specs=[pl.BlockSpec(memory_space=pltpu.SMEM)] + [INSIDE] * 8,
        out_specs=(INSIDE,) * 3,
        scratch_shapes=[pltpu.VMEM((TILE, HD), F32), pltpu.VMEM(pair, F32), pltpu.VMEM(pair, F32)],
        compiler_params=pltpu.CompilerParams(vmem_limit_bytes=VMEM),
    )(meta, queries, here, there, grads, lse, delta, cosine, sine)


def to_far_x(block):
    return lax.ppermute(block, "tp", [(t, t ^ 1) for t in range(8)])


def padded(shard):
    return jnp.pad(shard, ((0, 0), (0, PACK - shard.shape[1])))


def rope_tables(positions):
    counter = jnp.arange(HD // 2, dtype=F32)
    inverse = jnp.exp(counter * (-2.0 / HD) * math.log(ROPE_BASE))
    angles = positions.astype(F32)[:, None] * inverse[None, :]
    cosine, sine = jnp.cos(angles), jnp.sin(angles)
    return jnp.concatenate([cosine, cosine], 1), jnp.concatenate([-sine, sine], 1)


def on_device(
    tokens,
    prefixes,
    norm_gain,
    query_weight,
    key_weight,
    value_weight,
    output_weight,
    feed_gain,
    gate_weight,
    up_weight,
    down_weight,
    cotangent,
):
    sequence = lax.axis_index("fsdp") // 2
    xh = lax.axis_index("tp") % 2
    hidden_here = gate_weight.shape[1]
    width = 2 * HD
    prefix = jnp.sum(jnp.where(jnp.arange(prefixes.shape[0], dtype=jnp.int32) == sequence, prefixes, 0))
    meta = jnp.stack([prefix, xh]).astype(jnp.int32)
    j = jnp.arange(8 * ROWS, dtype=jnp.int32)
    cosine, sine = rope_tables(2 * j - j % ROWS + xh * ROWS)
    gain_one = norm_gain.astype(F32)[None]
    gain_two = feed_gain.astype(F32)[None]
    shard_one = jnp.concatenate([query_weight, key_weight, value_weight, output_weight.T], 1)
    shard_two = jnp.concatenate([padded(gate_weight), padded(up_weight), padded(down_weight.T)], 1)

    rows_one, full_one = enter(tokens, gain_one, shard_one)
    rows_one = rows_one.reshape(-1, WIDE)
    full_one = full_one.reshape(WIDE, -1)
    queries, keys, values = project(rows_one, full_one, cosine, sine)
    here = jnp.stack([keys, values])
    there = to_far_x(here)
    attended, lse = attend(meta, queries, here, there)
    (part,) = partial_rows([(attended, full_one, width, 3)], "attention_out")
    mid, rows_two, grad_rows, full_two = middle(part.reshape(8, ROWS, WIDE), tokens, gain_two, cotangent, shard_two)
    rows_two, grad_rows, full_two = (a.reshape(-1, a.shape[-1]) for a in (rows_two, grad_rows, full_two.reshape(WIDE, -1)))
    hidden, d_gate, d_up = feed_forward(rows_two, grad_rows, full_two)
    part, part_out = partial_rows(
        [(d_gate, full_two, PACK, 0), (d_up, full_two, PACK, 1)], "feed_back", [(hidden, full_two, PACK, 2)]
    )
    grads_two = outer([(rows_two, (d_gate, d_up)), (grad_rows, (hidden,))], "feed_grads")
    layer_output, grad_mid, mid_rows, feed_part, ffn_grad = turn(
        part.reshape(8, ROWS, WIDE), part_out.reshape(8, ROWS, WIDE), mid, gain_two, cotangent, grads_two
    )
    mid_rows = mid_rows.reshape(-1, WIDE)
    grad_mixed = back_to_heads(mid_rows, full_one)
    delta = jnp.sum((grad_mixed.astype(F32) * attended.astype(F32)).reshape(4, TILE, 2, HD), -1)
    delta = delta.transpose(2, 0, 1).reshape(8, TILE)
    d_query, near, far = attend_back(meta, queries, here, there, grad_mixed, lse, delta, cosine, sine)
    d_pair = near + to_far_x(far).astype(F32)
    d_key = (d_pair[0] * SCALE).reshape(-1, 2, HD)
    d_key = d_key * cosine[:, None] - jnp.roll(d_key, HD // 2, -1) * sine[:, None]
    d_qkv = jnp.concatenate([d_query, d_key.reshape(-1, width).astype(BF16), d_pair[1].astype(BF16)], 1)
    (part,) = partial_rows([(d_qkv, full_one, PACK, 0)], "attention_back")
    grads_one = outer([(rows_one, (d_qkv,)), (mid_rows, (attended,))], "attention_grads")
    token_grad, gains, attention_grad = leave(part.reshape(8, ROWS, WIDE), tokens, gain_one, grad_mid, feed_part, grads_one)
    return (
        layer_output,
        token_grad,
        gains[0],
        attention_grad[:, :width],
        attention_grad[:, width : 2 * width],
        attention_grad[:, 2 * width : 3 * width],
        attention_grad[:, 3 * width :].T,
        gains[1],
        ffn_grad[:, :hidden_here],
        ffn_grad[:, PACK : PACK + hidden_here],
        ffn_grad[:, 2 * PACK : 2 * PACK + hidden_here].T,
    )


def solution(mesh):
    rows = P(("fsdp", "tp"), None)
    wide = P("fsdp", "tp")
    tall = P("tp", "fsdp")
    return jax.shard_map(
        on_device,
        mesh=mesh,
        in_specs=(rows, P(), P(), wide, wide, wide, tall, P(), wide, wide, tall, rows),
        out_specs=(rows, rows, P("fsdp"), wide, wide, wide, tall, P("fsdp"), wide, wide, tall),
        check_vma=False,
    )
```

```python
import functools
import math

import jax
import jax.numpy as jnp
from jax import lax
from jax.experimental import pallas as pl
from jax.experimental.pallas import tpu as pltpu
from jax.sharding import PartitionSpec as P

HD = 128
EPS = 1e-05
ROPE_BASE = 10000.0
F32 = jnp.float32
BF16 = jnp.bfloat16
MESH = pl.DeviceIdType.MESH
AXES = ("fsdp", "tp")
ROWS = 128
WIDE = 2048
PACK = 768
SCALE = 1.0 / math.sqrt(HD)
LOG2E = 1.4426950408889634
VMEM = 56 << 20


class Spot:
    def __init__(self):
        f, t = lax.axis_index("fsdp"), lax.axis_index("tp")
        self.y, self.xl, self.c = lax.div(f, 4), lax.rem(lax.div(f, 2), 2), lax.rem(f, 2)
        self.z, self.xh = lax.div(t, 2), lax.rem(t, 2)
        self.x = self.xh * 2 + self.xl
        self.own = self.xl * 2 + self.c
        self.away = lax.rem(self.xh + self.c, 2)
        self.home = self.away == 0

    def at(self, dy=0, dx=0, dz=0, core=None):
        y, z, x = lax.rem(self.y + dy, 4), lax.rem(self.z + dz, 4), lax.rem(self.x + dx, 4)
        return (y * 4 + lax.rem(x, 2) * 2 + (self.c if core is None else core), z * 2 + lax.div(x, 2))

    def other(self):
        return self.at(core=1 - self.c)

    def seat(self, slot):
        return (self.y * 4 + slot, self.z * 2 + self.c)

    def bench(self, slot):
        return (self.y * 4 + slot, self.z * 2 + self.xh)

    def block(self, dz=0, flip=False):
        return (1 - self.c if flip else self.c) * 4 + lax.rem(self.z + dz, 4)


class Post:
    def __init__(self, out_sems, in_sems):
        self.out_sems, self.in_sems, self.n_out, self.n_in = out_sems, in_sems, 0, 0

    def slots(self, n):
        base = self.n_in
        self.n_in += n
        return base

    def take_out(self, n):
        base = self.n_out
        self.n_out += n
        return base

    def copy(self, src, dst, device, slot=None):
        slot = self.slots(1) if slot is None else slot
        self.n_out += 1
        return pltpu.make_async_remote_copy(
            src_ref=src,
            dst_ref=dst,
            send_sem=self.out_sems.at[self.n_out - 1],
            recv_sem=self.in_sems.at[slot],
            device_id=device,
            device_id_type=MESH,
        )

    def local(self, src, dst):
        self.n_out += 1
        return pltpu.make_async_copy(src, dst, self.out_sems.at[self.n_out - 1])


def greet(spot, sources, away_source, count):
    barrier = pltpu.get_barrier_semaphore()
    for source in sources:
        pl.semaphore_signal(barrier, inc=1, device_id=source, device_id_type=MESH)
    if away_source is not None:

        @pl.when(jnp.logical_not(spot.home))
        def _():
            pl.semaphore_signal(barrier, inc=1, device_id=away_source, device_id_type=MESH)

        count = count + spot.away
    pl.semaphore_wait(barrier, count)


def row_peers(spot):
    return [spot.at(dz=1), spot.at(dz=3), spot.other()]


def y_peers(spot):
    return [spot.at(dy=k) for k in (1, 2, 3)]


def after(spot, k):
    return lax.rem(spot.own + k, 4)


def play(order, **jobs):
    for letter in order:
        next(jobs[letter], None)
    for job in jobs.values():
        for _ in job:
            pass


def gather_rows(spot, post, own, rows):
    up, down, core = spot.at(dz=1), spot.at(dz=3), spot.other()
    half = ROWS // 2
    low, high = pl.ds(0, half), pl.ds(half, half)
    here, below, above, far = (spot.block(dz) for dz in (0, 3, 1, 2))
    a = post.copy(own, rows.at[here], up)
    b = post.copy(own, rows.at[here], down)
    k0 = post.copy(own, rows.at[here], core)
    keep = post.local(own, rows.at[here])
    for copy in (a, b, k0, keep):
        copy.start()
    yield
    a.wait_recv()
    fa = post.copy(rows.at[below, low], rows.at[below, low], up)
    k1 = post.copy(rows.at[below], rows.at[below], core)
    fa.start()
    k1.start()
    b.wait_recv()
    fb = post.copy(rows.at[above, high], rows.at[above, high], down)
    k2 = post.copy(rows.at[above], rows.at[above], core)
    fb.start()
    k2.start()
    yield
    fa.wait_recv()
    fb.wait_recv()
    k3 = post.copy(rows.at[far], rows.at[far], core)
    k3.start()
    yield
    keep.wait()
    for copy in (k0, k1, k2, k3):
        copy.wait_recv()
    for copy in (a, b, fa, fb, k0, k1, k2, k3):
        copy.wait_send()


def in_strips(count, body):
    def step(i, carry):
        body(pl.ds(pl.multiple_of(i * 16, 16), 16))
        return carry

    lax.fori_loop(0, count // 16, step, 0)


def add_into(target, other, rows=ROWS, start=0):
    def body(strip):
        strip = pl.ds(pl.multiple_of(strip.start + start, 16), 16)
        target[strip, :] = (target[strip, :].astype(F32) + other[strip, :].astype(F32)).astype(BF16)

    in_strips(rows, body)


def scatter_rows(spot, post, part, mine, land, far, gone):
    up, down, core = spot.at(dz=1), spot.at(dz=3), spot.other()
    half = ROWS // 2
    low, high = pl.ds(0, half), pl.ds(half, half)
    steps = [lax.rem(spot.z + dz, 4) for dz in (2, 3, 1, 0)]
    to_core = [post.copy(part.at[(1 - spot.c) * 4 + s], land.at[s], core) for s in steps]
    load = [post.local(part.at[spot.c * 4 + s], mine.at[s]) for s in steps]
    for a, b in zip(to_core, load):
        a.start()
        b.start()
    yield

    def ready(k):
        to_core[k].wait_recv()
        load[k].wait()

    distant, lower, upper, here = steps
    ready(0)
    add_into(mine.at[distant], land.at[distant])
    f_low = post.copy(mine.at[distant, low], far.at[low], down)
    f_high = post.copy(mine.at[distant, high], far.at[high], up)
    f_low.start()
    f_high.start()
    ready(1)
    add_into(mine.at[lower], land.at[lower])
    d_high = post.copy(mine.at[lower, high], gone.at[0, high], down)
    d_high.start()
    ready(2)
    add_into(mine.at[upper], land.at[upper])
    u_low = post.copy(mine.at[upper, low], gone.at[1, low], up)
    u_low.start()
    ready(3)
    yield
    f_low.wait_recv()
    add_into(mine.at[lower], far, half)
    d_low = post.copy(mine.at[lower, low], gone.at[0, low], down)
    d_low.start()
    f_high.wait_recv()
    add_into(mine.at[upper], far, half, half)
    u_high = post.copy(mine.at[upper, high], gone.at[1, high], up)
    u_high.start()
    yield
    for copy in (d_high, u_low, d_low, u_high):
        copy.wait_recv()
    for copy in to_core + [f_low, f_high, d_high, u_low, d_low, u_high]:
        copy.wait_send()


def row_sum(spot, mine, land, gone, strip):
    parts = [mine[spot.z, strip, :], land[spot.z, strip, :], gone[0, strip, :], gone[1, strip, :]]
    return sum(part.astype(F32) for part in parts)


def scatter_scratch():
    block = (ROWS, WIDE)
    return [
        pltpu.VMEM((4,) + block, BF16),
        pltpu.VMEM((4,) + block, BF16),
        pltpu.VMEM(block, BF16),
        pltpu.VMEM((2,) + block, BF16),
    ]


def x_spread(spot, post, src, dst_at):
    base = post.slots(4)
    copies = [post.copy(src, dst_at(spot.own), spot.at(dx=k, core=spot.xh), base + spot.own) for k in range(4)]
    keep = post.local(src, dst_at(spot.own))
    return x_start(spot, post, copies, keep, lambda k: (src, dst_at(after(spot, k)), base + after(spot, k)))


def x_collect(spot, post, src_at, dst):
    base = post.slots(4)
    copies = [post.copy(src_at(spot.own), dst.at[spot.x], spot.seat(spot.own), base + spot.x)]
    copies += [
        post.copy(src_at(after(spot, k)), dst.at[spot.x], spot.seat(after(spot, k)), base + spot.x) for k in (1, 2, 3)
    ]
    keep = post.local(src_at(spot.own), dst.at[spot.x])

    def arrival(k):
        x = lax.rem(spot.x + k, 4)
        return src_at(spot.own), dst.at[x], base + x

    return x_start(spot, post, copies, keep, arrival)


def x_start(spot, post, copies, keep, arrival):
    for k in (2, 1, 3):
        copies[k].start()

    @pl.when(spot.home)
    def _():
        keep.start()

    @pl.when(jnp.logical_not(spot.home))
    def _():
        copies[0].start()

    def landed(k):
        src, dst, slot = arrival(k)
        pltpu.make_async_remote_copy(
            src_ref=src,
            dst_ref=dst,
            send_sem=post.out_sems.at[0],
            recv_sem=post.in_sems.at[slot],
            device_id=spot.at(dx=1),
            device_id_type=MESH,
        ).wait_recv()

    def arrive():
        for k in (1, 3, 2):
            landed(k)

        @pl.when(spot.home)
        def _():
            keep.wait()

        @pl.when(jnp.logical_not(spot.home))
        def _():
            landed(0)

    def leave():
        for k in (1, 2, 3):
            copies[k].wait_send()

        @pl.when(jnp.logical_not(spot.home))
        def _():
            copies[0].wait_send()

    return arrive, leave


def gather_first(spot, post, shard, row, stage):
    keep = post.local(shard.at[1], stage.at[spot.y])
    along_y = [post.copy(shard.at[1], stage.at[spot.y], spot.at(dy=k)) for k in (2, 1, 3)]
    for copy in [keep] + along_y:
        copy.start()
    yield
    arrive, leave = x_spread(spot, post, shard.at[0], lambda slot: row.at[slot])
    yield
    keep.wait()
    for copy in along_y:
        copy.wait_recv()
    arrive()
    leave()
    for copy in along_y:
        copy.wait_send()


def gather_second(spot, post, row, stage, full):
    here = full.at[spot.y, :, 0]
    keep = post.local(row, here)
    along_y = [post.copy(row, here, spot.at(dy=k)) for k in (2, 1, 3)]
    for copy in along_y + [keep]:
        copy.start()
    arrive, leave = x_spread(spot, post, stage, lambda slot: full.at[:, slot, 1])
    yield
    keep.wait()
    for copy in along_y:
        copy.wait_recv()
    arrive()
    leave()
    for copy in along_y:
        copy.wait_send()


def gather_x_y(spot, post, shard, row, full):
    arrive, leave = x_spread(spot, post, shard, lambda slot: row.at[slot])
    yield
    arrive()
    keep = post.local(row, full.at[spot.y])
    along_y = [post.copy(row, full.at[spot.y], spot.at(dy=k)) for k in (2, 1, 3)]
    for copy in along_y + [keep]:
        copy.start()
    leave()
    yield
    for copy in along_y:
        copy.wait_recv()
    keep.wait()
    for copy in along_y:
        copy.wait_send()


def gather_sources(spot):
    return [spot.seat(after(spot, k)) for k in (1, 2, 3)], spot.seat(spot.own)


def scatter_sources(spot):
    return [spot.at(dx=k, core=spot.xh) for k in (1, 2, 3)], spot.at(core=spot.xh)


def sum_four(parts, write, rows=64):
    def body(strip):
        write(strip, sum(part[strip, :].astype(F32) for part in parts))

    in_strips(rows, body)


class Gradients:
    def __init__(self, spot, post, groups, full, from_x, from_y, sum_a, sum_b):
        self.spot, self.groups, self.full, self.from_x, self.from_y = spot, groups, full, from_x, from_y
        self.sum_a, self.sum_b = sum_a, sum_b
        self.out_sems, self.in_sems = post.out_sems, post.in_sems
        self.out_x, self.out_y = post.take_out(16), post.take_out(4)
        self.in_x, self.in_y = post.slots(16), post.slots(4)

    def y_of(self, j):
        return lax.rem(self.spot.y + j + 1, 4)

    def along_x(self, j, k):
        spot, y, slot = self.spot, self.y_of(j), after(self.spot, k)
        return pltpu.make_async_remote_copy(
            src_ref=self.full.at[y, slot, 0],
            dst_ref=self.from_x.at[y, spot.x],
            send_sem=self.out_sems.at[self.out_x + 4 * j + k],
            recv_sem=self.in_sems.at[self.in_x + 4 * j + spot.x],
            device_id=spot.seat(slot),
            device_id_type=MESH,
        )

    def stay(self, j):
        spot, y = self.spot, self.y_of(j)
        return pltpu.make_async_copy(
            self.full.at[y, spot.own, 0], self.from_x.at[y, spot.x], self.out_sems.at[self.out_x + 4 * j]
        )

    def from_chip(self, j, k):
        spot, y = self.spot, self.y_of(j)
        x = lax.rem(spot.x + k, 4)
        return pltpu.make_async_remote_copy(
            src_ref=self.full.at[y, spot.own, 0],
            dst_ref=self.from_x.at[y, x],
            send_sem=self.out_sems.at[self.out_x],
            recv_sem=self.in_sems.at[self.in_x + 4 * j + x],
            device_id=spot.at(dx=1),
            device_id_type=MESH,
        )

    def along_y(self, j):
        spot, y = self.spot, self.y_of(j)
        return pltpu.make_async_remote_copy(
            src_ref=self.full.at[y, :, 1],
            dst_ref=self.from_y.at[j],
            send_sem=self.out_sems.at[self.out_y + j],
            recv_sem=self.in_sems.at[self.in_y + j],
            device_id=spot.at(dy=j + 1),
            device_id_type=MESH,
        )

    def make(self, j):
        spot, y = self.spot, self.y_of(j)

        def part(s, carry):
            columns = pl.ds(pl.multiple_of(y * 512 + s * 256, 256), 256)
            at = 0
            for rows, values in self.groups:
                left = rows[:, columns]
                for value in values:
                    width = value.shape[1]
                    block = dot(left, value[...], 0, 0).astype(BF16)
                    for i in range(4):
                        self.full[y, 2 * s + i // 2, i % 2, :, at : at + width] = block[i * 64 : (i + 1) * 64]
                    at += width
            return carry

        lax.fori_loop(0, 2, part, 0)
        for k in (2, 1, 3):
            self.along_x(j, k).start()

        @pl.when(spot.home)
        def _():
            self.stay(j).start()

        @pl.when(jnp.logical_not(spot.home))
        def _():
            self.along_x(j, 0).start()

        if j < 3:
            self.along_y(j).start()

    def sum_x(self, j):
        spot, y = self.spot, self.y_of(j)
        for k in (1, 2, 3):
            self.from_chip(j, k).wait_recv()
            self.along_x(j, k).wait_send()

        @pl.when(spot.home)
        def _():
            self.stay(j).wait()

        @pl.when(jnp.logical_not(spot.home))
        def _():
            self.from_chip(j, 0).wait_recv()
            self.along_x(j, 0).wait_send()

        def write(strip, total):
            self.sum_a[y, strip, :] = total.astype(BF16)

        sum_four([self.from_x.at[y, x] for x in range(4)], write)

    def sum_y(self):
        for j in range(3):
            self.along_y(j).wait_recv()
            self.along_y(j).wait_send()

        def slot_sum(slot, carry):
            def write(strip, total):
                self.sum_b[slot, strip, :] = total.astype(BF16)

            sum_four([self.from_y.at[j, slot] for j in range(3)] + [self.full.at[self.spot.y, slot, 1]], write)
            return carry

        lax.fori_loop(0, 4, slot_sum, 0)

    def steps(self):
        for j in range(4):
            self.make(j)
            yield
        for j in range(4):
            self.sum_x(j)
            yield
        self.sum_y()


def load(post, pairs):
    copies = [post.local(src, dst) for src, dst in pairs]
    for copy in copies:
        copy.start()
    return copies


def gradient_scratch(n):
    return [pltpu.VMEM((4, 4, 2, 64, n), BF16), pltpu.VMEM((4, 4, 64, n), BF16), pltpu.VMEM((3, 4, 64, n), BF16)]


def scatter_second(spot, post, sum_a, sum_b, out, last_y, last_x):
    along_y = []
    for i, k in enumerate((2, 1, 3)):
        along_y.append(post.copy(sum_a.at[lax.rem(spot.y + k, 4)], last_y.at[i], spot.at(dy=k)))
    keep = post.local(sum_a.at[spot.y], last_y.at[3])
    for copy in along_y + [keep]:
        copy.start()
    arrive, leave = x_collect(spot, post, lambda slot: sum_b.at[slot], last_x)
    yield
    for copy in along_y:
        copy.wait_recv()
    keep.wait()

    def write_low(strip, total):
        out[strip, :] = total

    sum_four([last_y.at[j] for j in range(4)], write_low)
    arrive()

    def write_high(strip, total):
        out[pl.ds(pl.multiple_of(strip.start + 64, 16), 16), :] = total

    sum_four([last_x.at[j] for j in range(4)], write_high)
    leave()
    for copy in along_y:
        copy.wait_send()


def second_scratch(n):
    return [pltpu.VMEM((4, 64, n), BF16), pltpu.VMEM((4, 64, n), BF16)]


def sum_gains(spot, post, parts, out, from_y, over_y, from_chip, over_fsdp, from_tp):
    y_copies = []
    for i, k in enumerate((2, 1, 3)):
        y = lax.rem(spot.y + k, 4)
        y_copies.append(post.copy(parts.at[pl.ds(y * 4, 4)], from_y.at[i], spot.at(dy=k)))
        y_copies[-1].start()
    yield
    for copy in y_copies:
        copy.wait_recv()
    over_y[...] = parts[pl.ds(spot.y * 4, 4)] + from_y[0] + from_y[1] + from_y[2]
    chip_copies = []
    for i, k in enumerate((1, 2, 3)):
        slot = after(spot, k)
        chip_copies.append(post.copy(over_y.at[slot], from_chip.at[i], spot.bench(slot)))
        chip_copies[-1].start()
    yield
    for copy in chip_copies:
        copy.wait_recv()
    over_fsdp[...] = over_y[spot.own] + from_chip[0] + from_chip[1] + from_chip[2]
    tp_copies = []
    for i, (dz, dx) in enumerate(TP_MOVES):
        tp_copies.append(post.copy(over_fsdp, from_tp.at[i], spot.at(dz=dz, dx=dx)))
        tp_copies[-1].start()
    yield
    for copy in tp_copies:
        copy.wait_recv()
    out[...] = over_fsdp[...] + sum(from_tp[i] for i in range(7))
    for copy in y_copies + chip_copies + tp_copies:
        copy.wait_send()


TP_MOVES = [(dz, dx) for dx in (0, 2) for dz in (0, 1, 2, 3) if (dz, dx) != (0, 0)]


def gain_sources(spot):
    return (
        y_peers(spot)
        + [spot.bench(after(spot, k)) for k in (1, 2, 3)]
        + [spot.at(dz=(4 - dz) % 4, dx=dx) for dz, dx in TP_MOVES]
    )


ANY = pl.BlockSpec(memory_space=pl.ANY)
INSIDE = pl.BlockSpec(memory_space=pltpu.VMEM)


def sems(n):
    return [pltpu.SemaphoreType.DMA((n,)), pltpu.SemaphoreType.DMA((n,))]


def moving(kernel, name, outs, inputs, in_specs, out_specs, scratch, cid):
    return pl.pallas_call(
        kernel,
        name=name,
        out_shape=outs,
        in_specs=in_specs,
        out_specs=out_specs,
        scratch_shapes=scratch,
        compiler_params=pltpu.CompilerParams(collective_id=cid, has_side_effects=True, vmem_limit_bytes=VMEM),
    )(*inputs)


def shape(dims, dtype):
    return jax.ShapeDtypeStruct(dims, dtype)


def normed(rows, gain):
    inverse = lax.rsqrt(jnp.mean(rows * rows, -1, keepdims=True) + EPS)
    scaled = rows * inverse
    return inverse, scaled, (scaled * gain).astype(BF16)


def enter(tokens, gain, shard):
    n = shard.shape[1]

    def kernel(tokens_ref, gain_ref, shard_ref, rows_ref, full_ref, row_ref, stage_ref, own, out_sems, in_sems):
        spot, post = Spot(), Post(out_sems, in_sems)
        seats, away = gather_sources(spot)
        greet(spot, row_peers(spot) + y_peers(spot) + seats, away, 9)

        def weights():
            yield from gather_first(spot, post, shard_ref, row_ref, stage_ref)
            yield from gather_second(spot, post, row_ref, stage_ref, full_ref)

        w = weights()
        next(w)
        next(w)

        def body(strip):
            own[strip, :] = normed(tokens_ref[strip, :].astype(F32), gain_ref[...])[2]

        in_strips(ROWS, body)
        play("rwrrrw", r=gather_rows(spot, post, own, rows_ref), w=w)

    half = pltpu.VMEM((4, 64, n), BF16)
    return moving(
        kernel,
        "enter",
        (shape((8, ROWS, WIDE), BF16), shape((4, 4, 2, 64, n), BF16)),
        (tokens, gain, shard.reshape(2, 64, n)),
        [INSIDE] * 3,
        (ANY,) * 2,
        [half, half, pltpu.VMEM((ROWS, WIDE), BF16)] + sems(40),
        1,
    )


def middle(part, tokens, gain, row, stage):
    n = row.shape[-1]

    def kernel(part_ref, tokens_ref, gain_ref, row_ref, stage_ref, mid_ref, rows_ref, full_ref, own, *rest):
        scatter, (out_sems, in_sems) = rest[:4], rest[4:]
        mine, land, far, gone = scatter
        spot, post = Spot(), Post(out_sems, in_sems)
        seats, away = gather_sources(spot)
        greet(spot, row_peers(spot) + y_peers(spot) + seats, away, 9)

        def main():
            yield from scatter_rows(spot, post, part_ref, mine, land, far, gone)

            def body(strip):
                mid = tokens_ref[strip, :].astype(F32) + row_sum(spot, mine, land, gone, strip)
                mid_ref[strip, :] = mid
                own[strip, :] = normed(mid, gain_ref[...])[2]

            in_strips(ROWS, body)
            yield from gather_rows(spot, post, own, rows_ref)

        play("mwmmmmmm", m=main(), w=gather_second(spot, post, row_ref, stage_ref, full_ref))

    return moving(
        kernel,
        "middle",
        (shape((ROWS, WIDE), F32), shape((8, ROWS, WIDE), BF16), shape((4, 4, 2, 64, n), BF16)),
        (part, tokens, gain, row, stage),
        [ANY, INSIDE, INSIDE, INSIDE, INSIDE],
        (INSIDE, ANY, ANY),
        [pltpu.VMEM((ROWS, WIDE), BF16)] + scatter_scratch() + sems(64),
        2,
    )


def norm_back(upstream, rows, gain):
    inverse, scaled, _ = normed(rows, gain)
    weighted = upstream * gain
    through = inverse * (weighted - scaled * jnp.mean(weighted * scaled, -1, keepdims=True))
    return through, jnp.sum(upstream * scaled, 0, keepdims=True)


def turn(part, mid, gain, cotangent, rows, grads, d_gate, d_up, hidden, weights):
    n = 3 * PACK
    count = 8 * ROWS

    def kernel(
        part_ref, mid_ref, gain_ref, cot_ref, rows_hbm, grads_hbm, gate_hbm, up_hbm, hid_hbm, weights_hbm,
        grad_ref, mid_rows_ref, feed_ref, sum_a, sum_b, out_hbm,
        own, rows_ref, grads_ref, gate_ref, up_ref, hid_ref, down_ref, out_ref, *rest,
    ):
        first, room, (out_sems, in_sems) = rest[:4], rest[4:7], rest[7:]
        spot, post = Spot(), Post(out_sems, in_sems)
        sources, away = scatter_sources(spot)
        loads = load(
            post,
            [(gate_hbm, gate_ref), (up_hbm, up_ref), (rows_hbm, rows_ref), (hid_hbm, hid_ref), (grads_hbm, grads_ref)]
            + [(weights_hbm.at[:, pl.ds(2 * PACK, PACK)], down_ref)],
        )
        greet(spot, row_peers(spot) + y_peers(spot) + sources, away, 9)

        def main():
            yield from scatter_rows(spot, post, part_ref, *first)
            feed_ref[...] = jnp.zeros_like(feed_ref)

            def body(strip):
                upstream = row_sum(spot, first[0], first[1], first[3], strip)
                through, feed = norm_back(upstream, mid_ref[strip, :], gain_ref[...])
                grad = cot_ref[strip, :].astype(F32) + through
                grad_ref[strip, :] = grad
                own[strip, :] = grad.astype(BF16)
                feed_ref[...] += feed

            in_strips(ROWS, body)
            yield from gather_rows(spot, post, own, mid_rows_ref)

        def gradients():
            for copy in loads:
                copy.wait()
            groups = [(rows_ref, (gate_ref, up_ref)), (grads_ref, (hid_ref,))]
            yield from Gradients(spot, post, groups, *room, sum_a, sum_b).steps()

        def output():
            def step(i, carry):
                rows = pl.ds(pl.multiple_of(i * 256, 256), 256)
                out_ref[rows, :] = dot(hid_ref[rows, :], down_ref[...], 1, 1).astype(BF16)
                return carry

            lax.fori_loop(0, count // 256, step, 0)
            store = post.local(out_ref, out_hbm)
            store.start()
            yield
            store.wait()

        play("mgmgmgmgomgmmgggo", m=main(), g=gradients(), o=output())

    half = shape((4, 64, n), BF16)
    wide = pltpu.VMEM((count, WIDE), BF16)
    narrow = pltpu.VMEM((count, PACK), BF16)
    return moving(
        kernel,
        "turn",
        (
            shape((ROWS, WIDE), F32),
            shape((8, ROWS, WIDE), BF16),
            shape((1, WIDE), F32),
            half,
            half,
            shape((count, WIDE), BF16),
        ),
        (part, mid, gain, cotangent, rows, grads, d_gate, d_up, hidden, weights),
        [ANY, INSIDE, INSIDE, INSIDE] + [ANY] * 6,
        (INSIDE, ANY, INSIDE, INSIDE, INSIDE, ANY),
        [pltpu.VMEM((ROWS, WIDE), BF16), wide, wide, narrow, narrow, narrow, pltpu.VMEM((WIDE, PACK), BF16), wide]
        + scatter_scratch()
        + gradient_scratch(n)
        + sems(80),
        3,
    )


def leave(part, tokens, gain, grad_mid, feed_part, rows, d_qkv, mid_rows, mixed):
    n_qkv, n_out = d_qkv.shape[1], mixed.shape[1]
    n = n_qkv + n_out
    count = 8 * ROWS

    def kernel(
        part_ref, tokens_ref, gain_ref, grad_ref, feed_ref, rows_hbm, d_hbm, mid_hbm, mixed_hbm, token_ref, gains_ref,
        weight_ref, norm_part, parts, from_y, over_y, from_chip, over_fsdp, from_tp, rows_ref, d_ref, mid_ref, mixed_ref, *rest,
    ):
        first, room, (sum_a, sum_b), last, (out_sems, in_sems) = rest[:4], rest[4:7], rest[7:9], rest[9:11], rest[11:]
        spot, post = Spot(), Post(out_sems, in_sems)
        sources, away = scatter_sources(spot)
        loads = load(post, [(d_hbm, d_ref), (rows_hbm, rows_ref), (mixed_hbm, mixed_ref), (mid_hbm, mid_ref)])
        greet(spot, row_peers(spot) + y_peers(spot) + sources + gain_sources(spot), away, 9 + 13)

        def main():
            yield from scatter_rows(spot, post, part_ref, *first)
            norm_part[...] = jnp.zeros_like(norm_part)

            def body(strip):
                upstream = row_sum(spot, first[0], first[1], first[3], strip)
                through, norm = norm_back(upstream, tokens_ref[strip, :].astype(F32), gain_ref[...])
                token_ref[strip, :] = grad_ref[strip, :] + through
                norm_part[...] += norm

            in_strips(ROWS, body)
            parts[...] = jnp.zeros_like(parts)
            for f in range(16):
                parts[f, 0:1, :] = norm_part[:, f * 128 : (f + 1) * 128]
                parts[f, 1:2, :] = feed_ref[:, f * 128 : (f + 1) * 128]
            yield from sum_gains(spot, post, parts, gains_ref, from_y, over_y, from_chip, over_fsdp, from_tp)

        def gradients():
            for copy in loads:
                copy.wait()
            groups = [(rows_ref, (d_ref,)), (mid_ref, (mixed_ref,))]
            yield from Gradients(spot, post, groups, *room, sum_a, sum_b).steps()
            yield from scatter_second(spot, post, sum_a, sum_b, weight_ref, *last)

        play("mgmgmgggggmgmmgmgm", m=main(), g=gradients())

    small = (8, 128)
    wide = pltpu.VMEM((count, WIDE), BF16)
    return moving(
        kernel,
        "leave",
        (shape((ROWS, WIDE), F32), shape(small, F32), shape((ROWS, n), F32)),
        (part, tokens, gain, grad_mid, feed_part, rows, d_qkv, mid_rows, mixed),
        [ANY, INSIDE, INSIDE, INSIDE, INSIDE] + [ANY] * 4,
        (INSIDE, INSIDE, INSIDE),
        [pltpu.VMEM((1, WIDE), F32), pltpu.VMEM((16,) + small, F32)]
        + [pltpu.VMEM(dims + small, F32) for dims in ((3, 4), (4,), (3,), (), (7,))]
        + [wide, pltpu.VMEM((count, n_qkv), BF16), wide, pltpu.VMEM((count, n_out), BF16)]
        + scatter_scratch()
        + gradient_scratch(n)
        + second_scratch(n) * 2
        + sems(100),
        4,
    )


def dot(a, b, da=1, db=0):
    return lax.dot_general(a, b, (((da,), (db,)), ((), ())), preferred_element_type=F32)


def plain(kernel, name, grid, inputs, in_specs, outs, out_specs, scratch=()):
    return pl.pallas_call(
        kernel,
        name=name,
        out_shape=outs,
        grid=grid,
        in_specs=in_specs,
        out_specs=out_specs,
        scratch_shapes=list(scratch),
        compiler_params=pltpu.CompilerParams(vmem_limit_bytes=VMEM),
    )(*inputs)


def by_rows(n, width, column=0):
    return pl.BlockSpec((n, width), lambda i: (i, column))


def whole(dims, *index):
    at = index or (0,) * len(dims)
    return pl.BlockSpec(dims, lambda i: at)


def project(rows, weights, cosine, sine):
    step = 256

    def kernel(rows_ref, w_ref, cos_ref, sin_ref, q_ref, kv_ref):
        out = dot(rows_ref[...], w_ref[...])
        cos, sin = cos_ref[...], sin_ref[...]
        for head in range(4):
            u = out[:, head * HD : (head + 1) * HD]
            turned = (u * cos + pltpu.roll(u, HD // 2, 1) * sin).astype(BF16)
            target = q_ref if head < 2 else kv_ref.at[0]
            target[:, head % 2 * HD : (head % 2 + 1) * HD] = turned
        kv_ref[1] = out[:, 4 * HD :].astype(BF16)

    out = shape((8 * ROWS, 2 * HD), BF16)
    return plain(
        kernel,
        "project",
        (8 * ROWS // step,),
        (rows, weights, cosine, sine),
        [by_rows(step, WIDE), whole((WIDE, PACK)), by_rows(step, HD), by_rows(step, HD)],
        (out, shape((2,) + out.shape, BF16)),
        (by_rows(step, 2 * HD), pl.BlockSpec((2, step, 2 * HD), lambda i: (0, i, 0))),
    )


def partial_rows(pairs, name, extra=None):
    step = 256
    sets = [pairs] + ([extra] if extra else [])
    flat = [pair for group in sets for pair in group]

    def kernel(*refs):
        values, outs = refs[: 2 * len(flat)], refs[2 * len(flat) :]
        at = 0
        for group, out in zip(sets, outs):
            total = None
            for _ in group:
                term = dot(values[at][...], values[at + 1][...], 1, 1)
                total = term if total is None else total + term
                at += 2
            out[...] = total.astype(BF16)

    inputs, specs = [], []
    for a, b, width, column in flat:
        inputs += [a, b]
        specs += [by_rows(step, width), whole((WIDE, width), 0, column)]
    out = tuple(shape((8 * ROWS, WIDE), BF16) for _ in sets)
    return plain(kernel, name, (8 * ROWS // step,), inputs, specs, out, tuple(by_rows(step, WIDE) for _ in sets))


def feed_forward(rows, grads, weights):
    step = 256

    def kernel(rows_ref, grads_ref, g_ref, u_ref, d_ref, hid_ref, dgate_ref, dup_ref):
        gate = dot(rows_ref[...], g_ref[...])
        up = dot(rows_ref[...], u_ref[...])
        d_hid = dot(grads_ref[...], d_ref[...])
        sigma = 1.0 / (1.0 + jnp.exp(-gate))
        silu = gate * sigma
        hid_ref[...] = (silu * up).astype(BF16)
        dup_ref[...] = (d_hid * silu).astype(BF16)
        dgate_ref[...] = (d_hid * up * sigma * (1.0 + gate * (1.0 - sigma))).astype(BF16)

    out = shape((8 * ROWS, PACK), BF16)
    return plain(
        kernel,
        "feed_forward",
        (8 * ROWS // step,),
        (rows, grads, weights, weights, weights),
        [by_rows(step, WIDE)] * 2 + [whole((WIDE, PACK), 0, i) for i in range(3)],
        (out,) * 3,
        (by_rows(step, PACK),) * 3,
    )


def back_to_heads(rows, weights):
    step = 256

    def kernel(rows_ref, w_ref, out_ref):
        out_ref[...] = dot(rows_ref[...], w_ref[...]).astype(BF16)

    return plain(
        kernel,
        "back_to_heads",
        (8 * ROWS // step,),
        (rows, weights),
        [by_rows(step, WIDE), whole((WIDE, 2 * HD))],
        shape((8 * ROWS, 2 * HD), BF16),
        by_rows(step, 2 * HD),
    )


TILE = 256
CHUNK = 512


def place_of(start, count, xh, axis):
    dims = (count, 1) if axis == 0 else (1, count)
    j = lax.broadcasted_iota(jnp.int32, dims, axis)
    return 2 * (j + start) - lax.rem(j, ROWS) + xh * ROWS


SPANS = ((0, 512, False), (512, 256, True))
LAST = (768, 256, True)


def scores_of(keys, q, span, q_pos, prefix, xh):
    start, count, masked = span
    scores = dot(keys, q, 1, 1) * (SCALE * LOG2E)
    if masked:
        k_pos = place_of(start, count, xh, 0)
        scores = jnp.where(jnp.logical_or(k_pos <= q_pos, k_pos < prefix), scores, -1e30)
    return scores


def tile_at(i):
    head, tile = lax.div(i, 4), lax.rem(i, 4)
    return head, tile, pl.ds(pl.multiple_of(head * HD, HD), HD), pl.ds(pl.multiple_of(tile * TILE, TILE), TILE)


def exchange(post, src, dst, device):
    copy = post.copy(src, dst, device)
    copy.start()
    yield
    copy.wait_recv()
    yield
    copy.wait_send()


def attend(meta, queries, here, cotangent, shard, shard_out):
    n, n_out = shard.shape[1], shard_out.shape[1]

    def kernel(
        meta_ref, q_ref, here_ref, cot_ref, shard_ref, shard_out_ref, o_ref, lse_ref, there_ref, grads_ref, row_ref, stage_ref,
        out_ref, top_ref, sum_ref, acc_ref, row_out_ref, out_sems, in_sems,
    ):
        prefix = meta_ref[0]
        spot, post = Spot(), Post(out_sems, in_sems)
        seats, away = gather_sources(spot)
        partner = spot.at(dx=2)
        greet(spot, row_peers(spot) + y_peers(spot) + seats + [partner], away, 10)

        def compute():
            for side, keys_ref in enumerate((here_ref, there_ref)):
                xh = spot.xh if side == 0 else 1 - spot.xh

                def step(i, carry, side=side, keys_ref=keys_ref, xh=xh):
                    head, tile, cols, rows = tile_at(i)
                    q = q_ref[rows, cols]
                    q_pos = place_of(tile * TILE, TILE, spot.xh, 1)
                    one = pl.ds(i, 1)

                    def chunk(span, first):
                        keys = pl.ds(span[0], span[1])
                        scores = scores_of(keys_ref[0, keys, cols], q, span, q_pos, prefix, xh)
                        top = jnp.max(scores, 0, keepdims=True)
                        if not first:
                            before = top_ref[one, :]
                            top = jnp.maximum(top, before)
                        raised = jnp.exp2(scores - top)
                        total = jnp.sum(raised, 0, keepdims=True)
                        mixed = dot(keys_ref[1, keys, cols], raised.astype(BF16), 0, 0)
                        if not first:
                            fade = jnp.exp2(before - top)
                            total = total + sum_ref[one, :] * fade
                            mixed = mixed + acc_ref[i] * fade
                        top_ref[one, :] = top
                        sum_ref[one, :] = total
                        acc_ref[i] = mixed

                    for number, span in enumerate(SPANS):
                        chunk(span, side == 0 and number == 0)

                    @pl.when(tile == 3)
                    def _():
                        chunk(LAST, False)

                    if side == 1:
                        total = sum_ref[one, :]
                        o_ref[rows, cols] = (acc_ref[i] / total).T.astype(BF16)
                        lse_ref[one, :] = top_ref[one, :] + jnp.log2(total)
                    return carry

                lax.fori_loop(0, 8, step, 0)
                yield

        play(
            "vewscsvsewcesw",
            v=gather_x_y(spot, post, shard_out_ref, row_out_ref, out_ref),
            e=exchange(post, here_ref, there_ref, partner),
            w=gather_first(spot, post, shard_ref, row_ref, stage_ref),
            s=gather_rows(spot, post, cot_ref, grads_ref),
            c=compute(),
        )

    half = shape((4, 64, n), BF16)
    return moving(
        kernel,
        "attend",
        (
            shape((8 * ROWS, 2 * HD), BF16),
            shape((8, TILE), F32),
            shape(here.shape, BF16),
            shape((8, ROWS, WIDE), BF16),
            half,
            half,
            shape((4, 4, ROWS, n_out), BF16),
        ),
        (meta, queries, here, cotangent, shard.reshape(2, 64, n), shard_out),
        [pl.BlockSpec(memory_space=pltpu.SMEM)] + [INSIDE] * 5,
        (INSIDE, INSIDE, INSIDE, ANY, INSIDE, INSIDE, ANY),
        [pltpu.VMEM((8, TILE), F32), pltpu.VMEM((8, TILE), F32), pltpu.VMEM((8, HD, TILE), F32)]
        + [pltpu.VMEM((4, ROWS, n_out), BF16)]
        + sems(60),
        5,
    )


def attend_back(meta, queries, here, there, grads, mixed, lse, cosine, sine, out_part, mid, sum_a, sum_b):
    n = sum_a.shape[-1]

    def kernel(
        meta_ref, q_ref, here_ref, there_ref, g_ref, o_ref, lse_ref, cos_ref, sin_ref, part_ref, mid_ref, sum_a_ref, sum_b_ref,
        d_ref, layer_ref, weight_ref, delta_ref, dq_ref, acc_ref, near_ref, away_ref, land_ref, *rest,
    ):
        second, last, (out_sems, in_sems) = rest[:4], rest[4:6], rest[6:]
        prefix = meta_ref[0]
        spot, post = Spot(), Post(out_sems, in_sems)
        sources, away = scatter_sources(spot)
        partner = spot.at(dx=2)
        greet(spot, row_peers(spot) + y_peers(spot) + sources + [partner], away, 10)

        def sweep(head, side, keys_ref, into):
            xh = spot.xh if side == 0 else 1 - spot.xh
            cols = pl.ds(head * HD, HD)
            into[...] = jnp.zeros_like(into)

            def step(tile, carry):
                i = head * 4 + tile
                rows = pl.ds(pl.multiple_of(tile * TILE, TILE), TILE)
                q, g = q_ref[rows, cols], g_ref[rows, cols]
                q_pos = place_of(tile * TILE, TILE, spot.xh, 1)
                if side == 1:
                    product = g.astype(F32) * o_ref[rows, cols].astype(F32)
                    delta_ref[pl.ds(i, 1), :] = jnp.sum(product.T, 0, keepdims=True)
                level, offset = lse_ref[pl.ds(i, 1), :], delta_ref[pl.ds(i, 1), :]

                def chunk(span, first):
                    span_rows = pl.ds(span[0], span[1])
                    keys = keys_ref[0, span_rows, cols]
                    probs = jnp.exp2(scores_of(keys, q, span, q_pos, prefix, xh) - level)
                    d_probs = dot(keys_ref[1, span_rows, cols], g, 1, 1)
                    d_scores = (probs * (d_probs - offset)).astype(BF16)
                    into[0, span_rows, :] += dot(d_scores, q)
                    into[1, span_rows, :] += dot(probs.astype(BF16), g)
                    d_query = dot(d_scores, keys, 0, 0)
                    dq_ref[i] = d_query if first else dq_ref[i] + d_query

                for number, span in enumerate(SPANS):
                    chunk(span, side == 1 and number == 0)

                @pl.when(tile == 3)
                def _():
                    chunk(LAST, False)

                if side == 0:
                    u = dq_ref[i] * SCALE
                    d_ref[rows, cols] = (u * cos_ref[rows, :] - pltpu.roll(u, HD // 2, 1) * sin_ref[rows, :]).astype(BF16)
                return carry

            lax.fori_loop(0, 4, step, 0)

        def compute():
            copies = []
            for head in range(2):
                sweep(head, 1, there_ref, acc_ref)
                away_ref[head] = acc_ref[...].astype(BF16)
                copies.append(post.copy(away_ref.at[head], land_ref.at[head], partner))
                copies[-1].start()
                yield
            for head in range(2):
                sweep(head, 0, here_ref, near_ref.at[head])
                yield
            for head in range(2):
                copies[head].wait_recv()
                cols = pl.ds(2 * HD + head * HD, HD)

                def finish(i, carry, head=head):
                    rows = pl.ds(pl.multiple_of(i * 128, 128), 128)
                    u = (near_ref[head, 0, rows, :] + land_ref[head, 0, rows, :].astype(F32)) * SCALE
                    back = u * cos_ref[rows, :] - pltpu.roll(u, HD // 2, 1) * sin_ref[rows, :]
                    d_ref[rows, pl.ds(2 * HD + head * HD, HD)] = back.astype(BF16)
                    v = near_ref[head, 1, rows, :] + land_ref[head, 1, rows, :].astype(F32)
                    d_ref[rows, pl.ds(4 * HD + head * HD, HD)] = v.astype(BF16)
                    return carry

                lax.fori_loop(0, 8, finish, 0)
            for copy in copies:
                copy.wait_send()

        def output():
            yield from scatter_rows(spot, post, part_ref, *second)

            def body(strip):
                layer_ref[strip, :] = (mid_ref[strip, :] + row_sum(spot, second[0], second[1], second[3], strip)).astype(BF16)

            in_strips(ROWS, body)

        play(
            "owcococowc",
            c=compute(),
            o=output(),
            w=scatter_second(spot, post, sum_a_ref, sum_b_ref, weight_ref, *last),
        )

    pair = (2, 8 * ROWS, HD)
    return moving(
        kernel,
        "attend_back",
        (shape((8 * ROWS, PACK), BF16), shape((ROWS, WIDE), BF16), shape((ROWS, n), F32)),
        (meta, queries, here, there, grads, mixed, lse, cosine, sine, out_part, mid, sum_a, sum_b),
        [pl.BlockSpec(memory_space=pltpu.SMEM)] + [INSIDE] * 8 + [ANY, INSIDE, ANY, ANY],
        (INSIDE,) * 3,
        [
            pltpu.VMEM((8, TILE), F32),
            pltpu.VMEM((8, TILE, HD), F32),
            pltpu.VMEM(pair, F32),
            pltpu.VMEM((2,) + pair, F32),
            pltpu.VMEM((2,) + pair, BF16),
            pltpu.VMEM((2,) + pair, BF16),
        ]
        + scatter_scratch()
        + second_scratch(n)
        + sems(64),
        6,
    )


def padded(shard):
    return jnp.pad(shard, ((0, 0), (0, PACK - shard.shape[1])))


def rope_tables(positions):
    counter = jnp.arange(HD // 2, dtype=F32)
    inverse = jnp.exp(counter * (-2.0 / HD) * math.log(ROPE_BASE))
    angles = positions.astype(F32)[:, None] * inverse[None, :]
    cosine, sine = jnp.cos(angles), jnp.sin(angles)
    return jnp.concatenate([cosine, cosine], 1), jnp.concatenate([-sine, sine], 1)


def on_device(
    tokens,
    prefixes,
    norm_gain,
    query_weight,
    key_weight,
    value_weight,
    output_weight,
    feed_gain,
    gate_weight,
    up_weight,
    down_weight,
    cotangent,
):
    sequence = lax.axis_index("fsdp") // 2
    xh = lax.axis_index("tp") % 2
    hidden_here = gate_weight.shape[1]
    width = 2 * HD
    prefix = jnp.sum(jnp.where(jnp.arange(prefixes.shape[0], dtype=jnp.int32) == sequence, prefixes, 0))
    meta = jnp.stack([prefix, xh]).astype(jnp.int32)
    j = jnp.arange(8 * ROWS, dtype=jnp.int32)
    cosine, sine = rope_tables(2 * j - j % ROWS + xh * ROWS)
    gain_one = norm_gain.astype(F32)[None]
    gain_two = feed_gain.astype(F32)[None]
    shard_one = jnp.concatenate([query_weight, key_weight, value_weight], 1)
    shard_two = jnp.concatenate([padded(gate_weight), padded(up_weight), padded(down_weight.T)], 1)

    rows_one, full_one = enter(tokens, gain_one, shard_one)
    rows_one = rows_one.reshape(-1, WIDE)
    full_one = full_one.reshape(WIDE, -1)
    queries, here = project(rows_one, full_one, cosine, sine)
    attended, lse, there, grad_rows, row_two, stage_two, full_out = attend(meta, queries, here, cotangent, shard_two, output_weight.T)
    full_out = full_out.reshape(WIDE, -1)
    (part,) = partial_rows([(attended, full_out, width, 0)], "attention_out")
    mid, rows_two, full_two = middle(part.reshape(8, ROWS, WIDE), tokens, gain_two, row_two, stage_two)
    rows_two, grad_rows, full_two = (a.reshape(-1, a.shape[-1]) for a in (rows_two, grad_rows, full_two.reshape(WIDE, -1)))
    hidden, d_gate, d_up = feed_forward(rows_two, grad_rows, full_two)
    (part,) = partial_rows([(d_gate, full_two, PACK, 0), (d_up, full_two, PACK, 1)], "feed_back")
    grad_mid, mid_rows, feed_part, sum_a, sum_b, part_out = turn(
        part.reshape(8, ROWS, WIDE), mid, gain_two, cotangent, rows_two, grad_rows, d_gate, d_up, hidden, full_two
    )
    mid_rows = mid_rows.reshape(-1, WIDE)
    grad_mixed = back_to_heads(mid_rows, full_out)
    d_qkv, layer_output, ffn_grad = attend_back(
        meta, queries, here, there, grad_mixed, attended, lse, cosine, sine, part_out.reshape(8, ROWS, WIDE), mid, sum_a, sum_b
    )
    (part,) = partial_rows([(d_qkv, full_one, PACK, 0)], "attention_back")
    token_grad, gains, attention_grad = leave(
        part.reshape(8, ROWS, WIDE), tokens, gain_one, grad_mid, feed_part, rows_one, d_qkv, mid_rows, attended
    )
    return (
        layer_output,
        token_grad,
        gains[0],
        attention_grad[:, :width],
        attention_grad[:, width : 2 * width],
        attention_grad[:, 2 * width : 3 * width],
        attention_grad[:, 3 * width :].T,
        gains[1],
        ffn_grad[:, :hidden_here],
        ffn_grad[:, PACK : PACK + hidden_here],
        ffn_grad[:, 2 * PACK : 2 * PACK + hidden_here].T,
    )


def solution(mesh):
    rows = P(("fsdp", "tp"), None)
    wide = P("fsdp", "tp")
    tall = P("tp", "fsdp")
    return jax.shard_map(
        on_device,
        mesh=mesh,
        in_specs=(rows, P(), P(), wide, wide, wide, tall, P(), wide, wide, tall, rows),
        out_specs=(rows, rows, P("fsdp"), wide, wide, wide, tall, P("fsdp"), wide, wide, tall),
        check_vma=False,
    )
```

```python
import functools
import math

import jax
import jax.numpy as jnp
from jax import lax
from jax.experimental import pallas as pl
from jax.experimental.pallas import tpu as pltpu
from jax.sharding import PartitionSpec as P

HD = 128
EPS = 1e-05
ROPE_BASE = 10000.0
F32 = jnp.float32
BF16 = jnp.bfloat16
MESH = pl.DeviceIdType.MESH
AXES = ("fsdp", "tp")
ROWS = 128
WIDE = 2048
PACK = 768
SCALE = 1.0 / math.sqrt(HD)
LOG2E = 1.4426950408889634
VMEM = 56 << 20


class Spot:
    def __init__(self):
        f, t = lax.axis_index("fsdp"), lax.axis_index("tp")
        self.y, self.xl, self.c = lax.div(f, 4), lax.rem(lax.div(f, 2), 2), lax.rem(f, 2)
        self.z, self.xh = lax.div(t, 2), lax.rem(t, 2)
        self.x = self.xh * 2 + self.xl
        self.own = self.xl * 2 + self.c
        self.away = lax.rem(self.xh + self.c, 2)
        self.home = self.away == 0
        self.turn = 1 - lax.rem(self.away + self.xl, 2)
        self.ahead = 1 + 2 * self.turn
        self.back = 3 - 2 * self.turn
        self.near = (1 - self.xl) * 2
        self.same = self.xl * 2

    def at(self, dy=0, dx=0, dz=0, core=None):
        y, z, x = lax.rem(self.y + dy, 4), lax.rem(self.z + dz, 4), lax.rem(self.x + dx, 4)
        return (y * 4 + lax.rem(x, 2) * 2 + (self.c if core is None else core), z * 2 + lax.div(x, 2))

    def other(self):
        return self.at(core=1 - self.c)

    def seat(self, slot):
        return (self.y * 4 + slot, self.z * 2 + self.c)

    def bench(self, slot):
        return (self.y * 4 + slot, self.z * 2 + self.xh)

    def block(self, dz=0, flip=False):
        return (1 - self.c if flip else self.c) * 4 + lax.rem(self.z + dz, 4)


class Post:
    def __init__(self, out_sems, in_sems):
        self.out_sems, self.in_sems, self.n_out, self.n_in = out_sems, in_sems, 0, 0

    def slots(self, n):
        base = self.n_in
        self.n_in += n
        return base

    def copy(self, src, dst, device, slot=None):
        slot = self.slots(1) if slot is None else slot
        self.n_out += 1
        return pltpu.make_async_remote_copy(
            src_ref=src,
            dst_ref=dst,
            send_sem=self.out_sems.at[self.n_out - 1],
            recv_sem=self.in_sems.at[slot],
            device_id=device,
            device_id_type=MESH,
        )

    def arrival(self, dst, device, slot):
        return pltpu.make_async_remote_copy(
            src_ref=dst,
            dst_ref=dst,
            send_sem=self.out_sems.at[0],
            recv_sem=self.in_sems.at[slot],
            device_id=device,
            device_id_type=MESH,
        )

    def local(self, src, dst):
        self.n_out += 1
        return pltpu.make_async_copy(src, dst, self.out_sems.at[self.n_out - 1])


def greet(spot, sources, count, home=(), away=()):
    barrier = pltpu.get_barrier_semaphore()

    def signal(devices):
        for device in devices:
            pl.semaphore_signal(barrier, inc=1, device_id=device, device_id_type=MESH)

    signal(sources)
    if home:
        count = count + 3 + spot.away

        @pl.when(spot.home)
        def _():
            signal(home)

        @pl.when(jnp.logical_not(spot.home))
        def _():
            signal(away)

    pl.semaphore_wait(barrier, count)


def row_peers(spot):
    return [spot.at(dz=1), spot.at(dz=3), spot.other()]


def y_peers(spot):
    return [spot.at(dy=1), spot.at(dy=3)]


def gather_peers(spot):
    near = [spot.at(dx=spot.back, core=0), spot.at(dx=spot.back, core=1)]
    return {"home": near + [spot.other()], "away": near + [spot.at(dx=1), spot.at(dx=3)]}


def collect_peers(spot):
    usual = [spot.at(dx=1, core=spot.xh), spot.at(dx=3, core=spot.xh), spot.at(dx=spot.ahead)]
    return {"home": usual, "away": usual + [spot.other()]}


def half_of(ref, number):
    rows = ref.shape[0] // 2
    return ref.at[pl.ds(number * rows, rows)]


def after(spot, k):
    return lax.rem(spot.own + k, 4)


def play(order, **jobs):
    for letter in order:
        next(jobs[letter], None)
    for job in jobs.values():
        for _ in job:
            pass


def gather_rows(spot, post, own, rows):
    up, down, core = spot.at(dz=1), spot.at(dz=3), spot.other()
    half = ROWS // 2
    low, high = pl.ds(0, half), pl.ds(half, half)
    here, below, above, far = (spot.block(dz) for dz in (0, 3, 1, 2))
    a = post.copy(own, rows.at[here], up)
    b = post.copy(own, rows.at[here], down)
    k0 = post.copy(own, rows.at[here], core)
    keep = post.local(own, rows.at[here])
    for copy in (a, b, k0, keep):
        copy.start()
    yield
    a.wait_recv()
    fa = post.copy(rows.at[below, low], rows.at[below, low], up)
    k1 = post.copy(rows.at[below], rows.at[below], core)
    fa.start()
    k1.start()
    b.wait_recv()
    fb = post.copy(rows.at[above, high], rows.at[above, high], down)
    k2 = post.copy(rows.at[above], rows.at[above], core)
    fb.start()
    k2.start()
    yield
    fa.wait_recv()
    fb.wait_recv()
    k3 = post.copy(rows.at[far], rows.at[far], core)
    k3.start()
    yield
    keep.wait()
    for copy in (k0, k1, k2, k3):
        copy.wait_recv()
    for copy in (a, b, fa, fb, k0, k1, k2, k3):
        copy.wait_send()


def in_strips(count, body):
    def step(i, carry):
        body(pl.ds(pl.multiple_of(i * 16, 16), 16))
        return carry

    lax.fori_loop(0, count // 16, step, 0)


def add_into(target, other, rows=ROWS, start=0):
    def body(strip):
        strip = pl.ds(pl.multiple_of(strip.start + start, 16), 16)
        target[strip, :] = (target[strip, :].astype(F32) + other[strip, :].astype(F32)).astype(BF16)

    in_strips(rows, body)


def scatter_rows(spot, post, part, mine, land, far, gone):
    up, down, core = spot.at(dz=1), spot.at(dz=3), spot.other()
    half = ROWS // 2
    low, high = pl.ds(0, half), pl.ds(half, half)
    steps = [lax.rem(spot.z + dz, 4) for dz in (2, 3, 1, 0)]
    to_core = [post.copy(part.at[(1 - spot.c) * 4 + s], land.at[s], core) for s in steps]
    load = [post.local(part.at[spot.c * 4 + s], mine.at[s]) for s in steps]
    for a, b in zip(to_core, load):
        a.start()
        b.start()
    yield

    def ready(k):
        to_core[k].wait_recv()
        load[k].wait()

    distant, lower, upper, here = steps
    ready(0)
    add_into(mine.at[distant], land.at[distant])
    f_low = post.copy(mine.at[distant, low], far.at[low], down)
    f_high = post.copy(mine.at[distant, high], far.at[high], up)
    f_low.start()
    f_high.start()
    ready(1)
    add_into(mine.at[lower], land.at[lower])
    d_high = post.copy(mine.at[lower, high], gone.at[0, high], down)
    d_high.start()
    ready(2)
    add_into(mine.at[upper], land.at[upper])
    u_low = post.copy(mine.at[upper, low], gone.at[1, low], up)
    u_low.start()
    ready(3)
    yield
    f_low.wait_recv()
    add_into(mine.at[lower], far, half)
    d_low = post.copy(mine.at[lower, low], gone.at[0, low], down)
    d_low.start()
    f_high.wait_recv()
    add_into(mine.at[upper], far, half, half)
    u_high = post.copy(mine.at[upper, high], gone.at[1, high], up)
    u_high.start()
    yield
    for copy in (d_high, u_low, d_low, u_high):
        copy.wait_recv()
    for copy in to_core + [f_low, f_high, d_high, u_low, d_low, u_high]:
        copy.wait_send()


def row_sum(spot, mine, land, gone, strip):
    parts = [mine[spot.z, strip, :], land[spot.z, strip, :], gone[0, strip, :], gone[1, strip, :]]
    return sum(part.astype(F32) for part in parts)


def scatter_scratch():
    block = (ROWS, WIDE)
    return [
        pltpu.VMEM((4,) + block, BF16),
        pltpu.VMEM((4,) + block, BF16),
        pltpu.VMEM(block, BF16),
        pltpu.VMEM((2,) + block, BF16),
    ]


def x_gather(spot, post, src, dst_at):
    base, far = post.slots(4), post.slots(4)
    sends = [post.copy(src, dst_at(spot.own), spot.at(dx=dx, core=spot.xh), base + spot.own) for dx in (1, 3)]
    cross = post.copy(src, dst_at(spot.own), spot.other(), base + spot.own)
    keep = post.local(src, dst_at(spot.own))
    for copy in sends:
        copy.start()

    @pl.when(spot.home)
    def _():
        keep.start()

    @pl.when(jnp.logical_not(spot.home))
    def _():
        cross.start()

    def landed(dst, slot):
        post.arrival(dst, spot.at(dx=1), slot).wait_recv()

    yield
    for core in range(2):
        block = dst_at(spot.near + core)
        landed(block, base + spot.near + core)
        part = half_of(block, spot.turn)
        sends.append(post.copy(part, part, spot.at(dx=spot.ahead), far + 2 * core + spot.turn))
        sends[-1].start()
    yield

    @pl.when(spot.home)
    def _():
        slot = spot.same + 1 - spot.c
        landed(dst_at(slot), base + slot)
        keep.wait()

    @pl.when(jnp.logical_not(spot.home))
    def _():
        for core in range(2):
            for number in range(2):
                landed(half_of(dst_at(spot.same + core), number), far + 2 * core + number)
        cross.wait_send()

    for copy in sends:
        copy.wait_send()


def y_gather(spot, post, src, dst_at):
    up, down = spot.at(dy=1), spot.at(dy=3)
    here, below, above = dst_at(spot.y), dst_at(lax.rem(spot.y + 3, 4)), dst_at(lax.rem(spot.y + 1, 4))
    a, b, keep = post.copy(src, here, up), post.copy(src, here, down), post.local(src, here)
    for copy in (a, b, keep):
        copy.start()
    yield
    a.wait_recv()
    fa = post.copy(half_of(below, 0), half_of(below, 0), up)
    fa.start()
    b.wait_recv()
    fb = post.copy(half_of(above, 1), half_of(above, 1), down)
    fb.start()
    yield
    keep.wait()
    for copy in (fa, fb):
        copy.wait_recv()
    for copy in (a, b, fa, fb):
        copy.wait_send()


def together(*jobs):
    live = list(jobs)
    while live:
        live = [job for job in live if next(job, job) is not job]
        if live:
            yield


def gather_first(spot, post, shard, row, stage):
    return together(
        x_gather(spot, post, shard.at[0], lambda slot: row.at[slot]),
        y_gather(spot, post, shard.at[1], lambda y: stage.at[y]),
    )


def gather_second(spot, post, row, stage, full):
    return together(
        x_gather(spot, post, stage, lambda slot: full.at[:, slot, 1]),
        y_gather(spot, post, row, lambda y: full.at[y, :, 0]),
    )


def sum_parts(parts, write):
    def body(strip):
        write(strip, sum(part[strip, :].astype(F32) for part in parts))

    in_strips(parts[0].shape[0], body)


def add_block(target, other):
    if len(target.shape) == 2:
        add_into(target, other, target.shape[0])
    else:

        def step(i, carry):
            add_into(target.at[i], other.at[i], target.shape[1])
            return carry

        lax.fori_loop(0, target.shape[0], step, 0)


class XCollect:
    def __init__(self, spot, post, src_at, land, hop):
        self.spot, self.post, self.src_at, self.land, self.hop = spot, post, src_at, land, hop
        self.in_land, self.in_hop = post.slots(5), post.slots(2)
        self.sends = []

    def to_near(self, core, src, number):
        spot = self.spot
        copy = self.post.copy(
            src,
            half_of(self.land.at[spot.turn], number),
            spot.seat(spot.near + core),
            self.in_land + 2 * spot.turn + number,
        )
        copy.start()
        self.sends.append(copy)

    def start(self):
        spot, post = self.spot, self.post
        cross_slot = spot.same + 1 - spot.c
        self.cross = post.copy(self.src_at(cross_slot), self.land.at[2], spot.other(), self.in_land + 4)
        self.keep = post.local(self.src_at(spot.own), self.land.at[2])
        self.far = []
        for core in range(2):
            for number, dx in ((0, 3), (1, 1)):
                src = half_of(self.src_at(spot.same + core), number)
                self.far.append(post.copy(src, self.hop.at[core], spot.at(dx=dx), self.in_hop + core))

        @pl.when(spot.home)
        def _():
            self.cross.start()
            self.keep.start()

        @pl.when(jnp.logical_not(spot.home))
        def _():
            for copy in self.far:
                copy.start()

        for core in range(2):
            self.to_near(core, half_of(self.src_at(spot.near + core), 1 - spot.turn), 1 - spot.turn)

    def relay(self):
        spot, post = self.spot, self.post
        for core in range(2):
            post.arrival(self.hop.at[core], spot.at(dx=1), self.in_hop + core).wait_recv()
            add_block(self.hop.at[core], half_of(self.src_at(spot.near + core), spot.turn))
            self.to_near(core, self.hop.at[core], spot.turn)

    def finish(self):
        spot, post = self.spot, self.post
        for side in range(2):
            for number in range(2):
                dst = half_of(self.land.at[side], number)
                post.arrival(dst, spot.at(dx=1), self.in_land + 2 * side + number).wait_recv()

        @pl.when(spot.home)
        def _():
            self.keep.wait()
            self.cross.wait_send()

        @pl.when(jnp.logical_not(spot.home))
        def _():
            post.arrival(self.land.at[2], spot.at(dx=1), self.in_land + 4).wait_recv()
            for copy in self.far:
                copy.wait_send()

        for copy in self.sends:
            copy.wait_send()

    def parts(self):
        return [self.land.at[side] for side in range(3)]


class YCollect:
    def __init__(self, spot, post, src_at, land, hop):
        self.spot, self.post, self.src_at, self.land, self.hop = spot, post, src_at, land, hop
        self.up, self.down = spot.at(dy=1), spot.at(dy=3)
        self.y = [lax.rem(spot.y + k, 4) for k in range(4)]

    def start_far(self):
        block = self.src_at(self.y[2])
        self.far = [
            self.post.copy(half_of(block, 0), self.hop.at[0], self.down),
            self.post.copy(half_of(block, 1), self.hop.at[1], self.up),
        ]
        for copy in self.far:
            copy.start()

    def start_lower(self):
        self.low = [self.post.copy(half_of(self.src_at(self.y[3]), 1), half_of(self.land.at[0], 1), self.down)]
        self.low[0].start()

    def start_upper(self):
        self.high = [self.post.copy(half_of(self.src_at(self.y[1]), 0), half_of(self.land.at[1], 0), self.up)]
        self.high[0].start()

    def relay(self):
        for number, k, target in ((0, 3, self.down), (1, 1, self.up)):
            self.far[number].wait_recv()
            hop = self.hop.at[number]
            add_block(hop, half_of(self.src_at(self.y[k]), number))
            copy = self.post.copy(hop, half_of(self.land.at[number], number), target)
            copy.start()
            (self.low if number == 0 else self.high).append(copy)

    def finish(self):
        for copy in self.low + self.high:
            copy.wait_recv()
        for copy in self.far + self.low + self.high:
            copy.wait_send()

    def parts(self):
        return [self.src_at(self.spot.y), self.land.at[0], self.land.at[1]]


class Gradients:
    def __init__(self, spot, post, groups, full, land_x, hop_x, land_y, hop_y, sum_a, sum_b):
        self.spot, self.groups, self.full, self.sum_a, self.sum_b = spot, groups, full, sum_a, sum_b
        self.y = [lax.rem(spot.y + k, 4) for k in (2, 3, 1, 0)]
        self.x = [
            XCollect(spot, post, lambda slot, y=y: full.at[y, slot, 0], land_x.at[j], hop_x.at[j])
            for j, y in enumerate(self.y)
        ]
        self.over_y = YCollect(spot, post, lambda y: full.at[y, :, 1], land_y, hop_y)

    def make(self, j):
        y = self.y[j]

        def part(s, carry):
            columns = pl.ds(pl.multiple_of(y * 512 + s * 256, 256), 256)
            at = 0
            for rows, values in self.groups:
                left = rows[:, columns]
                for value in values:
                    width = value.shape[1]
                    block = dot(left, value[...], 0, 0).astype(BF16)
                    for i in range(4):
                        self.full[y, 2 * s + i // 2, i % 2, :, at : at + width] = block[i * 64 : (i + 1) * 64]
                    at += width
            return carry

        lax.fori_loop(0, 2, part, 0)
        (self.over_y.start_far, self.over_y.start_lower, self.over_y.start_upper, lambda: None)[j]()
        self.x[j].start()

    def sum_x(self, j):
        def write(strip, total):
            self.sum_a[self.y[j], strip, :] = total.astype(BF16)

        self.x[j].finish()
        sum_parts(self.x[j].parts(), write)

    def sum_y(self):
        self.over_y.finish()

        def slot_sum(slot, carry):
            def write(strip, total):
                self.sum_b[slot, strip, :] = total.astype(BF16)

            sum_parts([part.at[slot] for part in self.over_y.parts()], write)
            return carry

        lax.fori_loop(0, 4, slot_sum, 0)

    def steps(self):
        self.make(0)
        yield
        self.make(1)
        yield
        self.make(2)
        self.x[0].relay()
        yield
        self.make(3)
        self.x[1].relay()
        yield
        self.over_y.relay()
        self.x[2].relay()
        yield
        self.x[3].relay()
        yield
        for j in range(4):
            self.sum_x(j)
            yield
        self.sum_y()


def load(post, pairs):
    copies = [post.local(src, dst) for src, dst in pairs]
    for copy in copies:
        copy.start()
    return copies


def gradient_scratch(n):
    return [
        pltpu.VMEM((4, 4, 2, 64, n), BF16),
        pltpu.VMEM((4, 3, 64, n), BF16),
        pltpu.VMEM((4, 2, 32, n), BF16),
        pltpu.VMEM((2, 4, 64, n), BF16),
        pltpu.VMEM((2, 2, 64, n), BF16),
    ]


def scatter_low(spot, post, sum_a, write, land, hop):
    over_y = YCollect(spot, post, lambda y: sum_a.at[y], land, hop)
    over_y.start_far()
    over_y.start_lower()
    over_y.start_upper()
    yield
    over_y.relay()
    yield
    over_y.finish()
    sum_parts(over_y.parts(), write)


def scatter_high(spot, post, sum_b, write, land, hop):
    over_x = XCollect(spot, post, lambda slot: sum_b.at[slot], land, hop)
    over_x.start()
    yield
    over_x.relay()
    yield
    over_x.finish()
    sum_parts(over_x.parts(), write)


def strip_writer(out, start=0):
    def write(strip, total):
        out[pl.ds(pl.multiple_of(strip.start + start, 16), 16), :] = total

    return write


def low_scratch(n):
    return [pltpu.VMEM((2, 64, n), BF16), pltpu.VMEM((2, 32, n), BF16)]


def high_scratch(n):
    return [pltpu.VMEM((3, 64, n), BF16), pltpu.VMEM((2, 32, n), BF16)]


def sum_gains(spot, post, parts, out, from_y, over_y, from_chip, over_fsdp, from_tp):
    y_copies = []
    for i, k in enumerate((2, 1, 3)):
        y = lax.rem(spot.y + k, 4)
        y_copies.append(post.copy(parts.at[pl.ds(y * 4, 4)], from_y.at[i], spot.at(dy=k)))
        y_copies[-1].start()
    yield
    for copy in y_copies:
        copy.wait_recv()
    over_y[...] = parts[pl.ds(spot.y * 4, 4)] + from_y[0] + from_y[1] + from_y[2]
    chip_copies = []
    for i, k in enumerate((1, 2, 3)):
        slot = after(spot, k)
        chip_copies.append(post.copy(over_y.at[slot], from_chip.at[i], spot.bench(slot)))
        chip_copies[-1].start()
    yield
    for copy in chip_copies:
        copy.wait_recv()
    over_fsdp[...] = over_y[spot.own] + from_chip[0] + from_chip[1] + from_chip[2]
    tp_copies = []
    for i, (dz, dx) in enumerate(TP_MOVES):
        tp_copies.append(post.copy(over_fsdp, from_tp.at[i], spot.at(dz=dz, dx=dx)))
        tp_copies[-1].start()
    yield
    for copy in tp_copies:
        copy.wait_recv()
    out[...] = over_fsdp[...] + sum(from_tp[i] for i in range(7))
    for copy in y_copies + chip_copies + tp_copies:
        copy.wait_send()


TP_MOVES = [(dz, dx) for dx in (0, 2) for dz in (0, 1, 2, 3) if (dz, dx) != (0, 0)]


def gain_sources(spot):
    return (
        [spot.at(dy=k) for k in (1, 2, 3)]
        + [spot.bench(after(spot, k)) for k in (1, 2, 3)]
        + [spot.at(dz=(4 - dz) % 4, dx=dx) for dz, dx in TP_MOVES]
    )


ANY = pl.BlockSpec(memory_space=pl.ANY)
INSIDE = pl.BlockSpec(memory_space=pltpu.VMEM)


def sems(n):
    return [pltpu.SemaphoreType.DMA((n,)), pltpu.SemaphoreType.DMA((n,))]


def moving(kernel, name, outs, inputs, in_specs, out_specs, scratch, cid):
    return pl.pallas_call(
        kernel,
        name=name,
        out_shape=outs,
        in_specs=in_specs,
        out_specs=out_specs,
        scratch_shapes=scratch,
        compiler_params=pltpu.CompilerParams(collective_id=cid, has_side_effects=True, vmem_limit_bytes=VMEM),
    )(*inputs)


def shape(dims, dtype):
    return jax.ShapeDtypeStruct(dims, dtype)


def normed(rows, gain):
    inverse = lax.rsqrt(jnp.mean(rows * rows, -1, keepdims=True) + EPS)
    scaled = rows * inverse
    return inverse, scaled, (scaled * gain).astype(BF16)


def enter(tokens, gain, query, key, value, out, gate, up, down):
    n_one, n_two, n_out = query.shape[1] * 3, PACK * 3, out.shape[0]

    def kernel(
        tokens_ref, gain_ref, query_ref, key_ref, value_ref, out_ref, gate_ref, up_ref, down_ref,
        rows_ref, full_ref, row_out_ref, row_ref, rest_ref, cos_ref, sin_ref,
        shard_one, row_one, stage_one, shard_out, shard_two, own, out_sems, in_sems,
    ):
        spot, post = Spot(), Post(out_sems, in_sems)
        for i in range(2):
            rows = pl.ds(i * 64, 64)
            for j, ref in enumerate((query_ref, key_ref, value_ref)):
                shard_one[i, :, j * 256 : (j + 1) * 256] = ref[rows, :]
        greet(spot, row_peers(spot) + y_peers(spot), 5, **gather_peers(spot))

        def weights():
            yield from gather_first(spot, post, shard_one, row_one, stage_one)
            yield from gather_second(spot, post, row_one, stage_one, full_ref)

        def tables():
            exponent = lax.broadcasted_iota(jnp.int32, (1, HD), 1)
            exponent = lax.rem(exponent, HD // 2).astype(F32)
            inverse = jnp.exp(exponent * (-2.0 / HD) * math.log(ROPE_BASE))
            sign = jnp.where(lax.broadcasted_iota(jnp.int32, (1, HD), 1) < HD // 2, -1.0, 1.0)

            def step(i, carry):
                angles = place_of(i * 16, 16, spot.xh, 0).astype(F32) * inverse
                strip = pl.ds(pl.multiple_of(i * 16, 16), 16)
                cos_ref[strip, :] = jnp.cos(angles)
                sin_ref[strip, :] = jnp.sin(angles) * sign
                return carry

            lax.fori_loop(0, 8 * ROWS // 16, step, 0)

        w = weights()
        next(w)

        def body(strip):
            own[strip, :] = normed(tokens_ref[strip, :].astype(F32), wide_gain(gain_ref))[2]

        in_strips(ROWS, body)
        r = gather_rows(spot, post, own, rows_ref)
        next(r)
        shard_out[...] = out_ref[...].astype(F32).T.astype(BF16)
        o = x_gather(spot, post, shard_out, lambda slot: row_out_ref.at[slot])
        next(o)
        shard_two[...] = jnp.zeros_like(shard_two)
        rest_ref[...] = jnp.zeros_like(rest_ref)
        wide = gate.shape[0]
        for j, ref in enumerate((gate_ref, up_ref, down_ref)):
            turned = ref[...].astype(F32).T.astype(BF16)
            shard_two[:, j * PACK : j * PACK + wide] = turned[:64]
            rest_ref[:, j * PACK : j * PACK + wide] = turned[64:]
        next(w)
        next(w)
        f = x_gather(spot, post, shard_two, lambda slot: row_ref.at[slot])
        next(f)
        next(o)
        next(r)
        tables()
        play("wfrwfor", r=r, w=w, f=f, o=o)

    half = pltpu.VMEM((4, 64, n_one), BF16)
    table = shape((8 * ROWS, HD), F32)
    return moving(
        kernel,
        "enter",
        (shape((8, ROWS, WIDE), BF16), shape((4, 4, 2, 64, n_one), BF16), shape((4, ROWS, n_out), BF16))
        + (shape((4, 64, n_two), BF16), shape((64, n_two), BF16), table, table),
        (tokens, gain, query, key, value, out, gate, up, down),
        [INSIDE] * 9,
        (ANY, ANY) + (INSIDE,) * 5,
        [pltpu.VMEM((2, 64, n_one), BF16), half, half, pltpu.VMEM((ROWS, n_out), BF16), pltpu.VMEM((64, n_two), BF16)]
        + [pltpu.VMEM((ROWS, WIDE), BF16)]
        + sems(60),
        1,
    )


def middle(part, tokens, gain, row, stage):
    n = row.shape[-1]

    def kernel(part_ref, tokens_ref, gain_ref, row_ref, stage_ref, mid_ref, rows_ref, full_ref, own, *rest):
        scatter, (out_sems, in_sems) = rest[:4], rest[4:]
        mine, land, far, gone = scatter
        spot, post = Spot(), Post(out_sems, in_sems)
        greet(spot, row_peers(spot) + y_peers(spot), 5, **gather_peers(spot))

        def main():
            yield from scatter_rows(spot, post, part_ref, mine, land, far, gone)

            def body(strip):
                mid = tokens_ref[strip, :].astype(F32) + row_sum(spot, mine, land, gone, strip)
                mid_ref[strip, :] = mid
                own[strip, :] = normed(mid, wide_gain(gain_ref))[2]

            in_strips(ROWS, body)
            yield from gather_rows(spot, post, own, rows_ref)

        play("mwmmmwmmm", m=main(), w=gather_second(spot, post, row_ref, stage_ref, full_ref))

    return moving(
        kernel,
        "middle",
        (shape((ROWS, WIDE), F32), shape((8, ROWS, WIDE), BF16), shape((4, 4, 2, 64, n), BF16)),
        (part, tokens, gain, row, stage),
        [ANY, INSIDE, INSIDE, INSIDE, INSIDE],
        (INSIDE, ANY, ANY),
        [pltpu.VMEM((ROWS, WIDE), BF16)] + scatter_scratch() + sems(64),
        2,
    )


def wide_gain(gain_ref):
    return gain_ref[...].astype(F32).reshape(1, WIDE)


def norm_back(upstream, rows, gain):
    inverse, scaled, _ = normed(rows, gain)
    weighted = upstream * gain
    through = inverse * (weighted - scaled * jnp.mean(weighted * scaled, -1, keepdims=True))
    return through, jnp.sum(upstream * scaled, 0, keepdims=True)


def turn(part, mid, gain, cotangent, rows, grads, d_gate, d_up, hidden, weights):
    n = 3 * PACK
    count = 8 * ROWS

    def kernel(
        part_ref, mid_ref, gain_ref, cot_ref, rows_hbm, grads_hbm, gate_hbm, up_hbm, hid_hbm, weights_hbm,
        grad_ref, mid_rows_ref, feed_ref, sum_a, sum_b, out_hbm,
        own, rows_ref, grads_ref, gate_ref, up_ref, hid_ref, down_ref, out_ref, *rest,
    ):
        first, room, (out_sems, in_sems) = rest[:4], rest[4:9], rest[9:]
        spot, post = Spot(), Post(out_sems, in_sems)
        loads = load(
            post,
            [(gate_hbm, gate_ref), (up_hbm, up_ref), (rows_hbm, rows_ref), (hid_hbm, hid_ref), (grads_hbm, grads_ref)]
            + [(weights_hbm.at[:, pl.ds(2 * PACK, PACK)], down_ref)],
        )
        greet(spot, row_peers(spot) + y_peers(spot), 5, **collect_peers(spot))

        def main():
            yield from scatter_rows(spot, post, part_ref, *first)
            feed_ref[...] = jnp.zeros_like(feed_ref)

            def body(strip):
                upstream = row_sum(spot, first[0], first[1], first[3], strip)
                through, feed = norm_back(upstream, mid_ref[strip, :], wide_gain(gain_ref))
                grad = cot_ref[strip, :].astype(F32) + through
                grad_ref[strip, :] = grad
                own[strip, :] = grad.astype(BF16)
                feed_ref[...] += feed

            in_strips(ROWS, body)
            yield from gather_rows(spot, post, own, mid_rows_ref)

        def gradients():
            for copy in loads:
                copy.wait()
            groups = [(rows_ref, (gate_ref, up_ref)), (grads_ref, (hid_ref,))]
            yield from Gradients(spot, post, groups, *room, sum_a, sum_b).steps()

        def output():
            def step(i, carry):
                rows = pl.ds(pl.multiple_of(i * 256, 256), 256)
                out_ref[rows, :] = dot(hid_ref[rows, :], down_ref[...], 1, 1).astype(BF16)
                return carry

            lax.fori_loop(0, count // 256, step, 0)
            store = post.local(out_ref, out_hbm)
            store.start()
            yield
            store.wait()

        play("mgmgmgmggomgmmgggggo", m=main(), g=gradients(), o=output())

    half = shape((4, 64, n), BF16)
    wide = pltpu.VMEM((count, WIDE), BF16)
    narrow = pltpu.VMEM((count, PACK), BF16)
    return moving(
        kernel,
        "turn",
        (
            shape((ROWS, WIDE), F32),
            shape((8, ROWS, WIDE), BF16),
            shape((1, WIDE), F32),
            half,
            half,
            shape((count, WIDE), BF16),
        ),
        (part, mid, gain, cotangent, rows, grads, d_gate, d_up, hidden, weights),
        [ANY, INSIDE, INSIDE, INSIDE] + [ANY] * 6,
        (INSIDE, ANY, INSIDE, INSIDE, INSIDE, ANY),
        [pltpu.VMEM((ROWS, WIDE), BF16), wide, wide, narrow, narrow, narrow, pltpu.VMEM((WIDE, PACK), BF16), wide]
        + scatter_scratch()
        + gradient_scratch(n)
        + sems(100),
        3,
    )


def leave(part, tokens, gain, grad_mid, feed_part, rows, d_qkv, mid_rows, mixed, sum_two):
    n_qkv, n_out = d_qkv.shape[1], mixed.shape[1]
    n, n_two = n_qkv + n_out, sum_two.shape[-1]
    count = 8 * ROWS

    def kernel(
        part_ref, tokens_ref, gain_ref, grad_ref, feed_ref, rows_hbm, d_hbm, mid_hbm, mixed_hbm, sum_two_ref,
        token_ref, gains_ref, weight_ref, high_ref,
        norm_part, parts, from_y, over_y, from_chip, over_fsdp, from_tp, rows_ref, d_ref, mid_ref, mixed_ref, *rest,
    ):
        first, room, (sum_a, sum_b), last, (out_sems, in_sems) = rest[:4], rest[4:9], rest[9:11], rest[11:17], rest[17:]
        spot, post = Spot(), Post(out_sems, in_sems)
        loads = load(post, [(d_hbm, d_ref), (rows_hbm, rows_ref), (mixed_hbm, mixed_ref), (mid_hbm, mid_ref)])
        greet(spot, row_peers(spot) + y_peers(spot) + gain_sources(spot), 5 + 13, **collect_peers(spot))

        def main():
            yield from scatter_rows(spot, post, part_ref, *first)
            norm_part[...] = jnp.zeros_like(norm_part)

            def body(strip):
                upstream = row_sum(spot, first[0], first[1], first[3], strip)
                through, norm = norm_back(upstream, tokens_ref[strip, :].astype(F32), wide_gain(gain_ref))
                token_ref[strip, :] = grad_ref[strip, :] + through
                norm_part[...] += norm

            in_strips(ROWS, body)
            parts[...] = jnp.zeros_like(parts)
            for f in range(16):
                parts[f, 0:1, :] = norm_part[:, f * 128 : (f + 1) * 128]
                parts[f, 1:2, :] = feed_ref[:, f * 128 : (f + 1) * 128]
            yield from sum_gains(spot, post, parts, gains_ref, from_y, over_y, from_chip, over_fsdp, from_tp)

        def gradients():
            for copy in loads:
                copy.wait()
            groups = [(rows_ref, (d_ref,)), (mid_ref, (mixed_ref,))]
            yield from Gradients(spot, post, groups, *room, sum_a, sum_b).steps()
            yield from together(
                scatter_low(spot, post, sum_a, strip_writer(weight_ref), *last[:2]),
                scatter_high(spot, post, sum_b, strip_writer(weight_ref, 64), *last[2:4]),
            )

        play(
            "mbgmgbmggggmgmgmggmgbgg",
            m=main(),
            g=gradients(),
            b=scatter_high(spot, post, sum_two_ref, strip_writer(high_ref), *last[4:]),
        )

    small = (8, 128)
    full_rows = pltpu.VMEM((count, WIDE), BF16)
    return moving(
        kernel,
        "leave",
        (shape((ROWS, WIDE), F32), shape(small, F32), shape((ROWS, n), F32), shape((64, n_two), F32)),
        (part, tokens, gain, grad_mid, feed_part, rows, d_qkv, mid_rows, mixed, sum_two),
        [ANY, INSIDE, INSIDE, INSIDE, INSIDE] + [ANY] * 4 + [INSIDE],
        (INSIDE,) * 4,
        [pltpu.VMEM((1, WIDE), F32), pltpu.VMEM((16,) + small, F32)]
        + [pltpu.VMEM(dims + small, F32) for dims in ((3, 4), (4,), (3,), (), (7,))]
        + [full_rows, pltpu.VMEM((count, n_qkv), BF16), full_rows, pltpu.VMEM((count, n_out), BF16)]
        + scatter_scratch()
        + gradient_scratch(n)
        + [pltpu.VMEM((4, 64, n), BF16)] * 2
        + low_scratch(n)
        + high_scratch(n)
        + high_scratch(n_two)
        + sems(120),
        4,
    )


def dot(a, b, da=1, db=0):
    return lax.dot_general(a, b, (((da,), (db,)), ((), ())), preferred_element_type=F32)


def plain(kernel, name, grid, inputs, in_specs, outs, out_specs, scratch=()):
    return pl.pallas_call(
        kernel,
        name=name,
        out_shape=outs,
        grid=grid,
        in_specs=in_specs,
        out_specs=out_specs,
        scratch_shapes=list(scratch),
        compiler_params=pltpu.CompilerParams(vmem_limit_bytes=VMEM),
    )(*inputs)


def by_rows(n, width, column=0):
    return pl.BlockSpec((n, width), lambda i: (i, column))


def whole(dims, *index):
    at = index or (0,) * len(dims)
    return pl.BlockSpec(dims, lambda i: at)


def project(rows, weights, cosine, sine):
    step = 256

    def kernel(rows_ref, w_ref, cos_ref, sin_ref, q_ref, kv_ref):
        out = dot(rows_ref[...], w_ref[...])
        cos, sin = cos_ref[...], sin_ref[...]
        for head in range(4):
            u = out[:, head * HD : (head + 1) * HD]
            turned = (u * cos + pltpu.roll(u, HD // 2, 1) * sin).astype(BF16)
            if head < 2:
                q_ref[:, head * HD : (head + 1) * HD] = turned
            else:
                kv_ref[head - 2, 0] = turned
                kv_ref[head - 2, 1] = out[:, (head + 2) * HD : (head + 3) * HD].astype(BF16)

    out = shape((8 * ROWS, 2 * HD), BF16)
    return plain(
        kernel,
        "project",
        (8 * ROWS // step,),
        (rows, weights, cosine, sine),
        [by_rows(step, WIDE), whole((WIDE, PACK)), by_rows(step, HD), by_rows(step, HD)],
        (out, shape((2, 2, 8 * ROWS, HD), BF16)),
        (by_rows(step, 2 * HD), pl.BlockSpec((2, 2, step, HD), lambda i: (0, 0, i, 0))),
    )


def partial_rows(pairs, name, extra=None):
    step = 256
    sets = [pairs] + ([extra] if extra else [])
    flat = [pair for group in sets for pair in group]

    def kernel(*refs):
        values, outs = refs[: 2 * len(flat)], refs[2 * len(flat) :]
        at = 0
        for group, out in zip(sets, outs):
            total = None
            for _ in group:
                term = dot(values[at][...], values[at + 1][...], 1, 1)
                total = term if total is None else total + term
                at += 2
            out[...] = total.astype(BF16)

    inputs, specs = [], []
    for a, b, width, column in flat:
        inputs += [a, b]
        specs += [by_rows(step, width), whole((WIDE, width), 0, column)]
    out = tuple(shape((8 * ROWS, WIDE), BF16) for _ in sets)
    return plain(kernel, name, (8 * ROWS // step,), inputs, specs, out, tuple(by_rows(step, WIDE) for _ in sets))


def feed_forward(rows, grads, weights):
    step = 256

    def kernel(rows_ref, grads_ref, g_ref, u_ref, d_ref, hid_ref, dgate_ref, dup_ref):
        gate = dot(rows_ref[...], g_ref[...])
        up = dot(rows_ref[...], u_ref[...])
        d_hid = dot(grads_ref[...], d_ref[...])
        sigma = 1.0 / (1.0 + jnp.exp(-gate))
        silu = gate * sigma
        hid_ref[...] = (silu * up).astype(BF16)
        dup_ref[...] = (d_hid * silu).astype(BF16)
        dgate_ref[...] = (d_hid * up * sigma * (1.0 + gate * (1.0 - sigma))).astype(BF16)

    out = shape((8 * ROWS, PACK), BF16)
    return plain(
        kernel,
        "feed_forward",
        (8 * ROWS // step,),
        (rows, grads, weights, weights, weights),
        [by_rows(step, WIDE)] * 2 + [whole((WIDE, PACK), 0, i) for i in range(3)],
        (out,) * 3,
        (by_rows(step, PACK),) * 3,
    )


def settle(layer, token_grad, gains, attention, low, high, wide):
    def kernel(
        layer_ref, token_ref, gains_ref, attention_ref, low_ref, high_ref,
        layer_out, token_out, norm_out, feed_out, query_out, key_out, value_out, out_out, gate_out, up_out, down_out,
    ):
        layer_out[...] = layer_ref[...]
        token_out[...] = token_ref[...]
        norm_out[...] = gains_ref[0:1, :]
        feed_out[...] = gains_ref[1:2, :]
        for i, out in enumerate((query_out, key_out, value_out)):
            out[...] = attention_ref[:, i * 2 * HD : (i + 1) * 2 * HD]
        out_out[...] = attention_ref[:, PACK:].T
        for i, out in enumerate((gate_out, up_out, down_out)):
            columns = slice(i * PACK, (i + 1) * PACK)
            out[...] = jnp.concatenate([low_ref[:, columns], high_ref[:, columns]], 0).T[:wide]

    vector = shape((1, 128), F32)
    square = shape((ROWS, 2 * HD), F32)
    tall = shape((wide, ROWS), F32)
    return pl.pallas_call(
        kernel,
        name="settle",
        out_shape=(shape(layer.shape, layer.dtype), shape(token_grad.shape, F32), vector, vector, square, square, square)
        + (shape((2 * HD, ROWS), F32), tall, tall, tall),
        in_specs=[INSIDE] * 6,
        out_specs=(INSIDE,) * 11,
        compiler_params=pltpu.CompilerParams(vmem_limit_bytes=VMEM),
    )(layer, token_grad, gains, attention, low, high)


def back_to_heads(rows, weights):
    step = 256

    def kernel(rows_ref, w_ref, out_ref):
        out_ref[...] = dot(rows_ref[...], w_ref[...]).astype(BF16)

    return plain(
        kernel,
        "back_to_heads",
        (8 * ROWS // step,),
        (rows, weights),
        [by_rows(step, WIDE), whole((WIDE, 2 * HD))],
        shape((8 * ROWS, 2 * HD), BF16),
        by_rows(step, 2 * HD),
    )


TILE = 256
CHUNK = 512


def place_of(start, count, xh, axis):
    dims = (count, 1) if axis == 0 else (1, count)
    j = lax.broadcasted_iota(jnp.int32, dims, axis)
    return 2 * (j + start) - lax.rem(j + start, ROWS) + xh * ROWS


SPANS = ((0, 512, False), (512, 256, True))
LAST = (768, 256, True)


def scores_of(keys, q, span, q_pos, prefix, xh):
    start, count, masked = span
    scores = dot(keys, q, 1, 1) * (SCALE * LOG2E)
    if masked:
        k_pos = place_of(start, count, xh, 0)
        scores = jnp.where(jnp.logical_or(k_pos <= q_pos, k_pos < prefix), scores, -1e30)
    return scores


def tile_at(i):
    head, tile = lax.div(i, 4), lax.rem(i, 4)
    return head, tile, pl.ds(pl.multiple_of(head * HD, HD), HD), pl.ds(pl.multiple_of(tile * TILE, TILE), TILE)


def exchange(post, pairs, device):
    copies = [post.copy(src, dst, device) for src, dst in pairs]
    for copy in copies:
        copy.start()
    yield
    for copy in copies:
        copy.wait_recv()
        yield
    for copy in copies:
        copy.wait_send()


def prefix_of(prefixes_ref):
    return prefixes_ref[lax.div(lax.axis_index("fsdp"), 2)]


def attend(prefixes, queries, here, cotangent, row_out, second):
    n, n_two = row_out.shape[-1], second.shape[-1]

    def kernel(
        prefixes_ref, q_ref, here_ref, cot_ref, row_ref, second_ref, o_ref, lse_ref, there_ref, grads_ref, out_ref, stage_ref,
        top_ref, sum_ref, acc_ref, out_sems, in_sems,
    ):
        prefix = prefix_of(prefixes_ref)
        spot, post = Spot(), Post(out_sems, in_sems)
        partner = spot.at(dx=2)
        greet(spot, row_peers(spot) + y_peers(spot) + [partner], 6)

        def sweep(side, begin, end):
            keys_ref = there_ref if side else here_ref
            xh = 1 - spot.xh if side else spot.xh

            def step(i, carry):
                head, tile, cols, rows = tile_at(i)
                q = q_ref[rows, cols]
                q_pos = place_of(tile * TILE, TILE, spot.xh, 1)
                one = pl.ds(i, 1)

                def chunk(span, first):
                    keys = pl.ds(span[0], span[1])
                    scores = scores_of(keys_ref[head, 0, keys, :], q, span, q_pos, prefix, xh)
                    top = jnp.max(scores, 0, keepdims=True)
                    if not first:
                        before = top_ref[one, :]
                        top = jnp.maximum(top, before)
                    raised = jnp.exp2(scores - top)
                    total = jnp.sum(raised, 0, keepdims=True)
                    mixed = dot(keys_ref[head, 1, keys, :], raised.astype(BF16), 0, 0)
                    if not first:
                        fade = jnp.exp2(before - top)
                        total = total + sum_ref[one, :] * fade
                        mixed = mixed + acc_ref[i] * fade
                    top_ref[one, :] = top
                    sum_ref[one, :] = total
                    acc_ref[i] = mixed

                for number, span in enumerate(SPANS):
                    chunk(span, side == 0 and number == 0)

                @pl.when(tile == 3)
                def _():
                    chunk(LAST, False)

                if side == 1:
                    total = sum_ref[one, :]
                    o_ref[rows, cols] = (acc_ref[i] / total).T.astype(BF16)
                    lse_ref[one, :] = top_ref[one, :] + jnp.log2(total)
                return carry

            lax.fori_loop(begin, end, step, 0)

        def compute():
            sweep(0, 0, 8)
            yield
            sweep(1, 0, 4)
            yield
            sweep(1, 4, 8)

        play(
            "vesfcvsfecvsfecse",
            v=y_gather(spot, post, row_ref, lambda y: out_ref.at[y]),
            f=y_gather(spot, post, second_ref, lambda y: stage_ref.at[y]),
            e=exchange(post, [(here_ref.at[head], there_ref.at[head]) for head in range(2)], partner),
            s=gather_rows(spot, post, cot_ref, grads_ref),
            c=compute(),
        )

    return moving(
        kernel,
        "attend",
        (
            shape((8 * ROWS, 2 * HD), BF16),
            shape((8, TILE), F32),
            shape(here.shape, BF16),
            shape((8, ROWS, WIDE), BF16),
            shape((4, 4, ROWS, n), BF16),
            shape((4, 64, n_two), BF16),
        ),
        (prefixes, queries, here, cotangent, row_out, second),
        [pl.BlockSpec(memory_space=pltpu.SMEM)] + [INSIDE] * 5,
        (INSIDE, INSIDE, INSIDE, ANY, ANY, INSIDE),
        [pltpu.VMEM((8, TILE), F32), pltpu.VMEM((8, TILE), F32), pltpu.VMEM((8, HD, TILE), F32)] + sems(60),
        5,
    )


def attend_back(prefixes, queries, here, there, grads, mixed, lse, cosine, sine, out_part, mid, sum_a):
    n = sum_a.shape[-1]

    def kernel(
        prefixes_ref, q_ref, here_ref, there_ref, g_ref, o_ref, lse_ref, cos_ref, sin_ref, part_ref, mid_ref, sum_a_ref,
        d_ref, layer_ref, weight_ref, delta_ref, dq_ref, acc_ref, near_ref, away_ref, land_ref, *rest,
    ):
        second, last, (out_sems, in_sems) = rest[:4], rest[4:6], rest[6:]
        prefix = prefix_of(prefixes_ref)
        spot, post = Spot(), Post(out_sems, in_sems)
        partner = spot.at(dx=2)
        greet(spot, row_peers(spot) + y_peers(spot) + [partner], 6)

        def sweep(head, side, keys_ref, into):
            xh = spot.xh if side == 0 else 1 - spot.xh
            cols = pl.ds(head * HD, HD)
            into[...] = jnp.zeros_like(into)

            def step(tile, carry):
                i = head * 4 + tile
                rows = pl.ds(pl.multiple_of(tile * TILE, TILE), TILE)
                q, g = q_ref[rows, cols], g_ref[rows, cols]
                q_pos = place_of(tile * TILE, TILE, spot.xh, 1)
                if side == 1:
                    product = g.astype(F32) * o_ref[rows, cols].astype(F32)
                    delta_ref[pl.ds(i, 1), :] = jnp.sum(product.T, 0, keepdims=True)
                level, offset = lse_ref[pl.ds(i, 1), :], delta_ref[pl.ds(i, 1), :]

                def chunk(span, first):
                    span_rows = pl.ds(span[0], span[1])
                    keys = keys_ref[head, 0, span_rows, :]
                    probs = jnp.exp2(scores_of(keys, q, span, q_pos, prefix, xh) - level)
                    d_probs = dot(keys_ref[head, 1, span_rows, :], g, 1, 1)
                    d_scores = (probs * (d_probs - offset)).astype(BF16)
                    into[0, span_rows, :] += dot(d_scores, q)
                    into[1, span_rows, :] += dot(probs.astype(BF16), g)
                    d_query = dot(d_scores, keys, 0, 0)
                    dq_ref[i] = d_query if first else dq_ref[i] + d_query

                for number, span in enumerate(SPANS):
                    chunk(span, side == 1 and number == 0)

                @pl.when(tile == 3)
                def _():
                    chunk(LAST, False)

                if side == 0:
                    u = dq_ref[i] * SCALE
                    d_ref[rows, cols] = (u * cos_ref[rows, :] - pltpu.roll(u, HD // 2, 1) * sin_ref[rows, :]).astype(BF16)
                return carry

            lax.fori_loop(0, 4, step, 0)

        def compute():
            copies = []
            for head in range(2):
                sweep(head, 1, there_ref, acc_ref)
                away_ref[head] = acc_ref[...].astype(BF16)
                copies.append(post.copy(away_ref.at[head], land_ref.at[head], partner))
                copies[-1].start()
                yield
            for head in range(2):
                sweep(head, 0, here_ref, near_ref.at[head])
                yield
            for head in range(2):
                copies[head].wait_recv()
                cols = pl.ds(2 * HD + head * HD, HD)

                def finish(i, carry, head=head):
                    rows = pl.ds(pl.multiple_of(i * 128, 128), 128)
                    u = (near_ref[head, 0, rows, :] + land_ref[head, 0, rows, :].astype(F32)) * SCALE
                    back = u * cos_ref[rows, :] - pltpu.roll(u, HD // 2, 1) * sin_ref[rows, :]
                    d_ref[rows, pl.ds(2 * HD + head * HD, HD)] = back.astype(BF16)
                    v = near_ref[head, 1, rows, :] + land_ref[head, 1, rows, :].astype(F32)
                    d_ref[rows, pl.ds(4 * HD + head * HD, HD)] = v.astype(BF16)
                    return carry

                lax.fori_loop(0, 8, finish, 0)
            for copy in copies:
                copy.wait_send()

        def output():
            yield from scatter_rows(spot, post, part_ref, *second)

            def body(strip):
                layer_ref[strip, :] = (mid_ref[strip, :] + row_sum(spot, second[0], second[1], second[3], strip)).astype(BF16)

            in_strips(ROWS, body)

        play(
            "owcocwocowc",
            c=compute(),
            o=output(),
            w=scatter_low(spot, post, sum_a_ref, strip_writer(weight_ref), *last),
        )

    pair = (2, 8 * ROWS, HD)
    return moving(
        kernel,
        "attend_back",
        (shape((8 * ROWS, PACK), BF16), shape((ROWS, WIDE), BF16), shape((64, n), F32)),
        (prefixes, queries, here, there, grads, mixed, lse, cosine, sine, out_part, mid, sum_a),
        [pl.BlockSpec(memory_space=pltpu.SMEM)] + [INSIDE] * 8 + [ANY, INSIDE, INSIDE],
        (INSIDE,) * 3,
        [
            pltpu.VMEM((8, TILE), F32),
            pltpu.VMEM((8, TILE, HD), F32),
            pltpu.VMEM(pair, F32),
            pltpu.VMEM((2,) + pair, F32),
            pltpu.VMEM((2,) + pair, BF16),
            pltpu.VMEM((2,) + pair, BF16),
        ]
        + scatter_scratch()
        + low_scratch(n)
        + sems(64),
        6,
    )


def on_device(
    tokens,
    prefixes,
    norm_gain,
    query_weight,
    key_weight,
    value_weight,
    output_weight,
    feed_gain,
    gate_weight,
    up_weight,
    down_weight,
    cotangent,
):
    rows_one, full_one, row_out, row_two, second, cosine, sine = enter(
        tokens, norm_gain, query_weight, key_weight, value_weight, output_weight, gate_weight.T, up_weight.T, down_weight
    )
    rows_one = rows_one.reshape(-1, WIDE)
    full_one = full_one.reshape(WIDE, -1)
    queries, here = project(rows_one, full_one, cosine, sine)
    attended, lse, there, grad_rows, full_out, stage_two = attend(prefixes, queries, here, cotangent, row_out, second)
    full_out = full_out.reshape(WIDE, -1)
    (part,) = partial_rows([(attended, full_out, 2 * HD, 0)], "attention_out")
    mid, rows_two, full_two = middle(part.reshape(8, ROWS, WIDE), tokens, feed_gain, row_two, stage_two)
    rows_two, grad_rows, full_two = (a.reshape(-1, a.shape[-1]) for a in (rows_two, grad_rows, full_two.reshape(WIDE, -1)))
    hidden, d_gate, d_up = feed_forward(rows_two, grad_rows, full_two)
    (part,) = partial_rows([(d_gate, full_two, PACK, 0), (d_up, full_two, PACK, 1)], "feed_back")
    grad_mid, mid_rows, feed_part, sum_a, sum_b, part_out = turn(
        part.reshape(8, ROWS, WIDE), mid, feed_gain, cotangent, rows_two, grad_rows, d_gate, d_up, hidden, full_two
    )
    mid_rows = mid_rows.reshape(-1, WIDE)
    grad_mixed = back_to_heads(mid_rows, full_out)
    d_qkv, layer_output, low = attend_back(
        prefixes, queries, here, there, grad_mixed, attended, lse, cosine, sine, part_out.reshape(8, ROWS, WIDE), mid, sum_a
    )
    (part,) = partial_rows([(d_qkv, full_one, PACK, 0)], "attention_back")
    token_grad, gains, attention, high = leave(
        part.reshape(8, ROWS, WIDE), tokens, norm_gain, grad_mid, feed_part, rows_one, d_qkv, mid_rows, attended, sum_b
    )
    layer_output, token_grad, norm_grad, feed_grad, *grads = settle(
        layer_output, token_grad, gains, attention, low, high, gate_weight.shape[1]
    )
    query_grad, key_grad, value_grad, output_grad, gate_grad, up_grad, down_grad = grads
    return (
        layer_output,
        token_grad,
        norm_grad[0],
        query_grad,
        key_grad,
        value_grad,
        output_grad,
        feed_grad[0],
        gate_grad.T,
        up_grad.T,
        down_grad,
    )


def solution(mesh):
    rows = P(("fsdp", "tp"), None)
    wide = P("fsdp", "tp")
    tall = P("tp", "fsdp")
    return jax.shard_map(
        on_device,
        mesh=mesh,
        in_specs=(rows, P(), P(), wide, wide, wide, tall, P(), wide, wide, tall, rows),
        out_specs=(rows, rows, P("fsdp"), wide, wide, wide, tall, P("fsdp"), wide, wide, tall),
        check_vma=False,
    )
```

```python
import functools
import math

import jax
import jax.numpy as jnp
from jax import lax
from jax.experimental import pallas as pl
from jax.experimental.pallas import tpu as pltpu
from jax.sharding import PartitionSpec as P

HD = 128
EPS = 1e-05
ROPE_BASE = 10000.0
F32 = jnp.float32
BF16 = jnp.bfloat16
MESH = pl.DeviceIdType.MESH
AXES = ("fsdp", "tp")
ROWS = 128
WIDE = 2048
PACK = 768
SCALE = 1.0 / math.sqrt(HD)
LOG2E = 1.4426950408889634
VMEM = 60 << 20


class Spot:
    def __init__(self):
        f, t = lax.axis_index("fsdp"), lax.axis_index("tp")
        self.y, self.xl, self.c = lax.div(f, 4), lax.rem(lax.div(f, 2), 2), lax.rem(f, 2)
        self.z, self.xh = lax.div(t, 2), lax.rem(t, 2)
        self.x = self.xh * 2 + self.xl
        self.own = self.xl * 2 + self.c
        self.away = lax.rem(self.xh + self.c, 2)
        self.home = self.away == 0
        self.turn = 1 - lax.rem(self.away + self.xl, 2)
        self.ahead = 1 + 2 * self.turn
        self.back = 3 - 2 * self.turn
        self.near = (1 - self.xl) * 2
        self.same = self.xl * 2

    def at(self, dy=0, dx=0, dz=0, core=None):
        y, z, x = lax.rem(self.y + dy, 4), lax.rem(self.z + dz, 4), lax.rem(self.x + dx, 4)
        return (y * 4 + lax.rem(x, 2) * 2 + (self.c if core is None else core), z * 2 + lax.div(x, 2))

    def other(self):
        return self.at(core=1 - self.c)

    def seat(self, slot):
        return (self.y * 4 + slot, self.z * 2 + self.c)

    def bench(self, slot):
        return (self.y * 4 + slot, self.z * 2 + self.xh)

    def block(self, dz=0, flip=False):
        return (1 - self.c if flip else self.c) * 4 + lax.rem(self.z + dz, 4)


class Post:
    def __init__(self, out_sems, in_sems):
        self.out_sems, self.in_sems, self.n_out, self.n_in = out_sems, in_sems, 0, 0

    def slots(self, n):
        base = self.n_in
        self.n_in += n
        return base

    def copy(self, src, dst, device, slot=None):
        slot = self.slots(1) if slot is None else slot
        self.n_out += 1
        return pltpu.make_async_remote_copy(
            src_ref=src,
            dst_ref=dst,
            send_sem=self.out_sems.at[self.n_out - 1],
            recv_sem=self.in_sems.at[slot],
            device_id=device,
            device_id_type=MESH,
        )

    def arrival(self, dst, device, slot):
        return pltpu.make_async_remote_copy(
            src_ref=dst,
            dst_ref=dst,
            send_sem=self.out_sems.at[0],
            recv_sem=self.in_sems.at[slot],
            device_id=device,
            device_id_type=MESH,
        )

    def local(self, src, dst):
        self.n_out += 1
        return pltpu.make_async_copy(src, dst, self.out_sems.at[self.n_out - 1])


def greet(spot, sources, count, home=(), away=()):
    barrier = pltpu.get_barrier_semaphore()

    def signal(devices):
        for device in devices:
            pl.semaphore_signal(barrier, inc=1, device_id=device, device_id_type=MESH)

    signal(sources)
    if home:
        count = count + 3 + spot.away

        @pl.when(spot.home)
        def _():
            signal(home)

        @pl.when(jnp.logical_not(spot.home))
        def _():
            signal(away)

    pl.semaphore_wait(barrier, count)


def row_peers(spot):
    return [spot.at(dz=1), spot.at(dz=3), spot.other()]


def y_peers(spot):
    return [spot.at(dy=1), spot.at(dy=3)]


def gather_peers(spot):
    near = [spot.at(dx=spot.back, core=0), spot.at(dx=spot.back, core=1)]
    return {"home": near + [spot.other()], "away": near + [spot.at(dx=1), spot.at(dx=3)]}


def collect_peers(spot):
    usual = [spot.at(dx=1, core=spot.xh), spot.at(dx=3, core=spot.xh), spot.at(dx=spot.ahead)]
    return {"home": usual, "away": usual + [spot.other()]}


def half_of(ref, number):
    rows = ref.shape[0] // 2
    return ref.at[pl.ds(number * rows, rows)]


def after(spot, k):
    return lax.rem(spot.own + k, 4)


def play(order, **jobs):
    for letter in order:
        next(jobs[letter], None)
    for job in jobs.values():
        for _ in job:
            pass


def gather_rows(spot, post, own, rows):
    up, down, core = spot.at(dz=1), spot.at(dz=3), spot.other()
    half = ROWS // 2
    low, high = pl.ds(0, half), pl.ds(half, half)
    here, below, above, far = (spot.block(dz) for dz in (0, 3, 1, 2))
    a = post.copy(own, rows.at[here], up)
    b = post.copy(own, rows.at[here], down)
    k0 = post.copy(own, rows.at[here], core)
    keep = post.local(own, rows.at[here])
    for copy in (a, b, k0, keep):
        copy.start()
    yield
    a.wait_recv()
    fa = post.copy(rows.at[below, low], rows.at[below, low], up)
    k1 = post.copy(rows.at[below], rows.at[below], core)
    fa.start()
    k1.start()
    b.wait_recv()
    fb = post.copy(rows.at[above, high], rows.at[above, high], down)
    k2 = post.copy(rows.at[above], rows.at[above], core)
    fb.start()
    k2.start()
    yield
    fa.wait_recv()
    fb.wait_recv()
    k3 = post.copy(rows.at[far], rows.at[far], core)
    k3.start()
    yield
    keep.wait()
    for copy in (k0, k1, k2, k3):
        copy.wait_recv()
    for copy in (a, b, fa, fb, k0, k1, k2, k3):
        copy.wait_send()


def in_strips(count, body):
    def step(i, carry):
        body(pl.ds(pl.multiple_of(i * 16, 16), 16))
        return carry

    lax.fori_loop(0, count // 16, step, 0)


def add_into(target, other, rows=ROWS, start=0):
    def body(strip):
        strip = pl.ds(pl.multiple_of(strip.start + start, 16), 16)
        target[strip, :] = (target[strip, :].astype(F32) + other[strip, :].astype(F32)).astype(BF16)

    in_strips(rows, body)


def row_products(spot, terms, outgoing, mine):
    def make(z):
        other, own = pl.ds(((1 - spot.c) * 4 + z) * ROWS, ROWS), pl.ds((spot.c * 4 + z) * ROWS, ROWS)

        def step(i, carry):
            columns = pl.ds(pl.multiple_of(i * 512, 512), 512)
            total = None
            for a, w, part in terms:
                term = dot(jnp.concatenate([a[other, :], a[own, :]], 0), w[columns, part], 1, 1)
                total = term if total is None else total + term
            outgoing[z, :, columns] = total[:ROWS].astype(BF16)
            mine[z, :, columns] = total[ROWS:].astype(BF16)
            return carry

        lax.fori_loop(0, WIDE // 512, step, 0)

    return make


def row_loads(spot, post, part, outgoing, mine):
    def make(z):
        copies = load(post, [(part.at[(1 - spot.c) * 4 + z], outgoing.at[z]), (part.at[spot.c * 4 + z], mine.at[z])])
        for copy in copies:
            copy.wait()

    return make


def scatter_rows(spot, post, make, outgoing, mine, land, far, gone):
    up, down, core = spot.at(dz=1), spot.at(dz=3), spot.other()
    half = ROWS // 2
    low, high = pl.ds(0, half), pl.ds(half, half)
    steps = [lax.rem(spot.z + dz, 4) for dz in (2, 3, 1, 0)]
    distant, lower, upper, here = steps
    to_core, others = [], []

    def begin(k):
        make(steps[k])
        to_core.append(post.copy(outgoing.at[steps[k]], land.at[steps[k]], core))
        to_core[k].start()

    def pass_on(src, dst, device):
        others.append(post.copy(src, dst, device))
        others[-1].start()
        return others[-1]

    def ready(k):
        to_core[k].wait_recv()
        if k < 3:
            add_into(mine.at[steps[k]], land.at[steps[k]])

    begin(0)
    begin(1)
    ready(0)
    f_low = pass_on(mine.at[distant, low], far.at[low], down)
    f_high = pass_on(mine.at[distant, high], far.at[high], up)
    begin(2)
    ready(1)
    gone_copies = [pass_on(mine.at[lower, high], gone.at[0, high], down)]
    begin(3)
    ready(2)
    gone_copies.append(pass_on(mine.at[upper, low], gone.at[1, low], up))
    yield
    ready(3)
    f_low.wait_recv()
    add_into(mine.at[lower], far, half)
    gone_copies.append(pass_on(mine.at[lower, low], gone.at[0, low], down))
    f_high.wait_recv()
    add_into(mine.at[upper], far, half, half)
    gone_copies.append(pass_on(mine.at[upper, high], gone.at[1, high], up))
    yield
    for copy in gone_copies:
        copy.wait_recv()
    for copy in to_core + others:
        copy.wait_send()


def row_sum(spot, mine, land, gone, strip):
    parts = [mine[spot.z, strip, :], land[spot.z, strip, :], gone[0, strip, :], gone[1, strip, :]]
    return sum(part.astype(F32) for part in parts)


def scatter_scratch():
    block = (ROWS, WIDE)
    return [
        pltpu.VMEM((4,) + block, BF16),
        pltpu.VMEM((4,) + block, BF16),
        pltpu.VMEM((4,) + block, BF16),
        pltpu.VMEM(block, BF16),
        pltpu.VMEM((2,) + block, BF16),
    ]


def x_gather(spot, post, src, dst_at):
    base, far = post.slots(4), post.slots(4)
    sends = [post.copy(src, dst_at(spot.own), spot.at(dx=dx, core=spot.xh), base + spot.own) for dx in (1, 3)]
    cross = post.copy(src, dst_at(spot.own), spot.other(), base + spot.own)
    keep = post.local(src, dst_at(spot.own))
    for copy in sends:
        copy.start()

    @pl.when(spot.home)
    def _():
        keep.start()

    @pl.when(jnp.logical_not(spot.home))
    def _():
        cross.start()

    def landed(dst, slot):
        post.arrival(dst, spot.at(dx=1), slot).wait_recv()

    yield
    for core in range(2):
        block = dst_at(spot.near + core)
        landed(block, base + spot.near + core)
        part = half_of(block, spot.turn)
        sends.append(post.copy(part, part, spot.at(dx=spot.ahead), far + 2 * core + spot.turn))
        sends[-1].start()
    yield

    @pl.when(spot.home)
    def _():
        slot = spot.same + 1 - spot.c
        landed(dst_at(slot), base + slot)
        keep.wait()

    @pl.when(jnp.logical_not(spot.home))
    def _():
        for core in range(2):
            for number in range(2):
                landed(half_of(dst_at(spot.same + core), number), far + 2 * core + number)
        cross.wait_send()

    for copy in sends:
        copy.wait_send()


def y_gather(spot, post, src, dst_at):
    up, down = spot.at(dy=1), spot.at(dy=3)
    here, below, above = dst_at(spot.y), dst_at(lax.rem(spot.y + 3, 4)), dst_at(lax.rem(spot.y + 1, 4))
    a, b, keep = post.copy(src, here, up), post.copy(src, here, down), post.local(src, here)
    for copy in (a, b, keep):
        copy.start()
    yield
    a.wait_recv()
    fa = post.copy(half_of(below, 0), half_of(below, 0), up)
    fa.start()
    b.wait_recv()
    fb = post.copy(half_of(above, 1), half_of(above, 1), down)
    fb.start()
    yield
    keep.wait()
    for copy in (fa, fb):
        copy.wait_recv()
    for copy in (a, b, fa, fb):
        copy.wait_send()


def together(*jobs):
    live = list(jobs)
    while live:
        live = [job for job in live if next(job, job) is not job]
        if live:
            yield


def gather_first(spot, post, shard, row, stage):
    return together(
        x_gather(spot, post, shard.at[0], lambda slot: row.at[slot]),
        y_gather(spot, post, shard.at[1], lambda y: stage.at[y]),
    )


def gather_second(spot, post, row, stage, full):
    return together(
        x_gather(spot, post, stage, lambda slot: full.at[:, slot, 1]),
        y_gather(spot, post, row, lambda y: full.at[y, :, 0]),
    )


def sum_parts(parts, write):
    def body(strip):
        write(strip, sum(part[strip, :].astype(F32) for part in parts))

    in_strips(parts[0].shape[0], body)


def add_block(target, other):
    if len(target.shape) == 2:
        add_into(target, other, target.shape[0])
    else:

        def step(i, carry):
            add_into(target.at[i], other.at[i], target.shape[1])
            return carry

        lax.fori_loop(0, target.shape[0], step, 0)


class XCollect:
    def __init__(self, spot, post, src_at, land, hop):
        self.spot, self.post, self.src_at, self.land, self.hop = spot, post, src_at, land, hop
        self.in_land, self.in_hop = post.slots(5), post.slots(2)
        self.sends = []

    def to_near(self, core, src, number):
        spot = self.spot
        copy = self.post.copy(
            src,
            half_of(self.land.at[spot.turn], number),
            spot.seat(spot.near + core),
            self.in_land + 2 * spot.turn + number,
        )
        copy.start()
        self.sends.append(copy)

    def start(self):
        spot, post = self.spot, self.post
        cross_slot = spot.same + 1 - spot.c
        self.cross = post.copy(self.src_at(cross_slot), self.land.at[2], spot.other(), self.in_land + 4)
        self.keep = post.local(self.src_at(spot.own), self.land.at[2])
        self.far = []
        for core in range(2):
            for number, dx in ((0, 3), (1, 1)):
                src = half_of(self.src_at(spot.same + core), number)
                self.far.append(post.copy(src, self.hop.at[core], spot.at(dx=dx), self.in_hop + core))

        @pl.when(spot.home)
        def _():
            self.cross.start()
            self.keep.start()

        @pl.when(jnp.logical_not(spot.home))
        def _():
            for copy in self.far:
                copy.start()

        for core in range(2):
            self.to_near(core, half_of(self.src_at(spot.near + core), 1 - spot.turn), 1 - spot.turn)

    def relay(self):
        spot, post = self.spot, self.post
        for core in range(2):
            post.arrival(self.hop.at[core], spot.at(dx=1), self.in_hop + core).wait_recv()
            add_block(self.hop.at[core], half_of(self.src_at(spot.near + core), spot.turn))
            self.to_near(core, self.hop.at[core], spot.turn)

    def finish(self):
        spot, post = self.spot, self.post
        for side in range(2):
            for number in range(2):
                dst = half_of(self.land.at[side], number)
                post.arrival(dst, spot.at(dx=1), self.in_land + 2 * side + number).wait_recv()

        @pl.when(spot.home)
        def _():
            self.keep.wait()
            self.cross.wait_send()

        @pl.when(jnp.logical_not(spot.home))
        def _():
            post.arrival(self.land.at[2], spot.at(dx=1), self.in_land + 4).wait_recv()
            for copy in self.far:
                copy.wait_send()

        for copy in self.sends:
            copy.wait_send()

    def parts(self):
        return [self.land.at[side] for side in range(3)]


class YCollect:
    def __init__(self, spot, post, src_at, land, hop):
        self.spot, self.post, self.src_at, self.land, self.hop = spot, post, src_at, land, hop
        self.up, self.down = spot.at(dy=1), spot.at(dy=3)
        self.y = [lax.rem(spot.y + k, 4) for k in range(4)]

    def start_far(self):
        block = self.src_at(self.y[2])
        self.far = [
            self.post.copy(half_of(block, 0), self.hop.at[0], self.down),
            self.post.copy(half_of(block, 1), self.hop.at[1], self.up),
        ]
        for copy in self.far:
            copy.start()

    def start_lower(self):
        self.low = [self.post.copy(half_of(self.src_at(self.y[3]), 1), half_of(self.land.at[0], 1), self.down)]
        self.low[0].start()

    def start_upper(self):
        self.high = [self.post.copy(half_of(self.src_at(self.y[1]), 0), half_of(self.land.at[1], 0), self.up)]
        self.high[0].start()

    def relay(self):
        for number, k, target in ((0, 3, self.down), (1, 1, self.up)):
            self.far[number].wait_recv()
            hop = self.hop.at[number]
            add_block(hop, half_of(self.src_at(self.y[k]), number))
            copy = self.post.copy(hop, half_of(self.land.at[number], number), target)
            copy.start()
            (self.low if number == 0 else self.high).append(copy)

    def finish(self):
        for copy in self.low + self.high:
            copy.wait_recv()
        for copy in self.far + self.low + self.high:
            copy.wait_send()

    def parts(self):
        return [self.src_at(self.spot.y), self.land.at[0], self.land.at[1]]


class Gradients:
    def __init__(self, spot, post, groups, full, land_x, hop_x, land_y, hop_y, sum_a, sum_b):
        self.spot, self.groups, self.full, self.sum_a, self.sum_b = spot, groups, full, sum_a, sum_b
        self.y = [lax.rem(spot.y + k, 4) for k in (2, 3, 1, 0)]
        self.x = [
            XCollect(spot, post, lambda slot, y=y: full.at[y, slot, 0], land_x.at[j], hop_x.at[j])
            for j, y in enumerate(self.y)
        ]
        self.over_y = YCollect(spot, post, lambda y: full.at[y, :, 1], land_y, hop_y)

    def make(self, j):
        y = self.y[j]

        def part(s, carry):
            columns = pl.ds(pl.multiple_of(y * 512 + s * 256, 256), 256)
            at = 0
            for rows, values in self.groups:
                left = rows[:, columns]
                for value in values:
                    width = value.shape[1]
                    block = dot(left, value[...], 0, 0).astype(BF16)
                    for i in range(4):
                        self.full[y, 2 * s + i // 2, i % 2, :, at : at + width] = block[i * 64 : (i + 1) * 64]
                    at += width
            return carry

        lax.fori_loop(0, 2, part, 0)
        (self.over_y.start_far, self.over_y.start_lower, self.over_y.start_upper, lambda: None)[j]()
        self.x[j].start()

    def sum_x(self, j):
        def write(strip, total):
            self.sum_a[self.y[j], strip, :] = total.astype(BF16)

        self.x[j].finish()
        sum_parts(self.x[j].parts(), write)

    def sum_y(self):
        self.over_y.finish()

        def slot_sum(slot, carry):
            def write(strip, total):
                self.sum_b[slot, strip, :] = total.astype(BF16)

            sum_parts([part.at[slot] for part in self.over_y.parts()], write)
            return carry

        lax.fori_loop(0, 4, slot_sum, 0)

    def steps(self):
        self.make(0)
        yield
        self.make(1)
        yield
        self.make(2)
        self.x[0].relay()
        yield
        self.make(3)
        self.x[1].relay()
        yield
        self.over_y.relay()
        self.x[2].relay()
        yield
        self.x[3].relay()
        yield
        for j in range(4):
            self.sum_x(j)
            yield
        self.sum_y()


def load(post, pairs):
    copies = [post.local(src, dst) for src, dst in pairs]
    for copy in copies:
        copy.start()
    return copies


def gradient_scratch(n):
    return [
        pltpu.VMEM((4, 4, 2, 64, n), BF16),
        pltpu.VMEM((4, 3, 64, n), BF16),
        pltpu.VMEM((4, 2, 32, n), BF16),
        pltpu.VMEM((2, 4, 64, n), BF16),
        pltpu.VMEM((2, 2, 64, n), BF16),
    ]


def scatter_low(spot, post, sum_a, write, land, hop):
    over_y = YCollect(spot, post, lambda y: sum_a.at[y], land, hop)
    over_y.start_far()
    over_y.start_lower()
    over_y.start_upper()
    yield
    over_y.relay()
    yield
    over_y.finish()
    sum_parts(over_y.parts(), write)


def scatter_high(spot, post, sum_b, write, land, hop):
    over_x = XCollect(spot, post, lambda slot: sum_b.at[slot], land, hop)
    over_x.start()
    yield
    over_x.relay()
    yield
    over_x.finish()
    sum_parts(over_x.parts(), write)


def strip_writer(out, start=0):
    def write(strip, total):
        out[pl.ds(pl.multiple_of(strip.start + start, 16), 16), :] = total

    return write


def low_scratch(n):
    return [pltpu.VMEM((2, 64, n), BF16), pltpu.VMEM((2, 32, n), BF16)]


def high_scratch(n):
    return [pltpu.VMEM((3, 64, n), BF16), pltpu.VMEM((2, 32, n), BF16)]


def sum_gains(spot, post, parts, out, from_y, over_y, from_chip, over_fsdp, from_tp):
    y_copies = []
    for i, k in enumerate((2, 1, 3)):
        y = lax.rem(spot.y + k, 4)
        y_copies.append(post.copy(parts.at[pl.ds(y * 4, 4)], from_y.at[i], spot.at(dy=k)))
        y_copies[-1].start()
    yield
    for copy in y_copies:
        copy.wait_recv()
    over_y[...] = parts[pl.ds(spot.y * 4, 4)] + from_y[0] + from_y[1] + from_y[2]
    chip_copies = []
    for i, k in enumerate((1, 2, 3)):
        slot = after(spot, k)
        chip_copies.append(post.copy(over_y.at[slot], from_chip.at[i], spot.bench(slot)))
        chip_copies[-1].start()
    yield
    for copy in chip_copies:
        copy.wait_recv()
    over_fsdp[...] = over_y[spot.own] + from_chip[0] + from_chip[1] + from_chip[2]
    tp_copies = []
    for i, (dz, dx) in enumerate(TP_MOVES):
        tp_copies.append(post.copy(over_fsdp, from_tp.at[i], spot.at(dz=dz, dx=dx)))
        tp_copies[-1].start()
    yield
    for copy in tp_copies:
        copy.wait_recv()
    out[...] = over_fsdp[...] + sum(from_tp[i] for i in range(7))
    for copy in y_copies + chip_copies + tp_copies:
        copy.wait_send()


TP_MOVES = [(dz, dx) for dx in (0, 2) for dz in (0, 1, 2, 3) if (dz, dx) != (0, 0)]


def gain_sources(spot):
    return (
        [spot.at(dy=k) for k in (1, 2, 3)]
        + [spot.bench(after(spot, k)) for k in (1, 2, 3)]
        + [spot.at(dz=(4 - dz) % 4, dx=dx) for dz, dx in TP_MOVES]
    )


ANY = pl.BlockSpec(memory_space=pl.ANY)
INSIDE = pl.BlockSpec(memory_space=pltpu.VMEM)


def sems(n):
    return [pltpu.SemaphoreType.DMA((n,)), pltpu.SemaphoreType.DMA((n,))]


def moving(kernel, name, outs, inputs, in_specs, out_specs, scratch, cid):
    return pl.pallas_call(
        kernel,
        name=name,
        out_shape=outs,
        in_specs=in_specs,
        out_specs=out_specs,
        scratch_shapes=scratch,
        compiler_params=pltpu.CompilerParams(collective_id=cid, has_side_effects=True, vmem_limit_bytes=VMEM),
    )(*inputs)


def shape(dims, dtype):
    return jax.ShapeDtypeStruct(dims, dtype)


def normed(rows, gain):
    inverse = lax.rsqrt(jnp.mean(rows * rows, -1, keepdims=True) + EPS)
    scaled = rows * inverse
    return inverse, scaled, (scaled * gain).astype(BF16)


def enter(tokens, gain, query, key, value, out, gate, up, down):
    n_one, n_two, n_out = query.shape[1] * 3, PACK * 3, out.shape[0]

    def kernel(
        tokens_ref, gain_ref, query_ref, key_ref, value_ref, out_ref, gate_ref, up_ref, down_ref,
        rows_ref, full_ref, row_out_ref, row_ref, rest_ref, cos_ref, sin_ref,
        shard_one, row_one, stage_one, shard_out, shard_two, own, out_sems, in_sems,
    ):
        spot, post = Spot(), Post(out_sems, in_sems)
        for i in range(2):
            rows = pl.ds(i * 64, 64)
            for j, ref in enumerate((query_ref, key_ref, value_ref)):
                shard_one[i, :, j * 256 : (j + 1) * 256] = ref[rows, :]
        greet(spot, row_peers(spot) + y_peers(spot), 5, **gather_peers(spot))

        def weights():
            yield from gather_first(spot, post, shard_one, row_one, stage_one)
            yield from gather_second(spot, post, row_one, stage_one, full_ref)

        def tables():
            exponent = lax.broadcasted_iota(jnp.int32, (1, HD), 1)
            exponent = lax.rem(exponent, HD // 2).astype(F32)
            inverse = jnp.exp(exponent * (-2.0 / HD) * math.log(ROPE_BASE))
            sign = jnp.where(lax.broadcasted_iota(jnp.int32, (1, HD), 1) < HD // 2, -1.0, 1.0)

            def step(i, carry):
                angles = place_of(i * 16, 16, spot.xh, 0).astype(F32) * inverse
                strip = pl.ds(pl.multiple_of(i * 16, 16), 16)
                cos_ref[strip, :] = jnp.cos(angles)
                sin_ref[strip, :] = jnp.sin(angles) * sign
                return carry

            lax.fori_loop(0, 8 * ROWS // 16, step, 0)

        w = weights()
        next(w)

        def body(strip):
            own[strip, :] = normed(tokens_ref[strip, :].astype(F32), wide_gain(gain_ref))[2]

        in_strips(ROWS, body)
        r = gather_rows(spot, post, own, rows_ref)
        next(r)
        shard_out[...] = out_ref[...].astype(F32).T.astype(BF16)
        o = x_gather(spot, post, shard_out, lambda slot: row_out_ref.at[slot])
        next(o)
        shard_two[...] = jnp.zeros_like(shard_two)
        rest_ref[...] = jnp.zeros_like(rest_ref)
        wide = gate.shape[0]
        for j, ref in enumerate((gate_ref, up_ref, down_ref)):
            turned = ref[...].astype(F32).T.astype(BF16)
            shard_two[:, j * PACK : j * PACK + wide] = turned[:64]
            rest_ref[:, j * PACK : j * PACK + wide] = turned[64:]
        next(w)
        next(w)
        f = x_gather(spot, post, shard_two, lambda slot: row_ref.at[slot])
        next(f)
        next(o)
        next(r)
        tables()
        play("wfrwfor", r=r, w=w, f=f, o=o)

    half = pltpu.VMEM((4, 64, n_one), BF16)
    table = shape((8 * ROWS, HD), F32)
    return moving(
        kernel,
        "enter",
        (shape((8, ROWS, WIDE), BF16), shape((4, 4, 2, 64, n_one), BF16), shape((4, ROWS, n_out), BF16))
        + (shape((4, 64, n_two), BF16), shape((64, n_two), BF16), table, table),
        (tokens, gain, query, key, value, out, gate, up, down),
        [INSIDE] * 9,
        (ANY, ANY) + (INSIDE,) * 5,
        [pltpu.VMEM((2, 64, n_one), BF16), half, half, pltpu.VMEM((ROWS, n_out), BF16), pltpu.VMEM((64, n_two), BF16)]
        + [pltpu.VMEM((ROWS, WIDE), BF16)]
        + sems(60),
        1,
    )


def middle(mixed, weights, tokens, gain, row, stage):
    n = row.shape[-1]

    def kernel(
        mixed_hbm, weights_hbm, tokens_ref, gain_ref, row_ref, stage_ref, mid_ref, rows_ref, full_ref,
        mixed_ref, weights_ref, own, *rest,
    ):
        (outgoing, mine, land, far, gone), (out_sems, in_sems) = rest[:5], rest[5:]
        spot, post = Spot(), Post(out_sems, in_sems)
        loads = load(post, [(mixed_hbm, mixed_ref), (weights_hbm, weights_ref)])
        greet(spot, row_peers(spot) + y_peers(spot), 5, **gather_peers(spot))

        def main():
            for copy in loads:
                copy.wait()
            make = row_products(spot, [(mixed_ref, weights_ref, slice(None))], outgoing, mine)
            yield from scatter_rows(spot, post, make, outgoing, mine, land, far, gone)

            def body(strip):
                mid = tokens_ref[strip, :].astype(F32) + row_sum(spot, mine, land, gone, strip)
                mid_ref[strip, :] = mid
                own[strip, :] = normed(mid, wide_gain(gain_ref))[2]

            in_strips(ROWS, body)
            yield from gather_rows(spot, post, own, rows_ref)

        play("wmmmwmmm", m=main(), w=gather_second(spot, post, row_ref, stage_ref, full_ref))

    return moving(
        kernel,
        "middle",
        (shape((ROWS, WIDE), F32), shape((8, ROWS, WIDE), BF16), shape((4, 4, 2, 64, n), BF16)),
        (mixed, weights, tokens, gain, row, stage),
        [ANY, ANY, INSIDE, INSIDE, INSIDE, INSIDE],
        (INSIDE, ANY, ANY),
        [pltpu.VMEM(mixed.shape, BF16), pltpu.VMEM(weights.shape, BF16), pltpu.VMEM((ROWS, WIDE), BF16)]
        + scatter_scratch()
        + sems(64),
        2,
    )


def wide_gain(gain_ref):
    return gain_ref[...].astype(F32).reshape(1, WIDE)


def norm_back(upstream, rows, gain):
    inverse, scaled, _ = normed(rows, gain)
    weighted = upstream * gain
    through = inverse * (weighted - scaled * jnp.mean(weighted * scaled, -1, keepdims=True))
    return through, jnp.sum(upstream * scaled, 0, keepdims=True)


def turn(mid, gain, cotangent, rows, grads, d_gate, d_up, hidden, weights):
    n = 3 * PACK
    count = 8 * ROWS

    def kernel(
        mid_ref, gain_ref, cot_ref, rows_hbm, grads_hbm, gate_hbm, up_hbm, hid_hbm, weights_hbm,
        grad_ref, mid_rows_ref, feed_ref, sum_a, sum_b, out_hbm,
        own, rows_ref, grads_ref, gate_ref, up_ref, hid_ref, weights_ref, out_ref, *rest,
    ):
        (outgoing, mine, land, far, gone), room, (out_sems, in_sems) = rest[:5], rest[5:10], rest[10:]
        spot, post = Spot(), Post(out_sems, in_sems)
        loads = load(
            post,
            [(gate_hbm, gate_ref), (up_hbm, up_ref), (weights_hbm, weights_ref)]
            + [(rows_hbm, rows_ref), (hid_hbm, hid_ref), (grads_hbm, grads_ref)],
        )
        greet(spot, row_peers(spot) + y_peers(spot), 5, **collect_peers(spot))

        def main():
            for copy in loads[:3]:
                copy.wait()
            terms = [(ref, weights_ref, slice(i * PACK, (i + 1) * PACK)) for i, ref in enumerate((gate_ref, up_ref))]
            make = row_products(spot, terms, outgoing, mine)
            yield from scatter_rows(spot, post, make, outgoing, mine, land, far, gone)
            feed_ref[...] = jnp.zeros_like(feed_ref)

            def body(strip):
                upstream = row_sum(spot, mine, land, gone, strip)
                through, feed = norm_back(upstream, mid_ref[strip, :], wide_gain(gain_ref))
                grad = cot_ref[strip, :].astype(F32) + through
                grad_ref[strip, :] = grad
                own[strip, :] = grad.astype(BF16)
                feed_ref[...] += feed

            in_strips(ROWS, body)
            yield from gather_rows(spot, post, own, mid_rows_ref)

        def gradients():
            for copy in loads[3:]:
                copy.wait()
            groups = [(rows_ref, (gate_ref, up_ref)), (grads_ref, (hid_ref,))]
            yield from Gradients(spot, post, groups, *room, sum_a, sum_b).steps()

        def output():
            def step(i, carry):
                rows = pl.ds(pl.multiple_of(i * 256, 256), 256)
                out_ref[rows, :] = dot(hid_ref[rows, :], weights_ref[:, 2 * PACK :], 1, 1).astype(BF16)
                return carry

            lax.fori_loop(0, count // 256, step, 0)
            store = post.local(out_ref, out_hbm)
            store.start()
            yield
            store.wait()

        play("mggmgmgogmmgggggo", m=main(), g=gradients(), o=output())

    half = shape((4, 64, n), BF16)
    wide = pltpu.VMEM((count, WIDE), BF16)
    narrow = pltpu.VMEM((count, PACK), BF16)
    return moving(
        kernel,
        "turn",
        (
            shape((ROWS, WIDE), F32),
            shape((8, ROWS, WIDE), BF16),
            shape((1, WIDE), F32),
            half,
            half,
            shape((count, WIDE), BF16),
        ),
        (mid, gain, cotangent, rows, grads, d_gate, d_up, hidden, weights),
        [INSIDE, INSIDE, INSIDE] + [ANY] * 6,
        (INSIDE, ANY, INSIDE, INSIDE, INSIDE, ANY),
        [pltpu.VMEM((ROWS, WIDE), BF16), wide, wide, narrow, narrow, narrow, pltpu.VMEM((WIDE, n), BF16), wide]
        + scatter_scratch()
        + gradient_scratch(n)
        + sems(100),
        3,
    )


def leave(weights, tokens, gain, grad_mid, feed_part, rows, d_qkv, mid_rows, mixed, sum_two):
    n_qkv, n_out = d_qkv.shape[1], mixed.shape[1]
    n, n_two = n_qkv + n_out, sum_two.shape[-1]
    count = 8 * ROWS

    def kernel(
        weights_hbm, tokens_ref, gain_ref, grad_ref, feed_ref, rows_hbm, d_hbm, mid_hbm, mixed_hbm, sum_two_ref,
        token_ref, gains_ref, weight_ref, high_ref, norm_part, parts, from_y, over_y, from_chip, over_fsdp, from_tp,
        rows_ref, d_ref, mid_ref, mixed_ref, weights_ref, *rest,
    ):
        (outgoing, mine, land, far, gone), room, (sum_a, sum_b) = rest[:5], rest[5:10], rest[10:12]
        last, (out_sems, in_sems) = rest[12:18], rest[18:]
        spot, post = Spot(), Post(out_sems, in_sems)
        pairs = [(d_hbm, d_ref), (weights_hbm, weights_ref), (rows_hbm, rows_ref), (mixed_hbm, mixed_ref), (mid_hbm, mid_ref)]
        loads = load(post, pairs)
        greet(spot, row_peers(spot) + y_peers(spot) + gain_sources(spot), 5 + 13, **collect_peers(spot))

        def main():
            loads[1].wait()
            make = row_products(spot, [(d_ref, weights_ref, slice(None))], outgoing, mine)
            yield from scatter_rows(spot, post, make, outgoing, mine, land, far, gone)
            norm_part[...] = jnp.zeros_like(norm_part)

            def body(strip):
                upstream = row_sum(spot, mine, land, gone, strip)
                through, norm = norm_back(upstream, tokens_ref[strip, :].astype(F32), wide_gain(gain_ref))
                token_ref[strip, :] = grad_ref[strip, :] + through
                norm_part[...] += norm

            in_strips(ROWS, body)
            parts[...] = jnp.zeros_like(parts)
            for f in range(16):
                parts[f, 0:1, :] = norm_part[:, f * 128 : (f + 1) * 128]
                parts[f, 1:2, :] = feed_ref[:, f * 128 : (f + 1) * 128]
            yield from sum_gains(spot, post, parts, gains_ref, from_y, over_y, from_chip, over_fsdp, from_tp)

        def gradients():
            for copy in loads[:1] + loads[2:]:
                copy.wait()
            groups = [(rows_ref, (d_ref,)), (mid_ref, (mixed_ref,))]
            yield from Gradients(spot, post, groups, *room, sum_a, sum_b).steps()
            yield from together(
                scatter_low(spot, post, sum_a, strip_writer(weight_ref), *last[:2]),
                scatter_high(spot, post, sum_b, strip_writer(weight_ref, 64), *last[2:4]),
            )

        play(
            "bgmgbmgggmgggggmgmgmgbg",
            m=main(),
            g=gradients(),
            b=scatter_high(spot, post, sum_two_ref, strip_writer(high_ref), *last[4:]),
        )

    small = (8, 128)
    full_rows = pltpu.VMEM((count, WIDE), BF16)
    return moving(
        kernel,
        "leave",
        (shape((ROWS, WIDE), F32), shape(small, F32), shape((ROWS, n), F32), shape((64, n_two), F32)),
        (weights, tokens, gain, grad_mid, feed_part, rows, d_qkv, mid_rows, mixed, sum_two),
        [ANY, INSIDE, INSIDE, INSIDE, INSIDE] + [ANY] * 4 + [INSIDE],
        (INSIDE,) * 4,
        [pltpu.VMEM((1, WIDE), F32), pltpu.VMEM((16,) + small, F32)]
        + [pltpu.VMEM(dims + small, F32) for dims in ((3, 4), (4,), (3,), (), (7,))]
        + [full_rows, pltpu.VMEM((count, n_qkv), BF16), full_rows, pltpu.VMEM((count, n_out), BF16)]
        + [pltpu.VMEM(weights.shape, BF16)]
        + scatter_scratch()
        + gradient_scratch(n)
        + [pltpu.VMEM((4, 64, n), BF16)] * 2
        + low_scratch(n)
        + high_scratch(n)
        + high_scratch(n_two)
        + sems(120),
        4,
    )


def dot(a, b, da=1, db=0):
    return lax.dot_general(a, b, (((da,), (db,)), ((), ())), preferred_element_type=F32)


def plain(kernel, name, grid, inputs, in_specs, outs, out_specs, scratch=()):
    return pl.pallas_call(
        kernel,
        name=name,
        out_shape=outs,
        grid=grid,
        in_specs=in_specs,
        out_specs=out_specs,
        scratch_shapes=list(scratch),
        compiler_params=pltpu.CompilerParams(vmem_limit_bytes=VMEM),
    )(*inputs)


def by_rows(n, width, column=0):
    return pl.BlockSpec((n, width), lambda i: (i, column))


def whole(dims, *index):
    at = index or (0,) * len(dims)
    return pl.BlockSpec(dims, lambda i: at)


def project(rows, weights, cosine, sine):
    step = 512

    def kernel(rows_ref, w_ref, cos_ref, sin_ref, q_ref, kv_ref):
        out = dot(rows_ref[...], w_ref[...])
        cos, sin = cos_ref[...], sin_ref[...]
        for head in range(4):
            u = out[:, head * HD : (head + 1) * HD]
            turned = (u * cos + pltpu.roll(u, HD // 2, 1) * sin).astype(BF16)
            if head < 2:
                q_ref[:, head * HD : (head + 1) * HD] = turned
            else:
                kv_ref[head - 2, 0] = turned
                kv_ref[head - 2, 1] = out[:, (head + 2) * HD : (head + 3) * HD].astype(BF16)

    out = shape((8 * ROWS, 2 * HD), BF16)
    return plain(
        kernel,
        "project",
        (8 * ROWS // step,),
        (rows, weights, cosine, sine),
        [by_rows(step, WIDE), whole((WIDE, PACK)), by_rows(step, HD), by_rows(step, HD)],
        (out, shape((2, 2, 8 * ROWS, HD), BF16)),
        (by_rows(step, 2 * HD), pl.BlockSpec((2, 2, step, HD), lambda i: (0, 0, i, 0))),
    )


def feed_forward(rows, grads, weights):
    step = 256

    def kernel(rows_ref, grads_ref, g_ref, u_ref, d_ref, hid_ref, dgate_ref, dup_ref):
        gate = dot(rows_ref[...], g_ref[...])
        up = dot(rows_ref[...], u_ref[...])
        d_hid = dot(grads_ref[...], d_ref[...])
        sigma = 1.0 / (1.0 + jnp.exp(-gate))
        silu = gate * sigma
        hid_ref[...] = (silu * up).astype(BF16)
        dup_ref[...] = (d_hid * silu).astype(BF16)
        dgate_ref[...] = (d_hid * up * sigma * (1.0 + gate * (1.0 - sigma))).astype(BF16)

    out = shape((8 * ROWS, PACK), BF16)
    return plain(
        kernel,
        "feed_forward",
        (8 * ROWS // step,),
        (rows, grads, weights, weights, weights),
        [by_rows(step, WIDE)] * 2 + [whole((WIDE, PACK), 0, i) for i in range(3)],
        (out,) * 3,
        (by_rows(step, PACK),) * 3,
    )


def settle(layer, token_grad, gains, attention, low, high, wide):
    def kernel(
        layer_ref, token_ref, gains_ref, attention_ref, low_ref, high_ref,
        layer_out, token_out, norm_out, feed_out, query_out, key_out, value_out, out_out, gate_out, up_out, down_out,
    ):
        layer_out[...] = layer_ref[...]
        token_out[...] = token_ref[...]
        norm_out[...] = gains_ref[0:1, :]
        feed_out[...] = gains_ref[1:2, :]
        for i, out in enumerate((query_out, key_out, value_out)):
            out[...] = attention_ref[:, i * 2 * HD : (i + 1) * 2 * HD]
        out_out[...] = attention_ref[:, PACK:].T
        for i, out in enumerate((gate_out, up_out, down_out)):
            columns = slice(i * PACK, (i + 1) * PACK)
            out[...] = jnp.concatenate([low_ref[:, columns], high_ref[:, columns]], 0).T[:wide]

    vector = shape((1, 128), F32)
    square = shape((ROWS, 2 * HD), F32)
    tall = shape((wide, ROWS), F32)
    return pl.pallas_call(
        kernel,
        name="settle",
        out_shape=(shape(layer.shape, layer.dtype), shape(token_grad.shape, F32), vector, vector, square, square, square)
        + (shape((2 * HD, ROWS), F32), tall, tall, tall),
        in_specs=[INSIDE] * 6,
        out_specs=(INSIDE,) * 11,
        compiler_params=pltpu.CompilerParams(vmem_limit_bytes=VMEM),
    )(layer, token_grad, gains, attention, low, high)


TILE = 256
CHUNK = 512


def place_of(start, count, xh, axis):
    dims = (count, 1) if axis == 0 else (1, count)
    j = lax.broadcasted_iota(jnp.int32, dims, axis)
    return 2 * (j + start) - lax.rem(j + start, ROWS) + xh * ROWS


SPANS = ((0, 512, False), (512, 256, True))
LAST = (768, 256, True)


def scores_of(keys, q, span, q_pos, prefix, xh):
    start, count, masked = span
    scores = dot(keys, q, 1, 1) * (SCALE * LOG2E)
    if masked:
        k_pos = place_of(start, count, xh, 0)
        scores = jnp.where(jnp.logical_or(k_pos <= q_pos, k_pos < prefix), scores, -1e30)
    return scores


def tile_at(i):
    head, tile = lax.div(i, 4), lax.rem(i, 4)
    return head, tile, pl.ds(pl.multiple_of(head * HD, HD), HD), pl.ds(pl.multiple_of(tile * TILE, TILE), TILE)


def exchange(post, pairs, device):
    copies = [post.copy(src, dst, device) for src, dst in pairs]
    for copy in copies:
        copy.start()
    yield
    for copy in copies:
        copy.wait_recv()
        yield
    for copy in copies:
        copy.wait_send()


def prefix_of(prefixes_ref):
    return prefixes_ref[lax.div(lax.axis_index("fsdp"), 2)]


def attend(prefixes, queries, here, cotangent, row_out, second):
    n, n_two = row_out.shape[-1], second.shape[-1]

    def kernel(
        prefixes_ref, q_ref, here_ref, cot_ref, row_ref, second_ref, o_ref, lse_ref, there_ref, grads_ref, out_ref, stage_ref,
        top_ref, sum_ref, acc_ref, out_sems, in_sems,
    ):
        prefix = prefix_of(prefixes_ref)
        spot, post = Spot(), Post(out_sems, in_sems)
        partner = spot.at(dx=2)
        greet(spot, row_peers(spot) + y_peers(spot) + [partner], 6)

        def sweep(side, begin, end):
            keys_ref = there_ref if side else here_ref
            xh = 1 - spot.xh if side else spot.xh

            def step(i, carry):
                head, tile, cols, rows = tile_at(i)
                q = q_ref[rows, cols]
                q_pos = place_of(tile * TILE, TILE, spot.xh, 1)
                one = pl.ds(i, 1)

                def chunk(span, first):
                    keys = pl.ds(span[0], span[1])
                    scores = scores_of(keys_ref[head, 0, keys, :], q, span, q_pos, prefix, xh)
                    top = jnp.max(scores, 0, keepdims=True)
                    if not first:
                        before = top_ref[one, :]
                        top = jnp.maximum(top, before)
                    raised = jnp.exp2(scores - top)
                    total = jnp.sum(raised, 0, keepdims=True)
                    mixed = dot(keys_ref[head, 1, keys, :], raised.astype(BF16), 0, 0)
                    if not first:
                        fade = jnp.exp2(before - top)
                        total = total + sum_ref[one, :] * fade
                        mixed = mixed + acc_ref[i] * fade
                    top_ref[one, :] = top
                    sum_ref[one, :] = total
                    acc_ref[i] = mixed

                for number, span in enumerate(SPANS):
                    chunk(span, side == 0 and number == 0)

                @pl.when(tile == 3)
                def _():
                    chunk(LAST, False)

                if side == 1:
                    total = sum_ref[one, :]
                    o_ref[rows, cols] = (acc_ref[i] / total).T.astype(BF16)
                    lse_ref[one, :] = top_ref[one, :] + jnp.log2(total)
                return carry

            lax.fori_loop(begin, end, step, 0)

        def compute():
            sweep(0, 0, 8)
            yield
            sweep(1, 0, 4)
            yield
            sweep(1, 4, 8)

        play(
            "vesfcvsfecvsfecse",
            v=y_gather(spot, post, row_ref, lambda y: out_ref.at[y]),
            f=y_gather(spot, post, second_ref, lambda y: stage_ref.at[y]),
            e=exchange(post, [(here_ref.at[head], there_ref.at[head]) for head in range(2)], partner),
            s=gather_rows(spot, post, cot_ref, grads_ref),
            c=compute(),
        )

    return moving(
        kernel,
        "attend",
        (
            shape((8 * ROWS, 2 * HD), BF16),
            shape((8, TILE), F32),
            shape(here.shape, BF16),
            shape((8, ROWS, WIDE), BF16),
            shape((4, 4, ROWS, n), BF16),
            shape((4, 64, n_two), BF16),
        ),
        (prefixes, queries, here, cotangent, row_out, second),
        [pl.BlockSpec(memory_space=pltpu.SMEM)] + [INSIDE] * 5,
        (INSIDE, INSIDE, INSIDE, ANY, ANY, INSIDE),
        [pltpu.VMEM((8, TILE), F32), pltpu.VMEM((8, TILE), F32), pltpu.VMEM((8, HD, TILE), F32)] + sems(60),
        5,
    )


def attend_back(prefixes, queries, here, there, rows, weights, mixed, lse, cosine, sine, out_part, mid, sum_a):
    n = sum_a.shape[-1]

    def kernel(
        prefixes_ref, rows_hbm, weights_hbm, q_ref, here_ref, there_ref, o_ref, lse_ref, cos_ref, sin_ref, part_ref, mid_ref,
        sum_a_ref, d_ref, layer_ref, weight_ref, rows_ref, weights_ref, g_ref, delta_ref, dq_ref, acc_ref, near_ref, away_ref, land_ref, *rest,
    ):
        (outgoing, mine, land, far, gone), last, (out_sems, in_sems) = rest[:5], rest[5:7], rest[7:]
        prefix = prefix_of(prefixes_ref)
        spot, post = Spot(), Post(out_sems, in_sems)
        loads = load(post, [(weights_hbm, weights_ref), (rows_hbm, rows_ref)])
        partner = spot.at(dx=2)
        greet(spot, row_peers(spot) + y_peers(spot) + [partner], 6)

        def sweep(head, side, keys_ref, into):
            xh = spot.xh if side == 0 else 1 - spot.xh
            cols = pl.ds(head * HD, HD)
            into[...] = jnp.zeros_like(into)

            def step(tile, carry):
                i = head * 4 + tile
                rows = pl.ds(pl.multiple_of(tile * TILE, TILE), TILE)
                q, g = q_ref[rows, cols], g_ref[rows, cols]
                q_pos = place_of(tile * TILE, TILE, spot.xh, 1)
                if side == 1:
                    product = g.astype(F32) * o_ref[rows, cols].astype(F32)
                    delta_ref[pl.ds(i, 1), :] = jnp.sum(product.T, 0, keepdims=True)
                level, offset = lse_ref[pl.ds(i, 1), :], delta_ref[pl.ds(i, 1), :]

                def chunk(span, first):
                    span_rows = pl.ds(span[0], span[1])
                    keys = keys_ref[head, 0, span_rows, :]
                    probs = jnp.exp2(scores_of(keys, q, span, q_pos, prefix, xh) - level)
                    d_probs = dot(keys_ref[head, 1, span_rows, :], g, 1, 1)
                    d_scores = (probs * (d_probs - offset)).astype(BF16)
                    into[0, span_rows, :] += dot(d_scores, q)
                    into[1, span_rows, :] += dot(probs.astype(BF16), g)
                    d_query = dot(d_scores, keys, 0, 0)
                    dq_ref[i] = d_query if first else dq_ref[i] + d_query

                for number, span in enumerate(SPANS):
                    chunk(span, side == 1 and number == 0)

                @pl.when(tile == 3)
                def _():
                    chunk(LAST, False)

                if side == 0:
                    u = dq_ref[i] * SCALE
                    d_ref[rows, cols] = (u * cos_ref[rows, :] - pltpu.roll(u, HD // 2, 1) * sin_ref[rows, :]).astype(BF16)
                return carry

            lax.fori_loop(0, 4, step, 0)

        def compute():
            for copy in loads:
                copy.wait()

            def heads(i, carry):
                span = pl.ds(pl.multiple_of(i * 256, 256), 256)
                g_ref[span, :] = dot(rows_ref[span, :], weights_ref[...]).astype(BF16)
                return carry

            lax.fori_loop(0, 4, heads, 0)
            copies = []
            for head in range(2):
                sweep(head, 1, there_ref, acc_ref)
                away_ref[head] = acc_ref[...].astype(BF16)
                copies.append(post.copy(away_ref.at[head], land_ref.at[head], partner))
                copies[-1].start()
                yield
            for head in range(2):
                sweep(head, 0, here_ref, near_ref.at[head])
                yield
            for head in range(2):
                copies[head].wait_recv()
                cols = pl.ds(2 * HD + head * HD, HD)

                def finish(i, carry, head=head):
                    rows = pl.ds(pl.multiple_of(i * 128, 128), 128)
                    u = (near_ref[head, 0, rows, :] + land_ref[head, 0, rows, :].astype(F32)) * SCALE
                    back = u * cos_ref[rows, :] - pltpu.roll(u, HD // 2, 1) * sin_ref[rows, :]
                    d_ref[rows, pl.ds(2 * HD + head * HD, HD)] = back.astype(BF16)
                    v = near_ref[head, 1, rows, :] + land_ref[head, 1, rows, :].astype(F32)
                    d_ref[rows, pl.ds(4 * HD + head * HD, HD)] = v.astype(BF16)
                    return carry

                lax.fori_loop(0, 8, finish, 0)
            for copy in copies:
                copy.wait_send()

        def output():
            make = row_loads(spot, post, part_ref, outgoing, mine)
            yield from scatter_rows(spot, post, make, outgoing, mine, land, far, gone)

            def body(strip):
                layer_ref[strip, :] = (mid_ref[strip, :] + row_sum(spot, mine, land, gone, strip)).astype(BF16)

            in_strips(ROWS, body)

        play(
            "wcocowcoc",
            c=compute(),
            o=output(),
            w=scatter_low(spot, post, sum_a_ref, strip_writer(weight_ref), *last),
        )

    pair = (2, 8 * ROWS, HD)
    return moving(
        kernel,
        "attend_back",
        (shape((8 * ROWS, PACK), BF16), shape((ROWS, WIDE), BF16), shape((64, n), F32)),
        (prefixes, rows, weights, queries, here, there, mixed, lse, cosine, sine, out_part, mid, sum_a),
        [pl.BlockSpec(memory_space=pltpu.SMEM), ANY, ANY] + [INSIDE] * 7 + [ANY, INSIDE, INSIDE],
        (INSIDE,) * 3,
        [
            pltpu.VMEM(rows.shape, BF16),
            pltpu.VMEM(weights.shape, BF16),
            pltpu.VMEM((8 * ROWS, 2 * HD), BF16),
            pltpu.VMEM((8, TILE), F32),
            pltpu.VMEM((8, TILE, HD), F32),
            pltpu.VMEM(pair, F32),
            pltpu.VMEM((2,) + pair, F32),
            pltpu.VMEM((2,) + pair, BF16),
            pltpu.VMEM((2,) + pair, BF16),
        ]
        + scatter_scratch()
        + low_scratch(n)
        + sems(64),
        6,
    )


def on_device(
    tokens,
    prefixes,
    norm_gain,
    query_weight,
    key_weight,
    value_weight,
    output_weight,
    feed_gain,
    gate_weight,
    up_weight,
    down_weight,
    cotangent,
):
    rows_one, full_one, row_out, row_two, second, cosine, sine = enter(
        tokens, norm_gain, query_weight, key_weight, value_weight, output_weight, gate_weight.T, up_weight.T, down_weight
    )
    rows_one = rows_one.reshape(-1, WIDE)
    full_one = full_one.reshape(WIDE, -1)
    queries, here = project(rows_one, full_one, cosine, sine)
    attended, lse, there, grad_rows, full_out, stage_two = attend(prefixes, queries, here, cotangent, row_out, second)
    full_out = full_out.reshape(WIDE, -1)
    mid, rows_two, full_two = middle(attended, full_out, tokens, feed_gain, row_two, stage_two)
    rows_two, grad_rows, full_two = (a.reshape(-1, a.shape[-1]) for a in (rows_two, grad_rows, full_two.reshape(WIDE, -1)))
    hidden, d_gate, d_up = feed_forward(rows_two, grad_rows, full_two)
    grad_mid, mid_rows, feed_part, sum_a, sum_b, part_out = turn(
        mid, feed_gain, cotangent, rows_two, grad_rows, d_gate, d_up, hidden, full_two
    )
    mid_rows = mid_rows.reshape(-1, WIDE)
    d_qkv, layer_output, low = attend_back(
        prefixes, queries, here, there, mid_rows, full_out, attended, lse, cosine, sine, part_out.reshape(8, ROWS, WIDE), mid, sum_a
    )
    token_grad, gains, attention, high = leave(
        full_one, tokens, norm_gain, grad_mid, feed_part, rows_one, d_qkv, mid_rows, attended, sum_b
    )
    layer_output, token_grad, norm_grad, feed_grad, *grads = settle(
        layer_output, token_grad, gains, attention, low, high, gate_weight.shape[1]
    )
    query_grad, key_grad, value_grad, output_grad, gate_grad, up_grad, down_grad = grads
    return (
        layer_output,
        token_grad,
        norm_grad[0],
        query_grad,
        key_grad,
        value_grad,
        output_grad,
        feed_grad[0],
        gate_grad.T,
        up_grad.T,
        down_grad,
    )


def solution(mesh):
    rows = P(("fsdp", "tp"), None)
    wide = P("fsdp", "tp")
    tall = P("tp", "fsdp")
    return jax.shard_map(
        on_device,
        mesh=mesh,
        in_specs=(rows, P(), P(), wide, wide, wide, tall, P(), wide, wide, tall, rows),
        out_specs=(rows, rows, P("fsdp"), wide, wide, wide, tall, P("fsdp"), wide, wide, tall),
        check_vma=False,
    )
```

```python
import functools
import math

import jax
import jax.numpy as jnp
from jax import lax
from jax.experimental import pallas as pl
from jax.experimental.pallas import tpu as pltpu
from jax.sharding import PartitionSpec as P

HD = 128
EPS = 1e-05
ROPE_BASE = 10000.0
F32 = jnp.float32
BF16 = jnp.bfloat16
MESH = pl.DeviceIdType.MESH
AXES = ("fsdp", "tp")
ROWS = 128
WIDE = 2048
PACK = 768
SCALE = 1.0 / math.sqrt(HD)
LOG2E = 1.4426950408889634
VMEM = 60 << 20


class Spot:
    def __init__(self):
        f, t = lax.axis_index("fsdp"), lax.axis_index("tp")
        self.y, self.xl, self.c = lax.div(f, 4), lax.rem(lax.div(f, 2), 2), lax.rem(f, 2)
        self.z, self.xh = lax.div(t, 2), lax.rem(t, 2)
        self.x = self.xh * 2 + self.xl
        self.own = self.xl * 2 + self.c
        self.away = lax.rem(self.xh + self.c, 2)
        self.home = self.away == 0
        self.turn = 1 - lax.rem(self.away + self.xl, 2)
        self.ahead = 1 + 2 * self.turn
        self.back = 3 - 2 * self.turn
        self.near = (1 - self.xl) * 2
        self.same = self.xl * 2

    def at(self, dy=0, dx=0, dz=0, core=None):
        y, z, x = lax.rem(self.y + dy, 4), lax.rem(self.z + dz, 4), lax.rem(self.x + dx, 4)
        return (y * 4 + lax.rem(x, 2) * 2 + (self.c if core is None else core), z * 2 + lax.div(x, 2))

    def other(self):
        return self.at(core=1 - self.c)

    def seat(self, slot):
        return (self.y * 4 + slot, self.z * 2 + self.c)

    def bench(self, slot):
        return (self.y * 4 + slot, self.z * 2 + self.xh)

    def block(self, dz=0, flip=False):
        return (1 - self.c if flip else self.c) * 4 + lax.rem(self.z + dz, 4)


class Post:
    def __init__(self, out_sems, in_sems):
        self.out_sems, self.in_sems, self.n_out, self.n_in = out_sems, in_sems, 0, 0

    def slots(self, n):
        base = self.n_in
        self.n_in += n
        return base

    def copy(self, src, dst, device, slot=None):
        slot = self.slots(1) if slot is None else slot
        self.n_out += 1
        return pltpu.make_async_remote_copy(
            src_ref=src,
            dst_ref=dst,
            send_sem=self.out_sems.at[self.n_out - 1],
            recv_sem=self.in_sems.at[slot],
            device_id=device,
            device_id_type=MESH,
        )

    def arrival(self, dst, device, slot):
        return pltpu.make_async_remote_copy(
            src_ref=dst,
            dst_ref=dst,
            send_sem=self.out_sems.at[0],
            recv_sem=self.in_sems.at[slot],
            device_id=device,
            device_id_type=MESH,
        )

    def local(self, src, dst):
        self.n_out += 1
        return pltpu.make_async_copy(src, dst, self.out_sems.at[self.n_out - 1])


def greet(spot, sources, count, home=(), away=()):
    barrier = pltpu.get_barrier_semaphore()

    def signal(devices):
        for device in devices:
            pl.semaphore_signal(barrier, inc=1, device_id=device, device_id_type=MESH)

    signal(sources)
    if home:
        count = count + 3 + spot.away

        @pl.when(spot.home)
        def _():
            signal(home)

        @pl.when(jnp.logical_not(spot.home))
        def _():
            signal(away)

    pl.semaphore_wait(barrier, count)


def row_peers(spot):
    return [spot.at(dz=1), spot.at(dz=3), spot.other()]


def y_peers(spot):
    return [spot.at(dy=1), spot.at(dy=3)]


def gather_peers(spot):
    near = [spot.at(dx=spot.back, core=0), spot.at(dx=spot.back, core=1)]
    return {"home": near + [spot.other()], "away": near + [spot.at(dx=1), spot.at(dx=3)]}


def collect_peers(spot):
    usual = [spot.at(dx=1, core=spot.xh), spot.at(dx=3, core=spot.xh), spot.at(dx=spot.ahead)]
    return {"home": usual, "away": usual + [spot.other()]}


def half_of(ref, number):
    rows = ref.shape[0] // 2
    return ref.at[pl.ds(number * rows, rows)]


def after(spot, k):
    return lax.rem(spot.own + k, 4)


def play(order, **jobs):
    for letter in order:
        next(jobs[letter], None)
    for job in jobs.values():
        for _ in job:
            pass


def gather_rows(spot, post, own, rows):
    up, down, core = spot.at(dz=1), spot.at(dz=3), spot.other()
    half = ROWS // 2
    low, high = pl.ds(0, half), pl.ds(half, half)
    here, below, above, far = (spot.block(dz) for dz in (0, 3, 1, 2))
    a = post.copy(own, rows.at[here], up)
    b = post.copy(own, rows.at[here], down)
    k0 = post.copy(own, rows.at[here], core)
    keep = post.local(own, rows.at[here])
    for copy in (a, b, k0, keep):
        copy.start()
    yield
    a.wait_recv()
    fa = post.copy(rows.at[below, low], rows.at[below, low], up)
    k1 = post.copy(rows.at[below], rows.at[below], core)
    fa.start()
    k1.start()
    b.wait_recv()
    fb = post.copy(rows.at[above, high], rows.at[above, high], down)
    k2 = post.copy(rows.at[above], rows.at[above], core)
    fb.start()
    k2.start()
    yield
    fa.wait_recv()
    fb.wait_recv()
    k3 = post.copy(rows.at[far], rows.at[far], core)
    k3.start()
    yield
    keep.wait()
    for copy in (k0, k1, k2, k3):
        copy.wait_recv()
    for copy in (a, b, fa, fb, k0, k1, k2, k3):
        copy.wait_send()


def in_strips(count, body):
    def step(i, carry):
        body(pl.ds(pl.multiple_of(i * 16, 16), 16))
        return carry

    lax.fori_loop(0, count // 16, step, 0)


def add_into(target, other, rows=ROWS, start=0):
    def body(strip):
        strip = pl.ds(pl.multiple_of(strip.start + start, 16), 16)
        target[strip, :] = (target[strip, :].astype(F32) + other[strip, :].astype(F32)).astype(BF16)

    in_strips(rows, body)


def row_products(spot, terms, outgoing, mine):
    def make(k, z):
        other, own = pl.ds(((1 - spot.c) * 4 + z) * ROWS, ROWS), pl.ds((spot.c * 4 + z) * ROWS, ROWS)

        def step(i, carry):
            columns = pl.ds(pl.multiple_of(i * 512, 512), 512)
            total = None
            for a, w, part in terms:
                term = dot(jnp.concatenate([a[other, :], a[own, :]], 0), w[columns, part], 1, 1)
                total = term if total is None else total + term
            outgoing[z, :, columns] = total[:ROWS].astype(BF16)
            mine[z, :, columns] = total[ROWS:].astype(BF16)
            return carry

        lax.fori_loop(0, WIDE // 512, step, 0)

    return make


def row_loads(spot, post, part, outgoing, mine):
    copies = []
    for z in row_order(spot):
        pairs = [(part.at[(1 - spot.c) * 4 + z], outgoing.at[z]), (part.at[spot.c * 4 + z], mine.at[z])]
        copies.append(load(post, pairs))

    def make(k, z):
        for copy in copies[k]:
            copy.wait()

    return make


def row_order(spot):
    return [lax.rem(spot.z + dz, 4) for dz in (2, 3, 1, 0)]


def scatter_rows(spot, post, make, outgoing, mine, land, far, gone, ahead=False):
    up, down, core = spot.at(dz=1), spot.at(dz=3), spot.other()
    half = ROWS // 2
    low, high = pl.ds(0, half), pl.ds(half, half)
    steps = row_order(spot)
    distant, lower, upper, here = steps
    to_core, others = [], []

    def begin(k):
        if len(to_core) > k:
            return
        make(k, steps[k])
        to_core.append(post.copy(outgoing.at[steps[k]], land.at[steps[k]], core))
        to_core[k].start()

    def pass_on(src, dst, device):
        others.append(post.copy(src, dst, device))
        others[-1].start()
        return others[-1]

    def ready(k):
        to_core[k].wait_recv()
        if k < 3:
            add_into(mine.at[steps[k]], land.at[steps[k]])

    if ahead:
        for k in range(4):
            begin(k)
        yield
    begin(0)
    begin(1)
    ready(0)
    f_low = pass_on(mine.at[distant, low], far.at[low], down)
    f_high = pass_on(mine.at[distant, high], far.at[high], up)
    begin(2)
    ready(1)
    gone_copies = [pass_on(mine.at[lower, high], gone.at[0, high], down)]
    begin(3)
    ready(2)
    gone_copies.append(pass_on(mine.at[upper, low], gone.at[1, low], up))
    yield
    ready(3)
    f_low.wait_recv()
    add_into(mine.at[lower], far, half)
    gone_copies.append(pass_on(mine.at[lower, low], gone.at[0, low], down))
    f_high.wait_recv()
    add_into(mine.at[upper], far, half, half)
    gone_copies.append(pass_on(mine.at[upper, high], gone.at[1, high], up))
    yield
    for copy in gone_copies:
        copy.wait_recv()
    for copy in to_core + others:
        copy.wait_send()


def row_sum(spot, mine, land, gone, strip):
    parts = [mine[spot.z, strip, :], land[spot.z, strip, :], gone[0, strip, :], gone[1, strip, :]]
    return sum(part.astype(F32) for part in parts)


def scatter_scratch():
    block = (ROWS, WIDE)
    return [
        pltpu.VMEM((4,) + block, BF16),
        pltpu.VMEM((4,) + block, BF16),
        pltpu.VMEM((4,) + block, BF16),
        pltpu.VMEM(block, BF16),
        pltpu.VMEM((2,) + block, BF16),
    ]


def x_gather(spot, post, src, dst_at):
    base, far = post.slots(4), post.slots(4)
    sends = [post.copy(src, dst_at(spot.own), spot.at(dx=dx, core=spot.xh), base + spot.own) for dx in (1, 3)]
    cross = post.copy(src, dst_at(spot.own), spot.other(), base + spot.own)
    keep = post.local(src, dst_at(spot.own))
    for copy in sends:
        copy.start()

    @pl.when(spot.home)
    def _():
        keep.start()

    @pl.when(jnp.logical_not(spot.home))
    def _():
        cross.start()

    def landed(dst, slot):
        post.arrival(dst, spot.at(dx=1), slot).wait_recv()

    yield
    for core in range(2):
        block = dst_at(spot.near + core)
        landed(block, base + spot.near + core)
        part = half_of(block, spot.turn)
        sends.append(post.copy(part, part, spot.at(dx=spot.ahead), far + 2 * core + spot.turn))
        sends[-1].start()
    yield

    @pl.when(spot.home)
    def _():
        slot = spot.same + 1 - spot.c
        landed(dst_at(slot), base + slot)
        keep.wait()

    @pl.when(jnp.logical_not(spot.home))
    def _():
        for core in range(2):
            for number in range(2):
                landed(half_of(dst_at(spot.same + core), number), far + 2 * core + number)
        cross.wait_send()

    for copy in sends:
        copy.wait_send()


def y_gather(spot, post, src, dst_at):
    up, down = spot.at(dy=1), spot.at(dy=3)
    here, below, above = dst_at(spot.y), dst_at(lax.rem(spot.y + 3, 4)), dst_at(lax.rem(spot.y + 1, 4))
    a, b, keep = post.copy(src, here, up), post.copy(src, here, down), post.local(src, here)
    for copy in (a, b, keep):
        copy.start()
    yield
    a.wait_recv()
    fa = post.copy(half_of(below, 0), half_of(below, 0), up)
    fa.start()
    b.wait_recv()
    fb = post.copy(half_of(above, 1), half_of(above, 1), down)
    fb.start()
    yield
    keep.wait()
    for copy in (fa, fb):
        copy.wait_recv()
    for copy in (a, b, fa, fb):
        copy.wait_send()


def together(*jobs):
    live = list(jobs)
    while live:
        live = [job for job in live if next(job, job) is not job]
        if live:
            yield


def gather_first(spot, post, shard, row, stage):
    return together(
        x_gather(spot, post, shard.at[0], lambda slot: row.at[slot]),
        y_gather(spot, post, shard.at[1], lambda y: stage.at[y]),
    )


def gather_second(spot, post, row, stage, full):
    return together(
        x_gather(spot, post, stage, lambda slot: full.at[:, slot, 1]),
        y_gather(spot, post, row, lambda y: full.at[y, :, 0]),
    )


def sum_parts(parts, write):
    def body(strip):
        write(strip, sum(part[strip, :].astype(F32) for part in parts))

    in_strips(parts[0].shape[0], body)


def add_block(target, other):
    if len(target.shape) == 2:
        add_into(target, other, target.shape[0])
    else:

        def step(i, carry):
            add_into(target.at[i], other.at[i], target.shape[1])
            return carry

        lax.fori_loop(0, target.shape[0], step, 0)


class XCollect:
    def __init__(self, spot, post, src_at, land, hop):
        self.spot, self.post, self.src_at, self.land, self.hop = spot, post, src_at, land, hop
        self.in_land, self.in_hop = post.slots(5), post.slots(2)
        self.sends = []

    def to_near(self, core, src, number):
        spot = self.spot
        copy = self.post.copy(
            src,
            half_of(self.land.at[spot.turn], number),
            spot.seat(spot.near + core),
            self.in_land + 2 * spot.turn + number,
        )
        copy.start()
        self.sends.append(copy)

    def start(self):
        spot, post = self.spot, self.post
        cross_slot = spot.same + 1 - spot.c
        self.cross = post.copy(self.src_at(cross_slot), self.land.at[2], spot.other(), self.in_land + 4)
        self.keep = post.local(self.src_at(spot.own), self.land.at[2])
        self.far = []
        for core in range(2):
            for number, dx in ((0, 3), (1, 1)):
                src = half_of(self.src_at(spot.same + core), number)
                self.far.append(post.copy(src, self.hop.at[core], spot.at(dx=dx), self.in_hop + core))

        @pl.when(spot.home)
        def _():
            self.cross.start()
            self.keep.start()

        @pl.when(jnp.logical_not(spot.home))
        def _():
            for copy in self.far:
                copy.start()

        for core in range(2):
            self.to_near(core, half_of(self.src_at(spot.near + core), 1 - spot.turn), 1 - spot.turn)

    def relay(self):
        spot, post = self.spot, self.post
        for core in range(2):
            post.arrival(self.hop.at[core], spot.at(dx=1), self.in_hop + core).wait_recv()
            add_block(self.hop.at[core], half_of(self.src_at(spot.near + core), spot.turn))
            self.to_near(core, self.hop.at[core], spot.turn)

    def finish(self):
        spot, post = self.spot, self.post
        for side in range(2):
            for number in range(2):
                dst = half_of(self.land.at[side], number)
                post.arrival(dst, spot.at(dx=1), self.in_land + 2 * side + number).wait_recv()

        @pl.when(spot.home)
        def _():
            self.keep.wait()
            self.cross.wait_send()

        @pl.when(jnp.logical_not(spot.home))
        def _():
            post.arrival(self.land.at[2], spot.at(dx=1), self.in_land + 4).wait_recv()
            for copy in self.far:
                copy.wait_send()

        for copy in self.sends:
            copy.wait_send()

    def parts(self):
        return [self.land.at[side] for side in range(3)]


class YCollect:
    def __init__(self, spot, post, src_at, land, hop):
        self.spot, self.post, self.src_at, self.land, self.hop = spot, post, src_at, land, hop
        self.up, self.down = spot.at(dy=1), spot.at(dy=3)
        self.y = [lax.rem(spot.y + k, 4) for k in range(4)]

    def start_far(self):
        block = self.src_at(self.y[2])
        self.far = [
            self.post.copy(half_of(block, 0), self.hop.at[0], self.down),
            self.post.copy(half_of(block, 1), self.hop.at[1], self.up),
        ]
        for copy in self.far:
            copy.start()

    def start_lower(self):
        self.low = [self.post.copy(half_of(self.src_at(self.y[3]), 1), half_of(self.land.at[0], 1), self.down)]
        self.low[0].start()

    def start_upper(self):
        self.high = [self.post.copy(half_of(self.src_at(self.y[1]), 0), half_of(self.land.at[1], 0), self.up)]
        self.high[0].start()

    def relay(self):
        for number, k, target in ((0, 3, self.down), (1, 1, self.up)):
            self.far[number].wait_recv()
            hop = self.hop.at[number]
            add_block(hop, half_of(self.src_at(self.y[k]), number))
            copy = self.post.copy(hop, half_of(self.land.at[number], number), target)
            copy.start()
            (self.low if number == 0 else self.high).append(copy)

    def finish(self):
        for copy in self.low + self.high:
            copy.wait_recv()
        for copy in self.far + self.low + self.high:
            copy.wait_send()

    def parts(self):
        return [self.src_at(self.spot.y), self.land.at[0], self.land.at[1]]


class Gradients:
    def __init__(self, spot, post, groups, full, land_x, hop_x, land_y, hop_y, sum_a, sum_b):
        self.spot, self.groups, self.full, self.sum_a, self.sum_b = spot, groups, full, sum_a, sum_b
        self.y = [lax.rem(spot.y + k, 4) for k in (2, 3, 1, 0)]
        self.x = [
            XCollect(spot, post, lambda slot, y=y: full.at[y, slot, 0], land_x.at[j], hop_x.at[j])
            for j, y in enumerate(self.y)
        ]
        self.over_y = YCollect(spot, post, lambda y: full.at[y, :, 1], land_y, hop_y)

    def make(self, j):
        y = self.y[j]

        def part(s, carry):
            columns = pl.ds(pl.multiple_of(y * 512 + s * 256, 256), 256)
            at = 0
            for rows, values in self.groups:
                left = rows[:, columns]
                for value in values:
                    width = value.shape[1]
                    block = dot(left, value[...], 0, 0).astype(BF16)
                    for i in range(4):
                        self.full[y, 2 * s + i // 2, i % 2, :, at : at + width] = block[i * 64 : (i + 1) * 64]
                    at += width
            return carry

        lax.fori_loop(0, 2, part, 0)
        (self.over_y.start_far, self.over_y.start_lower, self.over_y.start_upper, lambda: None)[j]()
        self.x[j].start()

    def sum_x(self, j):
        def write(strip, total):
            self.sum_a[self.y[j], strip, :] = total.astype(BF16)

        self.x[j].finish()
        sum_parts(self.x[j].parts(), write)

    def sum_y(self):
        self.over_y.finish()

        def slot_sum(slot, carry):
            def write(strip, total):
                self.sum_b[slot, strip, :] = total.astype(BF16)

            sum_parts([part.at[slot] for part in self.over_y.parts()], write)
            return carry

        lax.fori_loop(0, 4, slot_sum, 0)

    def steps(self):
        self.make(0)
        yield
        self.make(1)
        yield
        self.make(2)
        self.x[0].relay()
        yield
        self.make(3)
        self.x[1].relay()
        yield
        self.over_y.relay()
        self.x[2].relay()
        yield
        self.x[3].relay()
        yield
        for j in range(4):
            self.sum_x(j)
            yield
        self.sum_y()


def load(post, pairs):
    copies = [post.local(src, dst) for src, dst in pairs]
    for copy in copies:
        copy.start()
    return copies


def gradient_scratch(n):
    return [
        pltpu.VMEM((4, 4, 2, 64, n), BF16),
        pltpu.VMEM((4, 3, 64, n), BF16),
        pltpu.VMEM((4, 2, 32, n), BF16),
        pltpu.VMEM((2, 4, 64, n), BF16),
        pltpu.VMEM((2, 2, 64, n), BF16),
    ]


def scatter_low(spot, post, sum_a, write, land, hop):
    over_y = YCollect(spot, post, lambda y: sum_a.at[y], land, hop)
    over_y.start_far()
    over_y.start_lower()
    over_y.start_upper()
    yield
    over_y.relay()
    yield
    over_y.finish()
    sum_parts(over_y.parts(), write)


def scatter_high(spot, post, sum_b, write, land, hop):
    over_x = XCollect(spot, post, lambda slot: sum_b.at[slot], land, hop)
    over_x.start()
    yield
    over_x.relay()
    yield
    over_x.finish()
    sum_parts(over_x.parts(), write)


def strip_writer(out, start=0):
    def write(strip, total):
        out[pl.ds(pl.multiple_of(strip.start + start, 16), 16), :] = total

    return write


def low_scratch(n):
    return [pltpu.VMEM((2, 64, n), BF16), pltpu.VMEM((2, 32, n), BF16)]


def high_scratch(n):
    return [pltpu.VMEM((3, 64, n), BF16), pltpu.VMEM((2, 32, n), BF16)]


def sum_gains(spot, post, parts, out, from_y, over_y, from_chip, over_fsdp, from_tp):
    y_copies = []
    for i, k in enumerate((2, 1, 3)):
        y = lax.rem(spot.y + k, 4)
        y_copies.append(post.copy(parts.at[pl.ds(y * 4, 4)], from_y.at[i], spot.at(dy=k)))
        y_copies[-1].start()
    yield
    for copy in y_copies:
        copy.wait_recv()
    over_y[...] = parts[pl.ds(spot.y * 4, 4)] + from_y[0] + from_y[1] + from_y[2]
    chip_copies = []
    for i, k in enumerate((1, 2, 3)):
        slot = after(spot, k)
        chip_copies.append(post.copy(over_y.at[slot], from_chip.at[i], spot.bench(slot)))
        chip_copies[-1].start()
    yield
    for copy in chip_copies:
        copy.wait_recv()
    over_fsdp[...] = over_y[spot.own] + from_chip[0] + from_chip[1] + from_chip[2]
    tp_copies = []
    for i, (dz, dx) in enumerate(TP_MOVES):
        tp_copies.append(post.copy(over_fsdp, from_tp.at[i], spot.at(dz=dz, dx=dx)))
        tp_copies[-1].start()
    yield
    for copy in tp_copies:
        copy.wait_recv()
    out[...] = over_fsdp[...] + sum(from_tp[i] for i in range(7))
    for copy in y_copies + chip_copies + tp_copies:
        copy.wait_send()


TP_MOVES = [(dz, dx) for dx in (0, 2) for dz in (0, 1, 2, 3) if (dz, dx) != (0, 0)]


def gain_sources(spot):
    return (
        [spot.at(dy=k) for k in (1, 2, 3)]
        + [spot.bench(after(spot, k)) for k in (1, 2, 3)]
        + [spot.at(dz=(4 - dz) % 4, dx=dx) for dz, dx in TP_MOVES]
    )


ANY = pl.BlockSpec(memory_space=pl.ANY)
INSIDE = pl.BlockSpec(memory_space=pltpu.VMEM)


def sems(n):
    return [pltpu.SemaphoreType.DMA((n,)), pltpu.SemaphoreType.DMA((n,))]


def moving(kernel, name, outs, inputs, in_specs, out_specs, scratch, cid):
    return pl.pallas_call(
        kernel,
        name=name,
        out_shape=outs,
        in_specs=in_specs,
        out_specs=out_specs,
        scratch_shapes=scratch,
        compiler_params=pltpu.CompilerParams(collective_id=cid, has_side_effects=True, vmem_limit_bytes=VMEM),
    )(*inputs)


def shape(dims, dtype):
    return jax.ShapeDtypeStruct(dims, dtype)


def normed(rows, gain):
    inverse = lax.rsqrt(jnp.mean(rows * rows, -1, keepdims=True) + EPS)
    scaled = rows * inverse
    return inverse, scaled, (scaled * gain).astype(BF16)


def enter(tokens, gain, query, key, value, out, gate, up, down):
    n_one, n_two, n_out = query.shape[1] * 3, PACK * 3, out.shape[0]

    def kernel(
        tokens_ref, gain_ref, query_ref, key_ref, value_ref, out_ref, gate_ref, up_ref, down_ref,
        rows_ref, full_ref, row_out_ref, row_ref, rest_ref, cos_ref, sin_ref,
        shard_one, row_one, stage_one, shard_out, shard_two, own, out_sems, in_sems,
    ):
        spot, post = Spot(), Post(out_sems, in_sems)
        for i in range(2):
            rows = pl.ds(i * 64, 64)
            for j, ref in enumerate((query_ref, key_ref, value_ref)):
                shard_one[i, :, j * 256 : (j + 1) * 256] = ref[rows, :]
        greet(spot, row_peers(spot) + y_peers(spot), 5, **gather_peers(spot))

        def weights():
            yield from gather_first(spot, post, shard_one, row_one, stage_one)
            yield from gather_second(spot, post, row_one, stage_one, full_ref)

        def tables():
            exponent = lax.broadcasted_iota(jnp.int32, (1, HD), 1)
            exponent = lax.rem(exponent, HD // 2).astype(F32)
            inverse = jnp.exp(exponent * (-2.0 / HD) * math.log(ROPE_BASE))
            sign = jnp.where(lax.broadcasted_iota(jnp.int32, (1, HD), 1) < HD // 2, -1.0, 1.0)

            def step(i, carry):
                angles = place_of(i * 16, 16, spot.xh, 0).astype(F32) * inverse
                strip = pl.ds(pl.multiple_of(i * 16, 16), 16)
                cos_ref[strip, :] = jnp.cos(angles)
                sin_ref[strip, :] = jnp.sin(angles) * sign
                return carry

            lax.fori_loop(0, 8 * ROWS // 16, step, 0)

        w = weights()
        next(w)

        def body(strip):
            own[strip, :] = normed(tokens_ref[strip, :].astype(F32), wide_gain(gain_ref))[2]

        in_strips(ROWS, body)
        r = gather_rows(spot, post, own, rows_ref)
        next(r)
        shard_out[...] = out_ref[...].astype(F32).T.astype(BF16)
        o = x_gather(spot, post, shard_out, lambda slot: row_out_ref.at[slot])
        next(o)
        shard_two[...] = jnp.zeros_like(shard_two)
        rest_ref[...] = jnp.zeros_like(rest_ref)
        wide = gate.shape[0]
        for j, ref in enumerate((gate_ref, up_ref, down_ref)):
            turned = ref[...].astype(F32).T.astype(BF16)
            shard_two[:, j * PACK : j * PACK + wide] = turned[:64]
            rest_ref[:, j * PACK : j * PACK + wide] = turned[64:]
        next(w)
        next(w)
        f = x_gather(spot, post, shard_two, lambda slot: row_ref.at[slot])
        next(f)
        next(o)
        next(r)
        tables()
        play("wfrwfor", r=r, w=w, f=f, o=o)

    half = pltpu.VMEM((4, 64, n_one), BF16)
    table = shape((8 * ROWS, HD), F32)
    return moving(
        kernel,
        "enter",
        (shape((8, ROWS, WIDE), BF16), shape((4, 4, 2, 64, n_one), BF16), shape((4, ROWS, n_out), BF16))
        + (shape((4, 64, n_two), BF16), shape((64, n_two), BF16), table, table),
        (tokens, gain, query, key, value, out, gate, up, down),
        [INSIDE] * 9,
        (ANY, ANY) + (INSIDE,) * 5,
        [pltpu.VMEM((2, 64, n_one), BF16), half, half, pltpu.VMEM((ROWS, n_out), BF16), pltpu.VMEM((64, n_two), BF16)]
        + [pltpu.VMEM((ROWS, WIDE), BF16)]
        + sems(60),
        1,
    )


def middle(mixed, weights, tokens, gain, row, stage):
    n = row.shape[-1]

    def kernel(
        mixed_hbm, weights_hbm, tokens_ref, gain_ref, row_ref, stage_ref, mid_ref, rows_ref, full_ref,
        mixed_ref, weights_ref, own, *rest,
    ):
        (outgoing, mine, land, far, gone), (out_sems, in_sems) = rest[:5], rest[5:]
        spot, post = Spot(), Post(out_sems, in_sems)
        loads = load(post, [(mixed_hbm, mixed_ref), (weights_hbm, weights_ref)])
        greet(spot, row_peers(spot) + y_peers(spot), 5, **gather_peers(spot))

        def main():
            for copy in loads:
                copy.wait()
            make = row_products(spot, [(mixed_ref, weights_ref, slice(None))], outgoing, mine)
            yield from scatter_rows(spot, post, make, outgoing, mine, land, far, gone)

            def body(strip):
                mid = tokens_ref[strip, :].astype(F32) + row_sum(spot, mine, land, gone, strip)
                mid_ref[strip, :] = mid
                own[strip, :] = normed(mid, wide_gain(gain_ref))[2]

            in_strips(ROWS, body)
            yield from gather_rows(spot, post, own, rows_ref)

        play("wmmmwmmm", m=main(), w=gather_second(spot, post, row_ref, stage_ref, full_ref))

    return moving(
        kernel,
        "middle",
        (shape((ROWS, WIDE), F32), shape((8, ROWS, WIDE), BF16), shape((4, 4, 2, 64, n), BF16)),
        (mixed, weights, tokens, gain, row, stage),
        [ANY, ANY, INSIDE, INSIDE, INSIDE, INSIDE],
        (INSIDE, ANY, ANY),
        [pltpu.VMEM(mixed.shape, BF16), pltpu.VMEM(weights.shape, BF16), pltpu.VMEM((ROWS, WIDE), BF16)]
        + scatter_scratch()
        + sems(64),
        2,
    )


def wide_gain(gain_ref):
    return gain_ref[...].astype(F32).reshape(1, WIDE)


def norm_back(upstream, rows, gain):
    inverse, scaled, _ = normed(rows, gain)
    weighted = upstream * gain
    through = inverse * (weighted - scaled * jnp.mean(weighted * scaled, -1, keepdims=True))
    return through, jnp.sum(upstream * scaled, 0, keepdims=True)


def turn(mid, gain, cotangent, rows, grads, d_gate, d_up, hidden, weights):
    n = 3 * PACK
    count = 8 * ROWS

    def kernel(
        mid_ref, gain_ref, cot_ref, rows_hbm, grads_hbm, gate_hbm, up_hbm, hid_hbm, weights_hbm,
        grad_ref, mid_rows_ref, feed_ref, sum_a, sum_b, out_hbm,
        own, rows_ref, grads_ref, gate_ref, up_ref, hid_ref, weights_ref, out_ref, *rest,
    ):
        (outgoing, mine, land, far, gone), room, (out_sems, in_sems) = rest[:5], rest[5:10], rest[10:]
        spot, post = Spot(), Post(out_sems, in_sems)
        loads = load(
            post,
            [(gate_hbm, gate_ref), (up_hbm, up_ref), (weights_hbm, weights_ref)]
            + [(rows_hbm, rows_ref), (hid_hbm, hid_ref), (grads_hbm, grads_ref)],
        )
        greet(spot, row_peers(spot) + y_peers(spot), 5, **collect_peers(spot))

        def main():
            for copy in loads[:3]:
                copy.wait()
            terms = [(ref, weights_ref, slice(i * PACK, (i + 1) * PACK)) for i, ref in enumerate((gate_ref, up_ref))]
            make = row_products(spot, terms, outgoing, mine)
            yield from scatter_rows(spot, post, make, outgoing, mine, land, far, gone)
            feed_ref[...] = jnp.zeros_like(feed_ref)

            def body(strip):
                upstream = row_sum(spot, mine, land, gone, strip)
                through, feed = norm_back(upstream, mid_ref[strip, :], wide_gain(gain_ref))
                grad = cot_ref[strip, :].astype(F32) + through
                grad_ref[strip, :] = grad
                own[strip, :] = grad.astype(BF16)
                feed_ref[...] += feed

            in_strips(ROWS, body)
            yield from gather_rows(spot, post, own, mid_rows_ref)

        def gradients():
            for copy in loads[3:]:
                copy.wait()
            groups = [(rows_ref, (gate_ref, up_ref)), (grads_ref, (hid_ref,))]
            yield from Gradients(spot, post, groups, *room, sum_a, sum_b).steps()

        def output():
            def step(i, carry):
                rows = pl.ds(pl.multiple_of(i * 256, 256), 256)
                out_ref[rows, :] = dot(hid_ref[rows, :], weights_ref[:, 2 * PACK :], 1, 1).astype(BF16)
                return carry

            lax.fori_loop(0, count // 256, step, 0)
            store = post.local(out_ref, out_hbm)
            store.start()
            yield
            store.wait()

        play("mggmgmgogmmgggggo", m=main(), g=gradients(), o=output())

    half = shape((4, 64, n), BF16)
    wide = pltpu.VMEM((count, WIDE), BF16)
    narrow = pltpu.VMEM((count, PACK), BF16)
    return moving(
        kernel,
        "turn",
        (
            shape((ROWS, WIDE), F32),
            shape((8, ROWS, WIDE), BF16),
            shape((1, WIDE), F32),
            half,
            half,
            shape((count, WIDE), BF16),
        ),
        (mid, gain, cotangent, rows, grads, d_gate, d_up, hidden, weights),
        [INSIDE, INSIDE, INSIDE] + [ANY] * 6,
        (INSIDE, ANY, INSIDE, INSIDE, INSIDE, ANY),
        [pltpu.VMEM((ROWS, WIDE), BF16), wide, wide, narrow, narrow, narrow, pltpu.VMEM((WIDE, n), BF16), wide]
        + scatter_scratch()
        + gradient_scratch(n)
        + sems(100),
        3,
    )


def leave(weights, tokens, gain, grad_mid, feed_part, rows, d_qkv, mid_rows, mixed, sum_two):
    n_qkv, n_out = d_qkv.shape[1], mixed.shape[1]
    n, n_two = n_qkv + n_out, sum_two.shape[-1]
    count = 8 * ROWS

    def kernel(
        weights_hbm, tokens_ref, gain_ref, grad_ref, feed_ref, rows_hbm, d_hbm, mid_hbm, mixed_hbm, sum_two_ref,
        token_ref, gains_ref, weight_ref, high_ref, norm_part, parts, from_y, over_y, from_chip, over_fsdp, from_tp,
        rows_ref, d_ref, mid_ref, mixed_ref, weights_ref, *rest,
    ):
        (outgoing, mine, land, far, gone), room, (sum_a, sum_b) = rest[:5], rest[5:10], rest[10:12]
        last, (out_sems, in_sems) = rest[12:18], rest[18:]
        spot, post = Spot(), Post(out_sems, in_sems)
        pairs = [(d_hbm, d_ref), (weights_hbm, weights_ref), (rows_hbm, rows_ref), (mixed_hbm, mixed_ref), (mid_hbm, mid_ref)]
        loads = load(post, pairs)
        greet(spot, row_peers(spot) + y_peers(spot) + gain_sources(spot), 5 + 13, **collect_peers(spot))

        def main():
            loads[1].wait()
            make = row_products(spot, [(d_ref, weights_ref, slice(None))], outgoing, mine)
            yield from scatter_rows(spot, post, make, outgoing, mine, land, far, gone)
            norm_part[...] = jnp.zeros_like(norm_part)

            def body(strip):
                upstream = row_sum(spot, mine, land, gone, strip)
                through, norm = norm_back(upstream, tokens_ref[strip, :].astype(F32), wide_gain(gain_ref))
                token_ref[strip, :] = grad_ref[strip, :] + through
                norm_part[...] += norm

            in_strips(ROWS, body)
            parts[...] = jnp.zeros_like(parts)
            for f in range(16):
                parts[f, 0:1, :] = norm_part[:, f * 128 : (f + 1) * 128]
                parts[f, 1:2, :] = feed_ref[:, f * 128 : (f + 1) * 128]
            yield from sum_gains(spot, post, parts, gains_ref, from_y, over_y, from_chip, over_fsdp, from_tp)

        def gradients():
            for copy in loads[:1] + loads[2:]:
                copy.wait()
            groups = [(rows_ref, (d_ref,)), (mid_ref, (mixed_ref,))]
            yield from Gradients(spot, post, groups, *room, sum_a, sum_b).steps()
            yield from together(
                scatter_low(spot, post, sum_a, strip_writer(weight_ref), *last[:2]),
                scatter_high(spot, post, sum_b, strip_writer(weight_ref, 64), *last[2:4]),
            )

        play(
            "bgmgbmgggmgggggmgmgmgbg",
            m=main(),
            g=gradients(),
            b=scatter_high(spot, post, sum_two_ref, strip_writer(high_ref), *last[4:]),
        )

    small = (8, 128)
    full_rows = pltpu.VMEM((count, WIDE), BF16)
    return moving(
        kernel,
        "leave",
        (shape((ROWS, WIDE), F32), shape(small, F32), shape((ROWS, n), F32), shape((64, n_two), F32)),
        (weights, tokens, gain, grad_mid, feed_part, rows, d_qkv, mid_rows, mixed, sum_two),
        [ANY, INSIDE, INSIDE, INSIDE, INSIDE] + [ANY] * 4 + [INSIDE],
        (INSIDE,) * 4,
        [pltpu.VMEM((1, WIDE), F32), pltpu.VMEM((16,) + small, F32)]
        + [pltpu.VMEM(dims + small, F32) for dims in ((3, 4), (4,), (3,), (), (7,))]
        + [full_rows, pltpu.VMEM((count, n_qkv), BF16), full_rows, pltpu.VMEM((count, n_out), BF16)]
        + [pltpu.VMEM(weights.shape, BF16)]
        + scatter_scratch()
        + gradient_scratch(n)
        + [pltpu.VMEM((4, 64, n), BF16)] * 2
        + low_scratch(n)
        + high_scratch(n)
        + high_scratch(n_two)
        + sems(120),
        4,
    )


def dot(a, b, da=1, db=0):
    return lax.dot_general(a, b, (((da,), (db,)), ((), ())), preferred_element_type=F32)


def plain(kernel, name, grid, inputs, in_specs, outs, out_specs, scratch=()):
    return pl.pallas_call(
        kernel,
        name=name,
        out_shape=outs,
        grid=grid,
        in_specs=in_specs,
        out_specs=out_specs,
        scratch_shapes=list(scratch),
        compiler_params=pltpu.CompilerParams(vmem_limit_bytes=VMEM),
    )(*inputs)


def by_rows(n, width, column=0):
    return pl.BlockSpec((n, width), lambda i: (i, column))


def whole(dims, *index):
    at = index or (0,) * len(dims)
    return pl.BlockSpec(dims, lambda i: at)


def project(rows, weights, cosine, sine):
    step = 512

    def kernel(rows_ref, w_ref, cos_ref, sin_ref, q_ref, kv_ref):
        out = dot(rows_ref[...], w_ref[...])
        cos, sin = cos_ref[...], sin_ref[...]
        for head in range(4):
            u = out[:, head * HD : (head + 1) * HD]
            turned = (u * cos + pltpu.roll(u, HD // 2, 1) * sin).astype(BF16)
            if head < 2:
                q_ref[:, head * HD : (head + 1) * HD] = turned
            else:
                kv_ref[head - 2, 0] = turned
                kv_ref[head - 2, 1] = out[:, (head + 2) * HD : (head + 3) * HD].astype(BF16)

    out = shape((8 * ROWS, 2 * HD), BF16)
    return plain(
        kernel,
        "project",
        (8 * ROWS // step,),
        (rows, weights, cosine, sine),
        [by_rows(step, WIDE), whole((WIDE, PACK)), by_rows(step, HD), by_rows(step, HD)],
        (out, shape((2, 2, 8 * ROWS, HD), BF16)),
        (by_rows(step, 2 * HD), pl.BlockSpec((2, 2, step, HD), lambda i: (0, 0, i, 0))),
    )


def feed_forward(rows, grads, weights):
    step = 256

    def kernel(rows_ref, grads_ref, g_ref, u_ref, d_ref, hid_ref, dgate_ref, dup_ref):
        gate = dot(rows_ref[...], g_ref[...])
        up = dot(rows_ref[...], u_ref[...])
        d_hid = dot(grads_ref[...], d_ref[...])
        sigma = 1.0 / (1.0 + jnp.exp(-gate))
        silu = gate * sigma
        hid_ref[...] = (silu * up).astype(BF16)
        dup_ref[...] = (d_hid * silu).astype(BF16)
        dgate_ref[...] = (d_hid * up * sigma * (1.0 + gate * (1.0 - sigma))).astype(BF16)

    out = shape((8 * ROWS, PACK), BF16)
    return plain(
        kernel,
        "feed_forward",
        (8 * ROWS // step,),
        (rows, grads, weights, weights, weights),
        [by_rows(step, WIDE)] * 2 + [whole((WIDE, PACK), 0, i) for i in range(3)],
        (out,) * 3,
        (by_rows(step, PACK),) * 3,
    )


def settle(layer, token_grad, gains, attention, low, high, wide):
    def kernel(
        layer_ref, token_ref, gains_ref, attention_ref, low_ref, high_ref,
        layer_out, token_out, norm_out, feed_out, query_out, key_out, value_out, out_out, gate_out, up_out, down_out,
    ):
        layer_out[...] = layer_ref[...]
        token_out[...] = token_ref[...]
        norm_out[...] = gains_ref[0:1, :]
        feed_out[...] = gains_ref[1:2, :]
        for i, out in enumerate((query_out, key_out, value_out)):
            out[...] = attention_ref[:, i * 2 * HD : (i + 1) * 2 * HD]
        out_out[...] = attention_ref[:, PACK:].T
        for i, out in enumerate((gate_out, up_out, down_out)):
            columns = slice(i * PACK, (i + 1) * PACK)
            out[...] = jnp.concatenate([low_ref[:, columns], high_ref[:, columns]], 0).T[:wide]

    vector = shape((1, 128), F32)
    square = shape((ROWS, 2 * HD), F32)
    tall = shape((wide, ROWS), F32)
    return pl.pallas_call(
        kernel,
        name="settle",
        out_shape=(shape(layer.shape, layer.dtype), shape(token_grad.shape, F32), vector, vector, square, square, square)
        + (shape((2 * HD, ROWS), F32), tall, tall, tall),
        in_specs=[INSIDE] * 6,
        out_specs=(INSIDE,) * 11,
        compiler_params=pltpu.CompilerParams(vmem_limit_bytes=VMEM),
    )(layer, token_grad, gains, attention, low, high)


TILE = 256
CHUNK = 512


def place_of(start, count, xh, axis):
    dims = (count, 1) if axis == 0 else (1, count)
    j = lax.broadcasted_iota(jnp.int32, dims, axis)
    return 2 * (j + start) - lax.rem(j + start, ROWS) + xh * ROWS


SPANS = ((0, 512, False), (512, 256, True))
LAST = (768, 256, True)


def scores_of(keys, q, span, q_pos, prefix, xh):
    start, count, masked = span
    scores = dot(keys, q, 1, 1) * (SCALE * LOG2E)
    if masked:
        k_pos = place_of(start, count, xh, 0)
        scores = jnp.where(jnp.logical_or(k_pos <= q_pos, k_pos < prefix), scores, -1e30)
    return scores


def tile_at(i):
    head, tile = lax.div(i, 4), lax.rem(i, 4)
    return head, tile, pl.ds(pl.multiple_of(head * HD, HD), HD), pl.ds(pl.multiple_of(tile * TILE, TILE), TILE)


def exchange(post, pairs, device):
    copies = [post.copy(src, dst, device) for src, dst in pairs]
    for copy in copies:
        copy.start()
    yield
    for copy in copies:
        copy.wait_recv()
        yield
    for copy in copies:
        copy.wait_send()


def prefix_of(prefixes_ref):
    return prefixes_ref[lax.div(lax.axis_index("fsdp"), 2)]


def attend(prefixes, queries, here, cotangent, row_out, second):
    n, n_two = row_out.shape[-1], second.shape[-1]

    def kernel(
        prefixes_ref, q_ref, here_ref, cot_ref, row_ref, second_ref, o_ref, lse_ref, there_ref, grads_ref, out_ref, stage_ref,
        top_ref, sum_ref, acc_ref, out_sems, in_sems,
    ):
        prefix = prefix_of(prefixes_ref)
        spot, post = Spot(), Post(out_sems, in_sems)
        partner = spot.at(dx=2)
        greet(spot, row_peers(spot) + y_peers(spot) + [partner], 6)

        def sweep(side, begin, end):
            keys_ref = there_ref if side else here_ref
            xh = 1 - spot.xh if side else spot.xh

            def step(i, carry):
                head, tile, cols, rows = tile_at(i)
                q = q_ref[rows, cols]
                q_pos = place_of(tile * TILE, TILE, spot.xh, 1)
                one = pl.ds(i, 1)

                def chunk(span, first):
                    keys = pl.ds(span[0], span[1])
                    scores = scores_of(keys_ref[head, 0, keys, :], q, span, q_pos, prefix, xh)
                    top = jnp.max(scores, 0, keepdims=True)
                    if not first:
                        before = top_ref[one, :]
                        top = jnp.maximum(top, before)
                    raised = jnp.exp2(scores - top)
                    total = jnp.sum(raised, 0, keepdims=True)
                    mixed = dot(keys_ref[head, 1, keys, :], raised.astype(BF16), 0, 0)
                    if not first:
                        fade = jnp.exp2(before - top)
                        total = total + sum_ref[one, :] * fade
                        mixed = mixed + acc_ref[i] * fade
                    top_ref[one, :] = top
                    sum_ref[one, :] = total
                    acc_ref[i] = mixed

                for number, span in enumerate(SPANS):
                    chunk(span, side == 0 and number == 0)

                @pl.when(tile == 3)
                def _():
                    chunk(LAST, False)

                if side == 1:
                    total = sum_ref[one, :]
                    o_ref[rows, cols] = (acc_ref[i] / total).T.astype(BF16)
                    lse_ref[one, :] = top_ref[one, :] + jnp.log2(total)
                return carry

            lax.fori_loop(begin, end, step, 0)

        def compute():
            sweep(0, 0, 8)
            yield
            sweep(1, 0, 4)
            yield
            sweep(1, 4, 8)

        play(
            "vesfcvsfecvsfecse",
            v=y_gather(spot, post, row_ref, lambda y: out_ref.at[y]),
            f=y_gather(spot, post, second_ref, lambda y: stage_ref.at[y]),
            e=exchange(post, [(here_ref.at[head], there_ref.at[head]) for head in range(2)], partner),
            s=gather_rows(spot, post, cot_ref, grads_ref),
            c=compute(),
        )

    return moving(
        kernel,
        "attend",
        (
            shape((8 * ROWS, 2 * HD), BF16),
            shape((8, TILE), F32),
            shape(here.shape, BF16),
            shape((8, ROWS, WIDE), BF16),
            shape((4, 4, ROWS, n), BF16),
            shape((4, 64, n_two), BF16),
        ),
        (prefixes, queries, here, cotangent, row_out, second),
        [pl.BlockSpec(memory_space=pltpu.SMEM)] + [INSIDE] * 5,
        (INSIDE, INSIDE, INSIDE, ANY, ANY, INSIDE),
        [pltpu.VMEM((8, TILE), F32), pltpu.VMEM((8, TILE), F32), pltpu.VMEM((8, HD, TILE), F32)] + sems(60),
        5,
    )


def attend_back(prefixes, queries, here, there, rows, weights, mixed, lse, cosine, sine, out_part, mid, sum_a):
    n = sum_a.shape[-1]

    def kernel(
        prefixes_ref, rows_hbm, weights_hbm, q_ref, here_ref, there_ref, o_ref, lse_ref, cos_ref, sin_ref, part_ref, mid_ref,
        sum_a_ref, d_ref, layer_ref, weight_ref, rows_ref, weights_ref, g_ref, delta_ref, dq_ref, acc_ref, near_ref, away_ref, land_ref, *rest,
    ):
        (outgoing, mine, land, far, gone), last, (out_sems, in_sems) = rest[:5], rest[5:7], rest[7:]
        prefix = prefix_of(prefixes_ref)
        spot, post = Spot(), Post(out_sems, in_sems)
        loads = load(post, [(weights_hbm, weights_ref), (rows_hbm, rows_ref)])
        partner = spot.at(dx=2)
        greet(spot, row_peers(spot) + y_peers(spot) + [partner], 6)

        def sweep(head, side, keys_ref, into):
            xh = spot.xh if side == 0 else 1 - spot.xh
            cols = pl.ds(head * HD, HD)
            into[...] = jnp.zeros_like(into)

            def step(tile, carry):
                i = head * 4 + tile
                rows = pl.ds(pl.multiple_of(tile * TILE, TILE), TILE)
                q, g = q_ref[rows, cols], g_ref[rows, cols]
                q_pos = place_of(tile * TILE, TILE, spot.xh, 1)
                if side == 1:
                    product = g.astype(F32) * o_ref[rows, cols].astype(F32)
                    delta_ref[pl.ds(i, 1), :] = jnp.sum(product.T, 0, keepdims=True)
                level, offset = lse_ref[pl.ds(i, 1), :], delta_ref[pl.ds(i, 1), :]

                def chunk(span, first):
                    span_rows = pl.ds(span[0], span[1])
                    keys = keys_ref[head, 0, span_rows, :]
                    probs = jnp.exp2(scores_of(keys, q, span, q_pos, prefix, xh) - level)
                    d_probs = dot(keys_ref[head, 1, span_rows, :], g, 1, 1)
                    d_scores = (probs * (d_probs - offset)).astype(BF16)
                    into[0, span_rows, :] += dot(d_scores, q)
                    into[1, span_rows, :] += dot(probs.astype(BF16), g)
                    d_query = dot(d_scores, keys, 0, 0)
                    dq_ref[i] = d_query if first else dq_ref[i] + d_query

                for number, span in enumerate(SPANS):
                    chunk(span, side == 1 and number == 0)

                @pl.when(tile == 3)
                def _():
                    chunk(LAST, False)

                if side == 0:
                    u = dq_ref[i] * SCALE
                    d_ref[rows, cols] = (u * cos_ref[rows, :] - pltpu.roll(u, HD // 2, 1) * sin_ref[rows, :]).astype(BF16)
                return carry

            lax.fori_loop(0, 4, step, 0)

        def compute():
            for copy in loads:
                copy.wait()

            def heads(i, carry):
                span = pl.ds(pl.multiple_of(i * 256, 256), 256)
                g_ref[span, :] = dot(rows_ref[span, :], weights_ref[...]).astype(BF16)
                return carry

            lax.fori_loop(0, 4, heads, 0)
            copies = []
            for head in range(2):
                sweep(head, 1, there_ref, acc_ref)
                away_ref[head] = acc_ref[...].astype(BF16)
                copies.append(post.copy(away_ref.at[head], land_ref.at[head], partner))
                copies[-1].start()
                yield
            for head in range(2):
                sweep(head, 0, here_ref, near_ref.at[head])
                yield
            for head in range(2):
                copies[head].wait_recv()
                cols = pl.ds(2 * HD + head * HD, HD)

                def finish(i, carry, head=head):
                    rows = pl.ds(pl.multiple_of(i * 128, 128), 128)
                    u = (near_ref[head, 0, rows, :] + land_ref[head, 0, rows, :].astype(F32)) * SCALE
                    back = u * cos_ref[rows, :] - pltpu.roll(u, HD // 2, 1) * sin_ref[rows, :]
                    d_ref[rows, pl.ds(2 * HD + head * HD, HD)] = back.astype(BF16)
                    v = near_ref[head, 1, rows, :] + land_ref[head, 1, rows, :].astype(F32)
                    d_ref[rows, pl.ds(4 * HD + head * HD, HD)] = v.astype(BF16)
                    return carry

                lax.fori_loop(0, 8, finish, 0)
            for copy in copies:
                copy.wait_send()

        make = row_loads(spot, post, part_ref, outgoing, mine)

        def output():
            yield from scatter_rows(spot, post, make, outgoing, mine, land, far, gone, True)

            def body(strip):
                layer_ref[strip, :] = (mid_ref[strip, :] + row_sum(spot, mine, land, gone, strip)).astype(BF16)

            in_strips(ROWS, body)

        play(
            "wcococwcoow",
            c=compute(),
            o=output(),
            w=scatter_low(spot, post, sum_a_ref, strip_writer(weight_ref), *last),
        )

    pair = (2, 8 * ROWS, HD)
    return moving(
        kernel,
        "attend_back",
        (shape((8 * ROWS, PACK), BF16), shape((ROWS, WIDE), BF16), shape((64, n), F32)),
        (prefixes, rows, weights, queries, here, there, mixed, lse, cosine, sine, out_part, mid, sum_a),
        [pl.BlockSpec(memory_space=pltpu.SMEM), ANY, ANY] + [INSIDE] * 7 + [ANY, INSIDE, INSIDE],
        (INSIDE,) * 3,
        [
            pltpu.VMEM(rows.shape, BF16),
            pltpu.VMEM(weights.shape, BF16),
            pltpu.VMEM((8 * ROWS, 2 * HD), BF16),
            pltpu.VMEM((8, TILE), F32),
            pltpu.VMEM((8, TILE, HD), F32),
            pltpu.VMEM(pair, F32),
            pltpu.VMEM((2,) + pair, F32),
            pltpu.VMEM((2,) + pair, BF16),
            pltpu.VMEM((2,) + pair, BF16),
        ]
        + scatter_scratch()
        + low_scratch(n)
        + sems(64),
        6,
    )


def on_device(
    tokens,
    prefixes,
    norm_gain,
    query_weight,
    key_weight,
    value_weight,
    output_weight,
    feed_gain,
    gate_weight,
    up_weight,
    down_weight,
    cotangent,
):
    rows_one, full_one, row_out, row_two, second, cosine, sine = enter(
        tokens, norm_gain, query_weight, key_weight, value_weight, output_weight, gate_weight.T, up_weight.T, down_weight
    )
    rows_one = rows_one.reshape(-1, WIDE)
    full_one = full_one.reshape(WIDE, -1)
    queries, here = project(rows_one, full_one, cosine, sine)
    attended, lse, there, grad_rows, full_out, stage_two = attend(prefixes, queries, here, cotangent, row_out, second)
    full_out = full_out.reshape(WIDE, -1)
    mid, rows_two, full_two = middle(attended, full_out, tokens, feed_gain, row_two, stage_two)
    rows_two, grad_rows, full_two = (a.reshape(-1, a.shape[-1]) for a in (rows_two, grad_rows, full_two.reshape(WIDE, -1)))
    hidden, d_gate, d_up = feed_forward(rows_two, grad_rows, full_two)
    grad_mid, mid_rows, feed_part, sum_a, sum_b, part_out = turn(
        mid, feed_gain, cotangent, rows_two, grad_rows, d_gate, d_up, hidden, full_two
    )
    mid_rows = mid_rows.reshape(-1, WIDE)
    d_qkv, layer_output, low = attend_back(
        prefixes, queries, here, there, mid_rows, full_out, attended, lse, cosine, sine, part_out.reshape(8, ROWS, WIDE), mid, sum_a
    )
    token_grad, gains, attention, high = leave(
        full_one, tokens, norm_gain, grad_mid, feed_part, rows_one, d_qkv, mid_rows, attended, sum_b
    )
    layer_output, token_grad, norm_grad, feed_grad, *grads = settle(
        layer_output, token_grad, gains, attention, low, high, gate_weight.shape[1]
    )
    query_grad, key_grad, value_grad, output_grad, gate_grad, up_grad, down_grad = grads
    return (
        layer_output,
        token_grad,
        norm_grad[0],
        query_grad,
        key_grad,
        value_grad,
        output_grad,
        feed_grad[0],
        gate_grad.T,
        up_grad.T,
        down_grad,
    )


def solution(mesh):
    rows = P(("fsdp", "tp"), None)
    wide = P("fsdp", "tp")
    tall = P("tp", "fsdp")
    return jax.shard_map(
        on_device,
        mesh=mesh,
        in_specs=(rows, P(), P(), wide, wide, wide, tall, P(), wide, wide, tall, rows),
        out_specs=(rows, rows, P("fsdp"), wide, wide, wide, tall, P("fsdp"), wide, wide, tall),
        check_vma=False,
    )
```

```python
import functools
import math

import jax
import jax.numpy as jnp
from jax import lax
from jax.experimental import pallas as pl
from jax.experimental.pallas import tpu as pltpu
from jax.sharding import PartitionSpec as P

HD = 128
EPS = 1e-05
ROPE_BASE = 10000.0
F32 = jnp.float32
BF16 = jnp.bfloat16
MESH = pl.DeviceIdType.MESH
AXES = ("fsdp", "tp")
ROWS = 128
WIDE = 2048
PACK = 768
SCALE = 1.0 / math.sqrt(HD)
LOG2E = 1.4426950408889634
VMEM = 60 << 20


class Spot:
    def __init__(self):
        f, t = lax.axis_index("fsdp"), lax.axis_index("tp")
        self.y, self.xl, self.c = lax.div(f, 4), lax.rem(lax.div(f, 2), 2), lax.rem(f, 2)
        self.z, self.xh = lax.div(t, 2), lax.rem(t, 2)
        self.x = self.xh * 2 + self.xl
        self.own = self.xl * 2 + self.c
        self.away = lax.rem(self.xh + self.c, 2)
        self.home = self.away == 0
        self.turn = 1 - lax.rem(self.away + self.xl, 2)
        self.ahead = 1 + 2 * self.turn
        self.back = 3 - 2 * self.turn
        self.near = (1 - self.xl) * 2
        self.same = self.xl * 2

    def at(self, dy=0, dx=0, dz=0, core=None):
        y, z, x = lax.rem(self.y + dy, 4), lax.rem(self.z + dz, 4), lax.rem(self.x + dx, 4)
        return (y * 4 + lax.rem(x, 2) * 2 + (self.c if core is None else core), z * 2 + lax.div(x, 2))

    def other(self):
        return self.at(core=1 - self.c)

    def seat(self, slot):
        return (self.y * 4 + slot, self.z * 2 + self.c)

    def bench(self, slot):
        return (self.y * 4 + slot, self.z * 2 + self.xh)

    def block(self, dz=0, flip=False):
        return (1 - self.c if flip else self.c) * 4 + lax.rem(self.z + dz, 4)


class Post:
    def __init__(self, out_sems, in_sems):
        self.out_sems, self.in_sems, self.n_out, self.n_in = out_sems, in_sems, 0, 0

    def slots(self, n):
        base = self.n_in
        self.n_in += n
        return base

    def copy(self, src, dst, device, slot=None):
        slot = self.slots(1) if slot is None else slot
        self.n_out += 1
        return pltpu.make_async_remote_copy(
            src_ref=src,
            dst_ref=dst,
            send_sem=self.out_sems.at[self.n_out - 1],
            recv_sem=self.in_sems.at[slot],
            device_id=device,
            device_id_type=MESH,
        )

    def arrival(self, dst, device, slot):
        return pltpu.make_async_remote_copy(
            src_ref=dst,
            dst_ref=dst,
            send_sem=self.out_sems.at[0],
            recv_sem=self.in_sems.at[slot],
            device_id=device,
            device_id_type=MESH,
        )

    def local(self, src, dst):
        self.n_out += 1
        return pltpu.make_async_copy(src, dst, self.out_sems.at[self.n_out - 1])


def greet(spot, sources, count, home=(), away=()):
    barrier = pltpu.get_barrier_semaphore()

    def signal(devices):
        for device in devices:
            pl.semaphore_signal(barrier, inc=1, device_id=device, device_id_type=MESH)

    signal(sources)
    if home:
        count = count + 3 + spot.away

        @pl.when(spot.home)
        def _():
            signal(home)

        @pl.when(jnp.logical_not(spot.home))
        def _():
            signal(away)

    pl.semaphore_wait(barrier, count)


def row_peers(spot):
    return [spot.at(dz=1), spot.at(dz=3), spot.other()]


def y_peers(spot):
    return [spot.at(dy=1), spot.at(dy=3)]


def gather_peers(spot):
    near = [spot.at(dx=spot.back, core=0), spot.at(dx=spot.back, core=1)]
    return {"home": near + [spot.other()], "away": near + [spot.at(dx=1), spot.at(dx=3)]}


def collect_peers(spot):
    usual = [spot.at(dx=1, core=spot.xh), spot.at(dx=3, core=spot.xh), spot.at(dx=spot.ahead)]
    return {"home": usual, "away": usual + [spot.other()]}


def half_of(ref, number):
    rows = ref.shape[0] // 2
    return ref.at[pl.ds(number * rows, rows)]


def after(spot, k):
    return lax.rem(spot.own + k, 4)


def play(order, **jobs):
    for letter in order:
        next(jobs[letter], None)
    for job in jobs.values():
        for _ in job:
            pass


def gather_rows(spot, post, own, rows):
    up, down, core = spot.at(dz=1), spot.at(dz=3), spot.other()
    half = ROWS // 2
    low, high = pl.ds(0, half), pl.ds(half, half)
    here, below, above, far = (spot.block(dz) for dz in (0, 3, 1, 2))
    a = post.copy(own, rows.at[here], up)
    b = post.copy(own, rows.at[here], down)
    k0 = post.copy(own, rows.at[here], core)
    keep = post.local(own, rows.at[here])
    for copy in (a, b, k0, keep):
        copy.start()
    yield
    a.wait_recv()
    fa = post.copy(rows.at[below, low], rows.at[below, low], up)
    k1 = post.copy(rows.at[below], rows.at[below], core)
    fa.start()
    k1.start()
    b.wait_recv()
    fb = post.copy(rows.at[above, high], rows.at[above, high], down)
    k2 = post.copy(rows.at[above], rows.at[above], core)
    fb.start()
    k2.start()
    yield
    fa.wait_recv()
    fb.wait_recv()
    k3 = post.copy(rows.at[far], rows.at[far], core)
    k3.start()
    yield
    keep.wait()
    for copy in (k0, k1, k2, k3):
        copy.wait_recv()
    for copy in (a, b, fa, fb, k0, k1, k2, k3):
        copy.wait_send()


def in_strips(count, body):
    def step(i, carry):
        body(pl.ds(pl.multiple_of(i * 16, 16), 16))
        return carry

    lax.fori_loop(0, count // 16, step, 0)


def add_into(target, other, rows=ROWS, start=0):
    def body(strip):
        strip = pl.ds(pl.multiple_of(strip.start + start, 16), 16)
        target[strip, :] = (target[strip, :].astype(F32) + other[strip, :].astype(F32)).astype(BF16)

    in_strips(rows, body)


def row_products(spot, terms, outgoing, mine):
    def make(k, z):
        other, own = pl.ds(((1 - spot.c) * 4 + z) * ROWS, ROWS), pl.ds((spot.c * 4 + z) * ROWS, ROWS)

        def step(i, carry):
            columns = pl.ds(pl.multiple_of(i * 512, 512), 512)
            total = None
            for a, w, part in terms:
                term = dot(jnp.concatenate([a[other, :], a[own, :]], 0), w[columns, part], 1, 1)
                total = term if total is None else total + term
            outgoing[z, :, columns] = total[:ROWS].astype(BF16)
            mine[z, :, columns] = total[ROWS:].astype(BF16)
            return carry

        lax.fori_loop(0, WIDE // 512, step, 0)

    return make


def row_loads(spot, post, part, outgoing, mine):
    copies = []
    for z in row_order(spot):
        pairs = [(part.at[(1 - spot.c) * 4 + z], outgoing.at[z]), (part.at[spot.c * 4 + z], mine.at[z])]
        copies.append(load(post, pairs))

    def make(k, z):
        for copy in copies[k]:
            copy.wait()

    return make


def row_order(spot):
    return [lax.rem(spot.z + dz, 4) for dz in (2, 3, 1, 0)]


def scatter_rows(spot, post, make, outgoing, mine, land, far, gone, ahead=False):
    up, down, core = spot.at(dz=1), spot.at(dz=3), spot.other()
    half = ROWS // 2
    low, high = pl.ds(0, half), pl.ds(half, half)
    steps = row_order(spot)
    distant, lower, upper, here = steps
    to_core, others = [], []

    def begin(k):
        if len(to_core) > k:
            return
        make(k, steps[k])
        to_core.append(post.copy(outgoing.at[steps[k]], land.at[steps[k]], core))
        to_core[k].start()

    def pass_on(src, dst, device):
        others.append(post.copy(src, dst, device))
        others[-1].start()
        return others[-1]

    def ready(k):
        to_core[k].wait_recv()
        if k < 3:
            add_into(mine.at[steps[k]], land.at[steps[k]])

    if ahead:
        for k in range(4):
            begin(k)
        yield
    begin(0)
    begin(1)
    ready(0)
    f_low = pass_on(mine.at[distant, low], far.at[low], down)
    f_high = pass_on(mine.at[distant, high], far.at[high], up)
    begin(2)
    ready(1)
    gone_copies = [pass_on(mine.at[lower, high], gone.at[0, high], down)]
    begin(3)
    ready(2)
    gone_copies.append(pass_on(mine.at[upper, low], gone.at[1, low], up))
    yield
    ready(3)
    f_low.wait_recv()
    add_into(mine.at[lower], far, half)
    gone_copies.append(pass_on(mine.at[lower, low], gone.at[0, low], down))
    f_high.wait_recv()
    add_into(mine.at[upper], far, half, half)
    gone_copies.append(pass_on(mine.at[upper, high], gone.at[1, high], up))
    yield
    for copy in gone_copies:
        copy.wait_recv()
    for copy in to_core + others:
        copy.wait_send()


def row_sum(spot, mine, land, gone, strip):
    parts = [mine[spot.z, strip, :], land[spot.z, strip, :], gone[0, strip, :], gone[1, strip, :]]
    return sum(part.astype(F32) for part in parts)


def scatter_scratch():
    block = (ROWS, WIDE)
    return [
        pltpu.VMEM((4,) + block, BF16),
        pltpu.VMEM((4,) + block, BF16),
        pltpu.VMEM((4,) + block, BF16),
        pltpu.VMEM(block, BF16),
        pltpu.VMEM((2,) + block, BF16),
    ]


def x_gather(spot, post, src, dst_at):
    base, far = post.slots(4), post.slots(4)
    sends = [post.copy(src, dst_at(spot.own), spot.at(dx=dx, core=spot.xh), base + spot.own) for dx in (1, 3)]
    cross = post.copy(src, dst_at(spot.own), spot.other(), base + spot.own)
    keep = post.local(src, dst_at(spot.own))
    for copy in sends:
        copy.start()

    @pl.when(spot.home)
    def _():
        keep.start()

    @pl.when(jnp.logical_not(spot.home))
    def _():
        cross.start()

    def landed(dst, slot):
        post.arrival(dst, spot.at(dx=1), slot).wait_recv()

    yield
    for core in range(2):
        block = dst_at(spot.near + core)
        landed(block, base + spot.near + core)
        part = half_of(block, spot.turn)
        sends.append(post.copy(part, part, spot.at(dx=spot.ahead), far + 2 * core + spot.turn))
        sends[-1].start()
    yield

    @pl.when(spot.home)
    def _():
        slot = spot.same + 1 - spot.c
        landed(dst_at(slot), base + slot)
        keep.wait()

    @pl.when(jnp.logical_not(spot.home))
    def _():
        for core in range(2):
            for number in range(2):
                landed(half_of(dst_at(spot.same + core), number), far + 2 * core + number)
        cross.wait_send()

    for copy in sends:
        copy.wait_send()


def y_gather(spot, post, src, dst_at):
    up, down = spot.at(dy=1), spot.at(dy=3)
    here, below, above = dst_at(spot.y), dst_at(lax.rem(spot.y + 3, 4)), dst_at(lax.rem(spot.y + 1, 4))
    a, b, keep = post.copy(src, here, up), post.copy(src, here, down), post.local(src, here)
    for copy in (a, b, keep):
        copy.start()
    yield
    a.wait_recv()
    fa = post.copy(half_of(below, 0), half_of(below, 0), up)
    fa.start()
    b.wait_recv()
    fb = post.copy(half_of(above, 1), half_of(above, 1), down)
    fb.start()
    yield
    keep.wait()
    for copy in (fa, fb):
        copy.wait_recv()
    for copy in (a, b, fa, fb):
        copy.wait_send()


def together(*jobs):
    live = list(jobs)
    while live:
        live = [job for job in live if next(job, job) is not job]
        if live:
            yield


def gather_first(spot, post, shard, row, stage):
    return together(
        x_gather(spot, post, shard.at[0], lambda slot: row.at[slot]),
        y_gather(spot, post, shard.at[1], lambda y: stage.at[y]),
    )


def gather_second(spot, post, row, stage, full):
    return together(
        x_gather(spot, post, stage, lambda slot: full.at[:, slot, 1]),
        y_gather(spot, post, row, lambda y: full.at[y, :, 0]),
    )


def sum_parts(parts, write):
    def body(strip):
        write(strip, sum(part[strip, :].astype(F32) for part in parts))

    in_strips(parts[0].shape[0], body)


def add_block(target, other):
    if len(target.shape) == 2:
        add_into(target, other, target.shape[0])
    else:

        def step(i, carry):
            add_into(target.at[i], other.at[i], target.shape[1])
            return carry

        lax.fori_loop(0, target.shape[0], step, 0)


class XCollect:
    def __init__(self, spot, post, src_at, land, hop):
        self.spot, self.post, self.src_at, self.land, self.hop = spot, post, src_at, land, hop
        self.in_land, self.in_hop = post.slots(5), post.slots(2)
        self.sends = []

    def to_near(self, core, src, number):
        spot = self.spot
        copy = self.post.copy(
            src,
            half_of(self.land.at[spot.turn], number),
            spot.seat(spot.near + core),
            self.in_land + 2 * spot.turn + number,
        )
        copy.start()
        self.sends.append(copy)

    def start(self):
        spot, post = self.spot, self.post
        cross_slot = spot.same + 1 - spot.c
        self.cross = post.copy(self.src_at(cross_slot), self.land.at[2], spot.other(), self.in_land + 4)
        self.keep = post.local(self.src_at(spot.own), self.land.at[2])
        self.far = []
        for core in range(2):
            for number, dx in ((0, 3), (1, 1)):
                src = half_of(self.src_at(spot.same + core), number)
                self.far.append(post.copy(src, self.hop.at[core], spot.at(dx=dx), self.in_hop + core))

        @pl.when(spot.home)
        def _():
            self.cross.start()
            self.keep.start()

        @pl.when(jnp.logical_not(spot.home))
        def _():
            for copy in self.far:
                copy.start()

        for core in range(2):
            self.to_near(core, half_of(self.src_at(spot.near + core), 1 - spot.turn), 1 - spot.turn)

    def relay(self):
        spot, post = self.spot, self.post
        for core in range(2):
            post.arrival(self.hop.at[core], spot.at(dx=1), self.in_hop + core).wait_recv()
            add_block(self.hop.at[core], half_of(self.src_at(spot.near + core), spot.turn))
            self.to_near(core, self.hop.at[core], spot.turn)

    def finish(self):
        spot, post = self.spot, self.post
        for side in range(2):
            for number in range(2):
                dst = half_of(self.land.at[side], number)
                post.arrival(dst, spot.at(dx=1), self.in_land + 2 * side + number).wait_recv()

        @pl.when(spot.home)
        def _():
            self.keep.wait()
            self.cross.wait_send()

        @pl.when(jnp.logical_not(spot.home))
        def _():
            post.arrival(self.land.at[2], spot.at(dx=1), self.in_land + 4).wait_recv()
            for copy in self.far:
                copy.wait_send()

        for copy in self.sends:
            copy.wait_send()

    def parts(self):
        return [self.land.at[side] for side in range(3)]


class YCollect:
    def __init__(self, spot, post, src_at, land, hop):
        self.spot, self.post, self.src_at, self.land, self.hop = spot, post, src_at, land, hop
        self.up, self.down = spot.at(dy=1), spot.at(dy=3)
        self.y = [lax.rem(spot.y + k, 4) for k in range(4)]

    def start_far(self):
        block = self.src_at(self.y[2])
        self.far = [
            self.post.copy(half_of(block, 0), self.hop.at[0], self.down),
            self.post.copy(half_of(block, 1), self.hop.at[1], self.up),
        ]
        for copy in self.far:
            copy.start()

    def start_lower(self):
        self.low = [self.post.copy(half_of(self.src_at(self.y[3]), 1), half_of(self.land.at[0], 1), self.down)]
        self.low[0].start()

    def start_upper(self):
        self.high = [self.post.copy(half_of(self.src_at(self.y[1]), 0), half_of(self.land.at[1], 0), self.up)]
        self.high[0].start()

    def relay(self):
        for number, k, target in ((0, 3, self.down), (1, 1, self.up)):
            self.far[number].wait_recv()
            hop = self.hop.at[number]
            add_block(hop, half_of(self.src_at(self.y[k]), number))
            copy = self.post.copy(hop, half_of(self.land.at[number], number), target)
            copy.start()
            (self.low if number == 0 else self.high).append(copy)

    def finish(self):
        for copy in self.low + self.high:
            copy.wait_recv()
        for copy in self.far + self.low + self.high:
            copy.wait_send()

    def parts(self):
        return [self.src_at(self.spot.y), self.land.at[0], self.land.at[1]]


class Gradients:
    def __init__(self, spot, post, groups, full, land_x, hop_x, land_y, hop_y, sum_a, sum_b):
        self.spot, self.groups, self.full, self.sum_a, self.sum_b = spot, groups, full, sum_a, sum_b
        self.y = [lax.rem(spot.y + k, 4) for k in (2, 3, 1, 0)]
        self.x = [
            XCollect(spot, post, lambda slot, y=y: full.at[y, slot, 0], land_x.at[j], hop_x.at[j])
            for j, y in enumerate(self.y)
        ]
        self.over_y = YCollect(spot, post, lambda y: full.at[y, :, 1], land_y, hop_y)

    def make(self, j):
        y = self.y[j]

        def part(s, carry):
            columns = pl.ds(pl.multiple_of(y * 512 + s * 256, 256), 256)
            at = 0
            for rows, values in self.groups:
                left = rows[:, columns]
                for value in values:
                    width = value.shape[1]
                    block = dot(left, value[...], 0, 0).astype(BF16)
                    for i in range(4):
                        self.full[y, 2 * s + i // 2, i % 2, :, at : at + width] = block[i * 64 : (i + 1) * 64]
                    at += width
            return carry

        lax.fori_loop(0, 2, part, 0)
        (self.over_y.start_far, self.over_y.start_lower, self.over_y.start_upper, lambda: None)[j]()
        self.x[j].start()

    def sum_x(self, j):
        def write(strip, total):
            self.sum_a[self.y[j], strip, :] = total.astype(BF16)

        self.x[j].finish()
        sum_parts(self.x[j].parts(), write)

    def sum_y(self):
        self.over_y.finish()

        def slot_sum(slot, carry):
            def write(strip, total):
                self.sum_b[slot, strip, :] = total.astype(BF16)

            sum_parts([part.at[slot] for part in self.over_y.parts()], write)
            return carry

        lax.fori_loop(0, 4, slot_sum, 0)

    def steps(self):
        self.make(0)
        yield
        self.make(1)
        yield
        self.make(2)
        self.x[0].relay()
        yield
        self.make(3)
        self.x[1].relay()
        yield
        self.over_y.relay()
        self.x[2].relay()
        yield
        self.x[3].relay()
        yield
        for j in range(4):
            self.sum_x(j)
            yield
        self.sum_y()


def load(post, pairs):
    copies = [post.local(src, dst) for src, dst in pairs]
    for copy in copies:
        copy.start()
    return copies


def gradient_scratch(n):
    return [
        pltpu.VMEM((4, 4, 2, 64, n), BF16),
        pltpu.VMEM((4, 3, 64, n), BF16),
        pltpu.VMEM((4, 2, 32, n), BF16),
        pltpu.VMEM((2, 4, 64, n), BF16),
        pltpu.VMEM((2, 2, 64, n), BF16),
    ]


def scatter_low(spot, post, sum_a, write, land, hop):
    over_y = YCollect(spot, post, lambda y: sum_a.at[y], land, hop)
    over_y.start_far()
    over_y.start_lower()
    over_y.start_upper()
    yield
    over_y.relay()
    yield
    over_y.finish()
    sum_parts(over_y.parts(), write)


def scatter_high(spot, post, sum_b, write, land, hop):
    over_x = XCollect(spot, post, lambda slot: sum_b.at[slot], land, hop)
    over_x.start()
    yield
    over_x.relay()
    yield
    over_x.finish()
    sum_parts(over_x.parts(), write)


def strip_writer(out, start=0):
    def write(strip, total):
        out[pl.ds(pl.multiple_of(strip.start + start, 16), 16), :] = total

    return write


def low_scratch(n):
    return [pltpu.VMEM((2, 64, n), BF16), pltpu.VMEM((2, 32, n), BF16)]


def high_scratch(n):
    return [pltpu.VMEM((3, 64, n), BF16), pltpu.VMEM((2, 32, n), BF16)]


def sum_gains(spot, post, parts, out, from_y, over_y, from_chip, over_fsdp, from_tp):
    y_copies = []
    for i, k in enumerate((2, 1, 3)):
        y = lax.rem(spot.y + k, 4)
        y_copies.append(post.copy(parts.at[pl.ds(y * 4, 4)], from_y.at[i], spot.at(dy=k)))
        y_copies[-1].start()
    yield
    for copy in y_copies:
        copy.wait_recv()
    over_y[...] = parts[pl.ds(spot.y * 4, 4)] + from_y[0] + from_y[1] + from_y[2]
    chip_copies = []
    for i, k in enumerate((1, 2, 3)):
        slot = after(spot, k)
        chip_copies.append(post.copy(over_y.at[slot], from_chip.at[i], spot.bench(slot)))
        chip_copies[-1].start()
    yield
    for copy in chip_copies:
        copy.wait_recv()
    over_fsdp[...] = over_y[spot.own] + from_chip[0] + from_chip[1] + from_chip[2]
    tp_copies = []
    for i, (dz, dx) in enumerate(TP_MOVES):
        tp_copies.append(post.copy(over_fsdp, from_tp.at[i], spot.at(dz=dz, dx=dx)))
        tp_copies[-1].start()
    yield
    for copy in tp_copies:
        copy.wait_recv()
    out[...] = over_fsdp[...] + sum(from_tp[i] for i in range(7))
    for copy in y_copies + chip_copies + tp_copies:
        copy.wait_send()


TP_MOVES = [(dz, dx) for dx in (0, 2) for dz in (0, 1, 2, 3) if (dz, dx) != (0, 0)]


def gain_sources(spot):
    return (
        [spot.at(dy=k) for k in (1, 2, 3)]
        + [spot.bench(after(spot, k)) for k in (1, 2, 3)]
        + [spot.at(dz=(4 - dz) % 4, dx=dx) for dz, dx in TP_MOVES]
    )


ANY = pl.BlockSpec(memory_space=pl.ANY)
INSIDE = pl.BlockSpec(memory_space=pltpu.VMEM)


def sems(n):
    return [pltpu.SemaphoreType.DMA((n,)), pltpu.SemaphoreType.DMA((n,))]


def moving(kernel, name, outs, inputs, in_specs, out_specs, scratch, cid):
    return pl.pallas_call(
        kernel,
        name=name,
        out_shape=outs,
        in_specs=in_specs,
        out_specs=out_specs,
        scratch_shapes=scratch,
        compiler_params=pltpu.CompilerParams(collective_id=cid, has_side_effects=True, vmem_limit_bytes=VMEM),
    )(*inputs)


def shape(dims, dtype):
    return jax.ShapeDtypeStruct(dims, dtype)


def normed(rows, gain):
    inverse = lax.rsqrt(jnp.mean(rows * rows, -1, keepdims=True) + EPS)
    scaled = rows * inverse
    return inverse, scaled, (scaled * gain).astype(BF16)


def enter(tokens, gain, query, key, value, out, gate, up, down):
    n_one, n_two, n_out = query.shape[1] * 3, PACK * 3, out.shape[0]

    def kernel(
        tokens_ref, gain_ref, query_ref, key_ref, value_ref, out_ref, gate_ref, up_ref, down_ref,
        rows_ref, full_ref, row_out_ref, row_ref, rest_ref, cos_ref, sin_ref,
        shard_one, row_one, stage_one, shard_out, shard_two, own, out_sems, in_sems,
    ):
        spot, post = Spot(), Post(out_sems, in_sems)
        for i in range(2):
            rows = pl.ds(i * 64, 64)
            for j, ref in enumerate((query_ref, key_ref, value_ref)):
                shard_one[i, :, j * 256 : (j + 1) * 256] = ref[rows, :]
        greet(spot, row_peers(spot) + y_peers(spot), 5, **gather_peers(spot))

        def weights():
            yield from gather_first(spot, post, shard_one, row_one, stage_one)
            yield from gather_second(spot, post, row_one, stage_one, full_ref)

        def tables():
            exponent = lax.broadcasted_iota(jnp.int32, (1, HD), 1)
            exponent = lax.rem(exponent, HD // 2).astype(F32)
            inverse = jnp.exp(exponent * (-2.0 / HD) * math.log(ROPE_BASE))
            sign = jnp.where(lax.broadcasted_iota(jnp.int32, (1, HD), 1) < HD // 2, -1.0, 1.0)

            def step(i, carry):
                angles = place_of(i * 16, 16, spot.xh, 0).astype(F32) * inverse
                strip = pl.ds(pl.multiple_of(i * 16, 16), 16)
                cos_ref[strip, :] = jnp.cos(angles)
                sin_ref[strip, :] = jnp.sin(angles) * sign
                return carry

            lax.fori_loop(0, 8 * ROWS // 16, step, 0)

        w = weights()
        next(w)

        def body(strip):
            own[strip, :] = normed(tokens_ref[strip, :].astype(F32), wide_gain(gain_ref))[2]

        in_strips(ROWS, body)
        r = gather_rows(spot, post, own, rows_ref)
        next(r)
        shard_out[...] = out_ref[...].astype(F32).T.astype(BF16)
        o = x_gather(spot, post, shard_out, lambda slot: row_out_ref.at[slot])
        next(o)
        shard_two[...] = jnp.zeros_like(shard_two)
        rest_ref[...] = jnp.zeros_like(rest_ref)
        wide = gate.shape[0]
        for j, ref in enumerate((gate_ref, up_ref, down_ref)):
            turned = ref[...].astype(F32).T.astype(BF16)
            shard_two[:, j * PACK : j * PACK + wide] = turned[:64]
            rest_ref[:, j * PACK : j * PACK + wide] = turned[64:]
        next(w)
        next(w)
        f = x_gather(spot, post, shard_two, lambda slot: row_ref.at[slot])
        next(f)
        next(o)
        next(r)
        tables()
        play("wfrwfor", r=r, w=w, f=f, o=o)

    half = pltpu.VMEM((4, 64, n_one), BF16)
    table = shape((8 * ROWS, HD), F32)
    return moving(
        kernel,
        "enter",
        (shape((8, ROWS, WIDE), BF16), shape((4, 4, 2, 64, n_one), BF16), shape((4, ROWS, n_out), BF16))
        + (shape((4, 64, n_two), BF16), shape((64, n_two), BF16), table, table),
        (tokens, gain, query, key, value, out, gate, up, down),
        [INSIDE] * 9,
        (ANY, ANY) + (INSIDE,) * 5,
        [pltpu.VMEM((2, 64, n_one), BF16), half, half, pltpu.VMEM((ROWS, n_out), BF16), pltpu.VMEM((64, n_two), BF16)]
        + [pltpu.VMEM((ROWS, WIDE), BF16)]
        + sems(60),
        1,
    )


def middle(mixed, weights, tokens, gain, row, stage):
    n = row.shape[-1]

    def kernel(
        mixed_hbm, weights_hbm, tokens_ref, gain_ref, row_ref, stage_ref, mid_ref, rows_ref, full_ref,
        mixed_ref, weights_ref, own, *rest,
    ):
        (outgoing, mine, land, far, gone), (out_sems, in_sems) = rest[:5], rest[5:]
        spot, post = Spot(), Post(out_sems, in_sems)
        loads = load(post, [(mixed_hbm, mixed_ref), (weights_hbm, weights_ref)])
        greet(spot, row_peers(spot) + y_peers(spot), 5, **gather_peers(spot))

        def main():
            for copy in loads:
                copy.wait()
            make = row_products(spot, [(mixed_ref, weights_ref, slice(None))], outgoing, mine)
            yield from scatter_rows(spot, post, make, outgoing, mine, land, far, gone)

            def body(strip):
                mid = tokens_ref[strip, :].astype(F32) + row_sum(spot, mine, land, gone, strip)
                mid_ref[strip, :] = mid
                own[strip, :] = normed(mid, wide_gain(gain_ref))[2]

            in_strips(ROWS, body)
            yield from gather_rows(spot, post, own, rows_ref)

        play("wmmmwmmm", m=main(), w=gather_second(spot, post, row_ref, stage_ref, full_ref))

    return moving(
        kernel,
        "middle",
        (shape((ROWS, WIDE), F32), shape((8, ROWS, WIDE), BF16), shape((4, 4, 2, 64, n), BF16)),
        (mixed, weights, tokens, gain, row, stage),
        [ANY, ANY, INSIDE, INSIDE, INSIDE, INSIDE],
        (INSIDE, ANY, ANY),
        [pltpu.VMEM(mixed.shape, BF16), pltpu.VMEM(weights.shape, BF16), pltpu.VMEM((ROWS, WIDE), BF16)]
        + scatter_scratch()
        + sems(64),
        2,
    )


def wide_gain(gain_ref):
    return gain_ref[...].astype(F32).reshape(1, WIDE)


def norm_back(upstream, rows, gain):
    inverse, scaled, _ = normed(rows, gain)
    weighted = upstream * gain
    through = inverse * (weighted - scaled * jnp.mean(weighted * scaled, -1, keepdims=True))
    return through, jnp.sum(upstream * scaled, 0, keepdims=True)


def turn(mid, gain, cotangent, rows, grads, d_gate, d_up, hidden, weights):
    n = 3 * PACK
    count = 8 * ROWS

    def kernel(
        mid_ref, gain_ref, cot_ref, rows_hbm, grads_hbm, gate_hbm, up_hbm, hid_hbm, weights_hbm,
        grad_ref, mid_rows_ref, feed_ref, sum_a, sum_b, out_hbm,
        own, rows_ref, grads_ref, gate_ref, up_ref, hid_ref, weights_ref, out_ref, *rest,
    ):
        (outgoing, mine, land, far, gone), room, (out_sems, in_sems) = rest[:5], rest[5:10], rest[10:]
        spot, post = Spot(), Post(out_sems, in_sems)
        loads = load(
            post,
            [(gate_hbm, gate_ref), (up_hbm, up_ref), (weights_hbm, weights_ref)]
            + [(rows_hbm, rows_ref), (hid_hbm, hid_ref), (grads_hbm, grads_ref)],
        )
        greet(spot, row_peers(spot) + y_peers(spot), 5, **collect_peers(spot))

        def main():
            for copy in loads[:3]:
                copy.wait()
            terms = [(ref, weights_ref, slice(i * PACK, (i + 1) * PACK)) for i, ref in enumerate((gate_ref, up_ref))]
            make = row_products(spot, terms, outgoing, mine)
            yield from scatter_rows(spot, post, make, outgoing, mine, land, far, gone)
            feed_ref[...] = jnp.zeros_like(feed_ref)

            def body(strip):
                upstream = row_sum(spot, mine, land, gone, strip)
                through, feed = norm_back(upstream, mid_ref[strip, :], wide_gain(gain_ref))
                grad = cot_ref[strip, :].astype(F32) + through
                grad_ref[strip, :] = grad
                own[strip, :] = grad.astype(BF16)
                feed_ref[...] += feed

            in_strips(ROWS, body)
            yield from gather_rows(spot, post, own, mid_rows_ref)

        def gradients():
            for copy in loads[3:]:
                copy.wait()
            groups = [(rows_ref, (gate_ref, up_ref)), (grads_ref, (hid_ref,))]
            yield from Gradients(spot, post, groups, *room, sum_a, sum_b).steps()

        def output():
            def step(i, carry):
                rows = pl.ds(pl.multiple_of(i * 256, 256), 256)
                out_ref[rows, :] = dot(hid_ref[rows, :], weights_ref[:, 2 * PACK :], 1, 1).astype(BF16)
                return carry

            lax.fori_loop(0, count // 256, step, 0)
            store = post.local(out_ref, out_hbm)
            store.start()
            yield
            store.wait()

        play("mggmgmgogmmgggggo", m=main(), g=gradients(), o=output())

    half = shape((4, 64, n), BF16)
    wide = pltpu.VMEM((count, WIDE), BF16)
    narrow = pltpu.VMEM((count, PACK), BF16)
    return moving(
        kernel,
        "turn",
        (
            shape((ROWS, WIDE), F32),
            shape((8, ROWS, WIDE), BF16),
            shape((1, WIDE), F32),
            half,
            half,
            shape((count, WIDE), BF16),
        ),
        (mid, gain, cotangent, rows, grads, d_gate, d_up, hidden, weights),
        [INSIDE, INSIDE, INSIDE] + [ANY] * 6,
        (INSIDE, ANY, INSIDE, INSIDE, INSIDE, ANY),
        [pltpu.VMEM((ROWS, WIDE), BF16), wide, wide, narrow, narrow, narrow, pltpu.VMEM((WIDE, n), BF16), wide]
        + scatter_scratch()
        + gradient_scratch(n)
        + sems(100),
        3,
    )


def leave(weights, tokens, gain, grad_mid, feed_part, rows, d_qkv, mid_rows, mixed, sum_two):
    n_qkv, n_out = d_qkv.shape[1], mixed.shape[1]
    n, n_two = n_qkv + n_out, sum_two.shape[-1]
    count = 8 * ROWS

    def kernel(
        weights_hbm, tokens_ref, gain_ref, grad_ref, feed_ref, rows_hbm, d_hbm, mid_hbm, mixed_hbm, sum_two_ref,
        token_ref, gains_ref, weight_ref, high_ref, norm_part, parts, from_y, over_y, from_chip, over_fsdp, from_tp,
        rows_ref, d_ref, mid_ref, mixed_ref, weights_ref, *rest,
    ):
        (outgoing, mine, land, far, gone), room, (sum_a, sum_b) = rest[:5], rest[5:10], rest[10:12]
        last, (out_sems, in_sems) = rest[12:18], rest[18:]
        spot, post = Spot(), Post(out_sems, in_sems)
        pairs = [(d_hbm, d_ref), (weights_hbm, weights_ref), (rows_hbm, rows_ref), (mixed_hbm, mixed_ref), (mid_hbm, mid_ref)]
        loads = load(post, pairs)
        greet(spot, row_peers(spot) + y_peers(spot) + gain_sources(spot), 5 + 13, **collect_peers(spot))

        def main():
            loads[1].wait()
            make = row_products(spot, [(d_ref, weights_ref, slice(None))], outgoing, mine)
            yield from scatter_rows(spot, post, make, outgoing, mine, land, far, gone)
            norm_part[...] = jnp.zeros_like(norm_part)

            def body(strip):
                upstream = row_sum(spot, mine, land, gone, strip)
                through, norm = norm_back(upstream, tokens_ref[strip, :].astype(F32), wide_gain(gain_ref))
                token_ref[strip, :] = grad_ref[strip, :] + through
                norm_part[...] += norm

            in_strips(ROWS, body)
            parts[...] = jnp.zeros_like(parts)
            for f in range(16):
                parts[f, 0:1, :] = norm_part[:, f * 128 : (f + 1) * 128]
                parts[f, 1:2, :] = feed_ref[:, f * 128 : (f + 1) * 128]
            yield from sum_gains(spot, post, parts, gains_ref, from_y, over_y, from_chip, over_fsdp, from_tp)

        def gradients():
            for copy in loads[:1] + loads[2:]:
                copy.wait()
            groups = [(rows_ref, (d_ref,)), (mid_ref, (mixed_ref,))]
            yield from Gradients(spot, post, groups, *room, sum_a, sum_b).steps()
            yield from together(
                scatter_low(spot, post, sum_a, strip_writer(weight_ref), *last[:2]),
                scatter_high(spot, post, sum_b, strip_writer(weight_ref, 64), *last[2:4]),
            )

        play(
            "bgmgbmgggmgggggmgmgmgbg",
            m=main(),
            g=gradients(),
            b=scatter_high(spot, post, sum_two_ref, strip_writer(high_ref), *last[4:]),
        )

    small = (8, 128)
    full_rows = pltpu.VMEM((count, WIDE), BF16)
    return moving(
        kernel,
        "leave",
        (shape((ROWS, WIDE), F32), shape(small, F32), shape((ROWS, n), F32), shape((64, n_two), F32)),
        (weights, tokens, gain, grad_mid, feed_part, rows, d_qkv, mid_rows, mixed, sum_two),
        [ANY, INSIDE, INSIDE, INSIDE, INSIDE] + [ANY] * 4 + [INSIDE],
        (INSIDE,) * 4,
        [pltpu.VMEM((1, WIDE), F32), pltpu.VMEM((16,) + small, F32)]
        + [pltpu.VMEM(dims + small, F32) for dims in ((3, 4), (4,), (3,), (), (7,))]
        + [full_rows, pltpu.VMEM((count, n_qkv), BF16), full_rows, pltpu.VMEM((count, n_out), BF16)]
        + [pltpu.VMEM(weights.shape, BF16)]
        + scatter_scratch()
        + gradient_scratch(n)
        + [pltpu.VMEM((4, 64, n), BF16)] * 2
        + low_scratch(n)
        + high_scratch(n)
        + high_scratch(n_two)
        + sems(120),
        4,
    )


def dot(a, b, da=1, db=0):
    return lax.dot_general(a, b, (((da,), (db,)), ((), ())), preferred_element_type=F32)


def plain(kernel, name, grid, inputs, in_specs, outs, out_specs, scratch=()):
    return pl.pallas_call(
        kernel,
        name=name,
        out_shape=outs,
        grid=grid,
        in_specs=in_specs,
        out_specs=out_specs,
        scratch_shapes=list(scratch),
        compiler_params=pltpu.CompilerParams(vmem_limit_bytes=VMEM),
    )(*inputs)


def by_rows(n, width, column=0):
    return pl.BlockSpec((n, width), lambda i: (i, column))


def whole(dims, *index):
    at = index or (0,) * len(dims)
    return pl.BlockSpec(dims, lambda i: at)


def project(rows, weights, cosine, sine):
    step = 512

    def kernel(rows_ref, w_ref, cos_ref, sin_ref, q_ref, kv_ref):
        out = dot(rows_ref[...], w_ref[...])
        cos, sin = cos_ref[...], sin_ref[...]
        for head in range(4):
            u = out[:, head * HD : (head + 1) * HD]
            turned = (u * cos + pltpu.roll(u, HD // 2, 1) * sin).astype(BF16)
            if head < 2:
                q_ref[:, head * HD : (head + 1) * HD] = turned
            else:
                kv_ref[head - 2, 0] = turned
                kv_ref[head - 2, 1] = out[:, (head + 2) * HD : (head + 3) * HD].astype(BF16)

    out = shape((8 * ROWS, 2 * HD), BF16)
    return plain(
        kernel,
        "project",
        (8 * ROWS // step,),
        (rows, weights, cosine, sine),
        [by_rows(step, WIDE), whole((WIDE, PACK)), by_rows(step, HD), by_rows(step, HD)],
        (out, shape((2, 2, 8 * ROWS, HD), BF16)),
        (by_rows(step, 2 * HD), pl.BlockSpec((2, 2, step, HD), lambda i: (0, 0, i, 0))),
    )


def feed_forward(rows, grads, weights):
    step = 256

    def kernel(rows_ref, grads_ref, g_ref, u_ref, d_ref, hid_ref, dgate_ref, dup_ref):
        gate = dot(rows_ref[...], g_ref[...])
        up = dot(rows_ref[...], u_ref[...])
        d_hid = dot(grads_ref[...], d_ref[...])
        sigma = 1.0 / (1.0 + jnp.exp(-gate))
        silu = gate * sigma
        hid_ref[...] = (silu * up).astype(BF16)
        dup_ref[...] = (d_hid * silu).astype(BF16)
        dgate_ref[...] = (d_hid * up * sigma * (1.0 + gate * (1.0 - sigma))).astype(BF16)

    out = shape((8 * ROWS, PACK), BF16)
    return plain(
        kernel,
        "feed_forward",
        (8 * ROWS // step,),
        (rows, grads, weights, weights, weights),
        [by_rows(step, WIDE)] * 2 + [whole((WIDE, PACK), 0, i) for i in range(3)],
        (out,) * 3,
        (by_rows(step, PACK),) * 3,
    )


def settle(layer, token_grad, gains, attention, low, high, wide):
    def kernel(
        layer_ref, token_ref, gains_ref, attention_ref, low_ref, high_ref,
        layer_out, token_out, norm_out, feed_out, query_out, key_out, value_out, out_out, gate_out, up_out, down_out,
        sem_ref,
    ):
        moves = [(layer_ref, layer_out), (token_ref, token_out)]
        for i, out in enumerate((query_out, key_out, value_out)):
            moves.append((attention_ref.at[:, pl.ds(i * 2 * HD, 2 * HD)], out))
        copies = [pltpu.make_async_copy(src, dst, sem_ref.at[i]) for i, (src, dst) in enumerate(moves)]
        for copy in copies:
            copy.start()
        norm_out[...] = gains_ref[0:1, :]
        feed_out[...] = gains_ref[1:2, :]
        out_out[...] = attention_ref[:, PACK:].T
        for i, out in enumerate((gate_out, up_out, down_out)):
            columns = slice(i * PACK, (i + 1) * PACK)
            out[...] = jnp.concatenate([low_ref[:, columns], high_ref[:, columns]], 0).T[:wide]
        for copy in copies:
            copy.wait()

    vector = shape((1, 128), F32)
    square = shape((ROWS, 2 * HD), F32)
    tall = shape((wide, ROWS), F32)
    return pl.pallas_call(
        kernel,
        name="settle",
        out_shape=(shape(layer.shape, layer.dtype), shape(token_grad.shape, F32), vector, vector, square, square, square)
        + (shape((2 * HD, ROWS), F32), tall, tall, tall),
        in_specs=[INSIDE] * 6,
        out_specs=(ANY, ANY, INSIDE, INSIDE, ANY, ANY, ANY) + (INSIDE,) * 4,
        scratch_shapes=[pltpu.SemaphoreType.DMA((5,))],
        compiler_params=pltpu.CompilerParams(vmem_limit_bytes=VMEM),
    )(layer, token_grad, gains, attention, low, high)


TILE = 256
CHUNK = 512


def place_of(start, count, xh, axis):
    dims = (count, 1) if axis == 0 else (1, count)
    j = lax.broadcasted_iota(jnp.int32, dims, axis)
    return 2 * (j + start) - lax.rem(j + start, ROWS) + xh * ROWS


SPANS = ((0, 512, False), (512, 256, True))
LAST = (768, 256, True)


def scores_of(keys, q, span, q_pos, prefix, xh):
    start, count, masked = span
    scores = dot(keys, q, 1, 1) * (SCALE * LOG2E)
    if masked:
        k_pos = place_of(start, count, xh, 0)
        scores = jnp.where(jnp.logical_or(k_pos <= q_pos, k_pos < prefix), scores, -1e30)
    return scores


def tile_at(i):
    head, tile = lax.div(i, 4), lax.rem(i, 4)
    return head, tile, pl.ds(pl.multiple_of(head * HD, HD), HD), pl.ds(pl.multiple_of(tile * TILE, TILE), TILE)


def exchange(post, pairs, device):
    copies = [post.copy(src, dst, device) for src, dst in pairs]
    for copy in copies:
        copy.start()
    yield
    for copy in copies:
        copy.wait_recv()
        yield
    for copy in copies:
        copy.wait_send()


def prefix_of(prefixes_ref):
    return prefixes_ref[lax.div(lax.axis_index("fsdp"), 2)]


def attend(prefixes, queries, here, cotangent, row_out, second):
    n, n_two = row_out.shape[-1], second.shape[-1]

    def kernel(
        prefixes_ref, q_ref, here_ref, cot_ref, row_ref, second_ref, o_ref, lse_ref, there_ref, grads_ref, out_ref, stage_ref,
        top_ref, sum_ref, acc_ref, out_sems, in_sems,
    ):
        prefix = prefix_of(prefixes_ref)
        spot, post = Spot(), Post(out_sems, in_sems)
        partner = spot.at(dx=2)
        greet(spot, row_peers(spot) + y_peers(spot) + [partner], 6)

        def sweep(side, begin, end):
            keys_ref = there_ref if side else here_ref
            xh = 1 - spot.xh if side else spot.xh

            def step(i, carry):
                head, tile, cols, rows = tile_at(i)
                q = q_ref[rows, cols]
                q_pos = place_of(tile * TILE, TILE, spot.xh, 1)
                one = pl.ds(i, 1)

                def chunk(span, first):
                    keys = pl.ds(span[0], span[1])
                    scores = scores_of(keys_ref[head, 0, keys, :], q, span, q_pos, prefix, xh)
                    top = jnp.max(scores, 0, keepdims=True)
                    if not first:
                        before = top_ref[one, :]
                        top = jnp.maximum(top, before)
                    raised = jnp.exp2(scores - top)
                    total = jnp.sum(raised, 0, keepdims=True)
                    mixed = dot(keys_ref[head, 1, keys, :], raised.astype(BF16), 0, 0)
                    if not first:
                        fade = jnp.exp2(before - top)
                        total = total + sum_ref[one, :] * fade
                        mixed = mixed + acc_ref[i] * fade
                    top_ref[one, :] = top
                    sum_ref[one, :] = total
                    acc_ref[i] = mixed

                for number, span in enumerate(SPANS):
                    chunk(span, side == 0 and number == 0)

                @pl.when(tile == 3)
                def _():
                    chunk(LAST, False)

                if side == 1:
                    total = sum_ref[one, :]
                    o_ref[rows, cols] = (acc_ref[i] / total).T.astype(BF16)
                    lse_ref[one, :] = top_ref[one, :] + jnp.log2(total)
                return carry

            lax.fori_loop(begin, end, step, 0)

        def compute():
            sweep(0, 0, 8)
            yield
            sweep(1, 0, 4)
            yield
            sweep(1, 4, 8)

        play(
            "vesfcvsfecvsfecse",
            v=y_gather(spot, post, row_ref, lambda y: out_ref.at[y]),
            f=y_gather(spot, post, second_ref, lambda y: stage_ref.at[y]),
            e=exchange(post, [(here_ref.at[head], there_ref.at[head]) for head in range(2)], partner),
            s=gather_rows(spot, post, cot_ref, grads_ref),
            c=compute(),
        )

    return moving(
        kernel,
        "attend",
        (
            shape((8 * ROWS, 2 * HD), BF16),
            shape((8, TILE), F32),
            shape(here.shape, BF16),
            shape((8, ROWS, WIDE), BF16),
            shape((4, 4, ROWS, n), BF16),
            shape((4, 64, n_two), BF16),
        ),
        (prefixes, queries, here, cotangent, row_out, second),
        [pl.BlockSpec(memory_space=pltpu.SMEM)] + [INSIDE] * 5,
        (INSIDE, INSIDE, INSIDE, ANY, ANY, INSIDE),
        [pltpu.VMEM((8, TILE), F32), pltpu.VMEM((8, TILE), F32), pltpu.VMEM((8, HD, TILE), F32)] + sems(60),
        5,
    )


def attend_back(prefixes, queries, here, there, rows, weights, mixed, lse, cosine, sine, out_part, mid, sum_a):
    n = sum_a.shape[-1]

    def kernel(
        prefixes_ref, rows_hbm, weights_hbm, q_ref, here_ref, there_ref, o_ref, lse_ref, cos_ref, sin_ref, part_ref, mid_ref,
        sum_a_ref, d_ref, layer_ref, weight_ref, rows_ref, weights_ref, g_ref, delta_ref, dq_ref, acc_ref, near_ref, away_ref, land_ref, *rest,
    ):
        (outgoing, mine, land, far, gone), last, (out_sems, in_sems) = rest[:5], rest[5:7], rest[7:]
        prefix = prefix_of(prefixes_ref)
        spot, post = Spot(), Post(out_sems, in_sems)
        loads = load(post, [(weights_hbm, weights_ref), (rows_hbm, rows_ref)])
        partner = spot.at(dx=2)
        greet(spot, row_peers(spot) + y_peers(spot) + [partner], 6)

        def sweep(head, side, keys_ref, into):
            xh = spot.xh if side == 0 else 1 - spot.xh
            cols = pl.ds(head * HD, HD)
            into[...] = jnp.zeros_like(into)

            def step(tile, carry):
                i = head * 4 + tile
                rows = pl.ds(pl.multiple_of(tile * TILE, TILE), TILE)
                q, g = q_ref[rows, cols], g_ref[rows, cols]
                q_pos = place_of(tile * TILE, TILE, spot.xh, 1)
                if side == 1:
                    product = g.astype(F32) * o_ref[rows, cols].astype(F32)
                    delta_ref[pl.ds(i, 1), :] = jnp.sum(product.T, 0, keepdims=True)
                level, offset = lse_ref[pl.ds(i, 1), :], delta_ref[pl.ds(i, 1), :]

                def chunk(span, first):
                    span_rows = pl.ds(span[0], span[1])
                    keys = keys_ref[head, 0, span_rows, :]
                    probs = jnp.exp2(scores_of(keys, q, span, q_pos, prefix, xh) - level)
                    d_probs = dot(keys_ref[head, 1, span_rows, :], g, 1, 1)
                    d_scores = (probs * (d_probs - offset)).astype(BF16)
                    into[0, span_rows, :] += dot(d_scores, q)
                    into[1, span_rows, :] += dot(probs.astype(BF16), g)
                    d_query = dot(d_scores, keys, 0, 0)
                    dq_ref[i] = d_query if first else dq_ref[i] + d_query

                for number, span in enumerate(SPANS):
                    chunk(span, side == 1 and number == 0)

                @pl.when(tile == 3)
                def _():
                    chunk(LAST, False)

                if side == 0:
                    u = dq_ref[i] * SCALE
                    d_ref[rows, cols] = (u * cos_ref[rows, :] - pltpu.roll(u, HD // 2, 1) * sin_ref[rows, :]).astype(BF16)
                return carry

            lax.fori_loop(0, 4, step, 0)

        def compute():
            for copy in loads:
                copy.wait()

            def heads(i, carry):
                span = pl.ds(pl.multiple_of(i * 256, 256), 256)
                g_ref[span, :] = dot(rows_ref[span, :], weights_ref[...]).astype(BF16)
                return carry

            lax.fori_loop(0, 4, heads, 0)
            copies = []
            for head in range(2):
                sweep(head, 1, there_ref, acc_ref)
                away_ref[head] = acc_ref[...].astype(BF16)
                copies.append(post.copy(away_ref.at[head], land_ref.at[head], partner))
                copies[-1].start()
                yield
            for head in range(2):
                sweep(head, 0, here_ref, near_ref.at[head])
                yield
            for head in range(2):
                copies[head].wait_recv()
                cols = pl.ds(2 * HD + head * HD, HD)

                def finish(i, carry, head=head):
                    rows = pl.ds(pl.multiple_of(i * 128, 128), 128)
                    u = (near_ref[head, 0, rows, :] + land_ref[head, 0, rows, :].astype(F32)) * SCALE
                    back = u * cos_ref[rows, :] - pltpu.roll(u, HD // 2, 1) * sin_ref[rows, :]
                    d_ref[rows, pl.ds(2 * HD + head * HD, HD)] = back.astype(BF16)
                    v = near_ref[head, 1, rows, :] + land_ref[head, 1, rows, :].astype(F32)
                    d_ref[rows, pl.ds(4 * HD + head * HD, HD)] = v.astype(BF16)
                    return carry

                lax.fori_loop(0, 8, finish, 0)
            for copy in copies:
                copy.wait_send()

        make = row_loads(spot, post, part_ref, outgoing, mine)

        def output():
            yield from scatter_rows(spot, post, make, outgoing, mine, land, far, gone, True)

            def body(strip):
                layer_ref[strip, :] = (mid_ref[strip, :] + row_sum(spot, mine, land, gone, strip)).astype(BF16)

            in_strips(ROWS, body)

        play(
            "wcococwcoow",
            c=compute(),
            o=output(),
            w=scatter_low(spot, post, sum_a_ref, strip_writer(weight_ref), *last),
        )

    pair = (2, 8 * ROWS, HD)
    return moving(
        kernel,
        "attend_back",
        (shape((8 * ROWS, PACK), BF16), shape((ROWS, WIDE), BF16), shape((64, n), F32)),
        (prefixes, rows, weights, queries, here, there, mixed, lse, cosine, sine, out_part, mid, sum_a),
        [pl.BlockSpec(memory_space=pltpu.SMEM), ANY, ANY] + [INSIDE] * 7 + [ANY, INSIDE, INSIDE],
        (INSIDE,) * 3,
        [
            pltpu.VMEM(rows.shape, BF16),
            pltpu.VMEM(weights.shape, BF16),
            pltpu.VMEM((8 * ROWS, 2 * HD), BF16),
            pltpu.VMEM((8, TILE), F32),
            pltpu.VMEM((8, TILE, HD), F32),
            pltpu.VMEM(pair, F32),
            pltpu.VMEM((2,) + pair, F32),
            pltpu.VMEM((2,) + pair, BF16),
            pltpu.VMEM((2,) + pair, BF16),
        ]
        + scatter_scratch()
        + low_scratch(n)
        + sems(64),
        6,
    )


def on_device(
    tokens,
    prefixes,
    norm_gain,
    query_weight,
    key_weight,
    value_weight,
    output_weight,
    feed_gain,
    gate_weight,
    up_weight,
    down_weight,
    cotangent,
):
    rows_one, full_one, row_out, row_two, second, cosine, sine = enter(
        tokens, norm_gain, query_weight, key_weight, value_weight, output_weight, gate_weight.T, up_weight.T, down_weight
    )
    rows_one = rows_one.reshape(-1, WIDE)
    full_one = full_one.reshape(WIDE, -1)
    queries, here = project(rows_one, full_one, cosine, sine)
    attended, lse, there, grad_rows, full_out, stage_two = attend(prefixes, queries, here, cotangent, row_out, second)
    full_out = full_out.reshape(WIDE, -1)
    mid, rows_two, full_two = middle(attended, full_out, tokens, feed_gain, row_two, stage_two)
    rows_two, grad_rows, full_two = (a.reshape(-1, a.shape[-1]) for a in (rows_two, grad_rows, full_two.reshape(WIDE, -1)))
    hidden, d_gate, d_up = feed_forward(rows_two, grad_rows, full_two)
    grad_mid, mid_rows, feed_part, sum_a, sum_b, part_out = turn(
        mid, feed_gain, cotangent, rows_two, grad_rows, d_gate, d_up, hidden, full_two
    )
    mid_rows = mid_rows.reshape(-1, WIDE)
    d_qkv, layer_output, low = attend_back(
        prefixes, queries, here, there, mid_rows, full_out, attended, lse, cosine, sine, part_out.reshape(8, ROWS, WIDE), mid, sum_a
    )
    token_grad, gains, attention, high = leave(
        full_one, tokens, norm_gain, grad_mid, feed_part, rows_one, d_qkv, mid_rows, attended, sum_b
    )
    layer_output, token_grad, norm_grad, feed_grad, *grads = settle(
        layer_output, token_grad, gains, attention, low, high, gate_weight.shape[1]
    )
    query_grad, key_grad, value_grad, output_grad, gate_grad, up_grad, down_grad = grads
    return (
        layer_output,
        token_grad,
        norm_grad[0],
        query_grad,
        key_grad,
        value_grad,
        output_grad,
        feed_grad[0],
        gate_grad.T,
        up_grad.T,
        down_grad,
    )


def solution(mesh):
    rows = P(("fsdp", "tp"), None)
    wide = P("fsdp", "tp")
    tall = P("tp", "fsdp")
    return jax.shard_map(
        on_device,
        mesh=mesh,
        in_specs=(rows, P(), P(), wide, wide, wide, tall, P(), wide, wide, tall, rows),
        out_specs=(rows, rows, P("fsdp"), wide, wide, wide, tall, P("fsdp"), wide, wide, tall),
        check_vma=False,
    )
```
